32 devices in a mesh: row: 8 (over y, x, core), col: 4 (over z).
Axes of the slice: x: 2, y: 2, z: 4, core: 2. Of those that a mesh axis runs over, the one named last changes fastest.
Arguments:
- question_vectors: bfloat16 [512, 2048], P('row', 'col'), may hold values from -0.5 to 0.5
- document_vectors: bfloat16 [512, 2048], P('col', 'row'), may hold values from -0.5 to 0.5
- positive: int32 [512], P('row'), may hold values from 0 to 511
- tokens: bfloat16 [4096, 2048], P(('row', 'col')), may hold values from -6 to 6
- expert_ids: int32 [4096, 8], P(('row', 'col')), may hold values from 0 to 31, all different within a row; in each aligned block of 128 rows (0 to 127, 128 to 255, ...) at most 36 rows name the same one
- route_weights: float32 [4096, 8], P(('row', 'col')), may hold values from 0.03 to 0.3
- expert_gate_up: bfloat16 [32, 2048, 1536], P(('row', 'col')), may hold values from -0.125 to 0.125
- expert_down: bfloat16 [32, 768, 2048], P(('row', 'col')), may hold values from -0.21875 to 0.21875
Outputs:
- passage_grad: float32 [512, 2048], P('col', 'row')
- token_grad: bfloat16 [4096, 2048], P(('row', 'col'))
- gate_up_grad: bfloat16 [32, 2048, 1536], P(('row', 'col'))
- down_grad: bfloat16 [32, 768, 2048], P(('row', 'col'))
The draws below stay inside these ranges and needn't reach their ends.
Inputs may be any that keep to these rules, and one draw needn't show every extreme that they name: `expert_ids`: each token names 8 different experts; among the 128 tokens of one device no expert is named more than 36 times, a bound that some block reaches.
All inputs are finite; a program needn't handle non-finite values.
Results may differ from the reference program's by a relative error of at most 0.018.
Values may be sent and summed in bfloat16 or wider, within the bound.
A program may use at most 192 MiB of HBM per device.

```python
import math
import jax
import jax.numpy as jnp
import numpy as np
from jax import lax

D = 2048
FF = 768
TOP = 8
SEQ_LEN = 8
TOK_DEV = 128
TOKENS = 4096
NQ = 512
NP = 512
EXPERTS = 32
CAP = 36
DEVICES = 32


sharpness_divisor = 0.02


def embed_pair(key):
    folded = jax.random.fold_in(key, 4099)
    subkeys = jax.random.split(folded, 9)
    question_vectors = jax.random.normal(subkeys[0], (NQ, D), jnp.float32) * 0.03
    document_vectors = jax.random.normal(subkeys[1], (NP, D), jnp.float32) * 0.03
    chosen_q = jax.random.permutation(subkeys[4], NQ)[:8]
    chosen_p = jax.random.permutation(subkeys[5], NP)[:16]
    sign_pattern = jax.random.randint(subkeys[6], (8, D), 0, 2).astype(jnp.float32) * 2.0 - 1.0
    direction_unit = sign_pattern / math.sqrt(D)
    correct_classes = jnp.array([110.0, 170.0, 230.0, 290.0, 140.0, 200.0, 260.0, 320.0], jnp.float32)
    magnitude = jnp.sqrt(correct_classes * sharpness_divisor)[:, None]
    query_planted = magnitude * direction_unit
    passage_planted = magnitude * direction_unit
    interval_lengths = jax.random.uniform(subkeys[7], (8,), jnp.float32, 1.0, 3.0)
    query_power = jnp.sum(query_planted * query_planted, axis=1, keepdims=True)
    jitter_shift = jax.random.normal(subkeys[8], (8, D), jnp.float32) * (0.2 / math.sqrt(D))
    jitter_shift = jitter_shift - jnp.sum(jitter_shift * query_planted, axis=1, keepdims=True) / query_power * query_planted
    distractor_vector = passage_planted - interval_lengths[:, None] * sharpness_divisor * query_planted / query_power + jitter_shift
    question_vectors = question_vectors.at[chosen_q].set(query_planted)
    document_vectors = document_vectors.at[chosen_p[:8]].set(passage_planted)
    document_vectors = document_vectors.at[chosen_p[8:]].set(distractor_vector)
    return (jnp.clip(question_vectors, -0.5, 0.5), jnp.clip(document_vectors, -0.5, 0.5))


def draw_question_vectors(key, part):
    return embed_pair(key)[0].astype(jnp.bfloat16)


def draw_document_vectors(key, part):
    return embed_pair(key)[1].astype(jnp.bfloat16)


def touch_ends(entries, stream_key, least, top_value):
    longest = entries.shape.index(max(entries.shape))
    spots = []
    for shift in (0, 1):
        where = [jax.random.randint(jax.random.fold_in(stream_key, axis), (), 0, length) for axis, length in enumerate(entries.shape)]
        where[longest] = (where[longest] + shift) % entries.shape[longest]
        spots.append(tuple(where))
    return entries.at[spots[0]].set(least).at[spots[1]].set(top_value)


def block_levels(key, shape, cuts, smallest, largest):
    loudness = 1.0
    for dim, blocks in cuts:
        steps = jax.random.uniform(jax.random.fold_in(jax.random.fold_in(key, 6), dim), (blocks,), jnp.float32, smallest / len(cuts), largest / len(cuts))
        loudness = loudness * jnp.repeat(jnp.exp(steps), shape[dim] // blocks).reshape((-1,) + (1,) * (len(shape) - 1 - dim))
    return loudness


def routed_block(rng, own, number, rows, amount, top, limit, skew):
    order = jax.random.permutation(rng, amount)
    crowded, usual = shares(amount, rows * top, limit, skew, True), shares(amount, rows * top, limit, skew, False)
    places = jnp.arange(amount)

    def named(tallies, offset_by):
        used = int((tallies > 0).sum())
        fixed = max(1, used // 4)
        shifted = fixed + (places - fixed + offset_by * (used - fixed)) % max(1, amount - fixed)
        return jnp.zeros((amount,), jnp.int32).at[order[jnp.where(places < fixed, places, shifted)]].set(jnp.asarray(tallies, jnp.int32))

    tallies = jnp.where(number % 4 == 0, named(crowded, number // 4), named(usual, number - number // 4 - 1))
    mixed = jax.random.permutation(jax.random.fold_in(own, 3), amount)
    donor, receiver = mixed[0:amount // 2 * 2:2], mixed[1:amount // 2 * 2:2]
    margin = jnp.minimum(tallies[donor] - 1, limit - tallies[receiver]) // 2
    margin = jnp.where((donor == order[0]) | (receiver == order[0]) | (tallies[receiver] == 0), 0, jnp.maximum(margin, 0))
    shifted = jax.random.randint(jax.random.fold_in(own, 4), (amount // 2,), 0, 1 << 20) % (margin + 1)
    tallies = tallies.at[donor].add(-shifted).at[receiver].add(shifted)
    members = jnp.searchsorted(jnp.cumsum(tallies), jnp.arange(rows * top), side="right").astype(jnp.int32)
    table = members.reshape(top, rows).T
    table = table[jax.random.permutation(jax.random.fold_in(own, 1), rows)]
    offset_by = jax.random.randint(jax.random.fold_in(own, 2), (rows, 1), 0, top)
    return jnp.take_along_axis(table, (jnp.arange(top)[None, :] + offset_by) % top, axis=1)


def shares(amount, total, limit, skew, full):
    weights = [(1 << 20) // math.isqrt(grade ** skew) + 1 for grade in range(1, amount + 1)]
    largest = limit if full else min(limit, max(-(-total // amount), total * weights[0] // sum(weights)))
    least = 1 if total - largest >= amount - 1 else 0
    counts, spare = [largest] + [least] * (amount - 1), total - largest - least * (amount - 1)
    while spare > 0:
        candidates = [i for i in range(1, amount) if counts[i] < largest] or [i for i in range(1, amount) if counts[i] < limit]
        whole, budget = sum([weights[i] for i in candidates]), spare
        for i in candidates:
            extra = min(limit - counts[i], max(1, budget * weights[i] // whole), spare)
            counts[i] = counts[i] + extra
            spare = spare - extra
    return np.array(counts)


def gaussian(own_key, extent, scale, most, pieces=(), held_as=jnp.bfloat16):
    values = scale * jax.random.normal(own_key, extent, jnp.float32)
    if pieces:
        values = values * block_levels(own_key, extent, pieces, -0.22, 0.18)
    return jnp.clip(values, -most, most).astype(held_as)


def setup_inputs(seed: int = 0) -> dict:
    key_list = jax.random.split(jax.random.key(seed), 9)
    question_vectors = draw_question_vectors(jax.random.fold_in(key_list[8], 71), 0)
    document_vectors = draw_document_vectors(jax.random.fold_in(key_list[8], 71), 0)
    positive = touch_ends(jax.random.randint(key_list[2], (NQ,), 0, NP), jax.random.fold_in(key_list[2], 1), 0, NP - 1).astype(jnp.int32)
    tokens = gaussian(key_list[3], (TOKENS, D), 1.0, 6.0, ((0, 32),))
    expert_ids_keys = jax.random.split(jax.random.fold_in(key_list[4], 1), TOKENS // TOK_DEV)
    expert_ids_turns = jax.random.permutation(jax.random.fold_in(key_list[4], 3), TOKENS // TOK_DEV)
    expert_ids = jax.vmap(lambda own, number: routed_block(jax.random.fold_in(key_list[4], 2), own, number, TOK_DEV, EXPERTS, TOP, CAP, 1))(expert_ids_keys, expert_ids_turns).reshape((TOKENS, TOP))
    route_weights = jnp.clip(jnp.exp(math.log(0.3) - 2.3025852 * jax.random.uniform(key_list[5], (TOKENS, TOP), jnp.float32) ** block_levels(key_list[5], (TOKENS, TOP), ((0, 32),), -0.2, 0.2)), 0.03, 0.3)
    expert_gate_up = gaussian(key_list[6], (EXPERTS, D, 2 * FF), D ** -0.5, 0.125, ((0, 32),))
    expert_down = gaussian(key_list[7], (EXPERTS, FF, D), FF ** -0.5, 0.21875, ((0, 32),))
    return dict(question_vectors=question_vectors, document_vectors=document_vectors, positive=positive, tokens=tokens, expert_ids=expert_ids, route_weights=route_weights, expert_gate_up=expert_gate_up, expert_down=expert_down)


sharpness_divisor = 0.02


def expert_backward(slot_inputs, slot_grads, gate_up, down_proj):
    projected = jnp.dot(slot_inputs, gate_up, preferred_element_type=jnp.float32)
    hidden_width = down_proj.shape[0]
    gate_part = projected[:, :hidden_width]
    up_part = projected[:, hidden_width:]
    sigmoid_gate = jax.nn.sigmoid(gate_part)
    activated = gate_part * sigmoid_gate
    hidden = (activated * up_part).astype(jnp.bfloat16)
    down_grad = lax.dot_general(hidden, slot_grads, (((0,), (0,)), ((), ())), preferred_element_type=jnp.float32).astype(jnp.bfloat16)
    hidden_grad = lax.dot_general(slot_grads, down_proj, (((1,), (1,)), ((), ())), preferred_element_type=jnp.float32)
    slope = sigmoid_gate * (1.0 + gate_part * (1.0 - sigmoid_gate))
    pre_grad = jnp.concatenate([hidden_grad * up_part * slope, hidden_grad * activated], axis=1).astype(jnp.bfloat16)
    gate_up_grad = lax.dot_general(slot_inputs, pre_grad, (((0,), (0,)), ((), ())), preferred_element_type=jnp.float32).astype(jnp.bfloat16)
    input_grad = lax.dot_general(pre_grad, gate_up, (((1,), (1,)), ((), ())), preferred_element_type=jnp.float32).astype(jnp.bfloat16)
    return input_grad, gate_up_grad, down_grad


def reference(question_vectors, document_vectors, positive, tokens, expert_ids, route_weights, expert_gate_up, expert_down):
    similarity_entries = jnp.dot(question_vectors, document_vectors.T, preferred_element_type=jnp.float32) / sharpness_divisor
    row_peak = jnp.max(similarity_entries, axis=1, keepdims=True)
    coefficient_entries = jnp.exp(similarity_entries - row_peak)
    partition_normalizer = jnp.sum(coefficient_entries, axis=1, keepdims=True)
    columns = jnp.arange(NP, dtype=jnp.int32)
    membership_table = (positive[:, None] == columns[None, :]).astype(jnp.float32)
    similarity_derivative = ((coefficient_entries / partition_normalizer - membership_table) / sharpness_divisor).astype(jnp.bfloat16)
    query_grad = jnp.dot(similarity_derivative, document_vectors, preferred_element_type=jnp.float32)
    passage_grad = jnp.dot(similarity_derivative.T, question_vectors, preferred_element_type=jnp.float32)
    cotangent = jnp.repeat(query_grad / SEQ_LEN, SEQ_LEN, axis=0).astype(jnp.bfloat16)

    blocks = expert_ids.reshape(DEVICES, TOK_DEV * TOP)
    expert_hit = (blocks[:, :, None] == jnp.arange(EXPERTS, dtype=jnp.int32)[None, None, :]).astype(jnp.int32)
    before = jnp.cumsum(expert_hit, axis=1) - expert_hit
    slot_number = jnp.sum(before * expert_hit, axis=2)
    source = jnp.arange(DEVICES, dtype=jnp.int32)[:, None]
    slot_index = (blocks * (DEVICES * CAP) + source * CAP + slot_number).reshape(-1).astype(jnp.int32)
    slot_owner = jnp.full((EXPERTS * DEVICES * CAP,), -1, jnp.int32)
    slot_owner = slot_owner.at[slot_index].set(jnp.arange(TOKENS * TOP, dtype=jnp.int32))
    slot_owner = slot_owner.reshape(EXPERTS, DEVICES * CAP)
    flat_weights = route_weights.reshape(-1)

    def per_expert(carried, inputs):
        owners, gate_up, down_proj = inputs
        filled = owners >= 0
        pair_row = jnp.maximum(owners, 0).astype(jnp.int32)
        token_row = (pair_row // TOP).astype(jnp.int32)
        slot_inputs = jnp.where(filled[:, None], tokens[token_row], jnp.zeros((), tokens.dtype))
        scaled = jnp.where(filled, flat_weights[pair_row], jnp.zeros((), flat_weights.dtype))
        slot_grads = (scaled[:, None] * cotangent[token_row].astype(jnp.float32)).astype(jnp.bfloat16)
        input_grad, gate_up_grad, down_grad = expert_backward(slot_inputs, slot_grads, gate_up, down_proj)
        addend = jnp.where(filled[:, None], input_grad.astype(jnp.float32), jnp.zeros((), jnp.float32))
        carried = carried.at[token_row].add(addend)
        return carried, (gate_up_grad, down_grad)

    start_grad = jnp.zeros((TOKENS, D), jnp.float32)
    summed, (gate_up_grad, down_grad) = lax.scan(per_expert, start_grad, (slot_owner, expert_gate_up, expert_down))
    token_grad = (cotangent.astype(jnp.float32) + summed).astype(jnp.bfloat16)
    return passage_grad, token_grad, gate_up_grad, down_grad
```

```python
import functools

import jax
import jax.numpy as jnp
from jax import lax
from jax.experimental import pallas as pl
from jax.experimental.pallas import tpu as pltpu
from jax.sharding import PartitionSpec as P

SEQ_LEN = 8
LANES = 128
CHUNKS = 4
VMEM_LIMIT = 67_000_000

sharpness_divisor = 0.02

BF = jnp.bfloat16
F32 = jnp.float32
MESH = pl.DeviceIdType.MESH


def contract(a, b, da, db):
    return lax.dot_general(a, b, (((da,), (db,)), ((), ())), preferred_element_type=F32)


def span(index, size):
    return pl.ds(pl.multiple_of(index * size, size), size)


def remote(src, dst, send_sem, recv_sem, to):
    return pltpu.make_async_remote_copy(
        src_ref=src, dst_ref=dst, send_sem=send_sem, recv_sem=recv_sem,
        device_id=to, device_id_type=MESH,
    )


def greet(rows, cols):
    row, col = lax.axis_index("row"), lax.axis_index("col")
    barrier = pltpu.get_barrier_semaphore()
    for s in range(1, rows):
        pl.semaphore_signal(
            barrier, inc=1, device_id=(lax.rem(row + s, rows), col), device_id_type=MESH
        )
    for s in range(1, cols):
        pl.semaphore_signal(
            barrier, inc=1, device_id=(row, lax.rem(col + s, cols)), device_id_type=MESH
        )
    pl.semaphore_wait(barrier, rows + cols - 2)


def dispatch_kernel(
    rows, cols, cap,
    tok_ref, doc_ref, qry_ref, meta_ref, wgu_ref,
    x_ref, docs_ref, qrys_ref, metas_ref, proj_ref, dm_ref,
    tokc, packed, w, own_sem, w_sem, zs, zr, gs, gr, rs, ds, dr,
):
    row, col = lax.axis_index("row"), lax.axis_index("col")
    n_tok, width = tok_ref.shape
    n_doc, w_doc = doc_ref.shape
    n_qry, w_qry = qry_ref.shape
    top = 8
    step = width // CHUNKS
    block = cols * cap
    chips = rows // 2
    core = lax.rem(row, 2)
    chip = lax.div(row, 2)
    sibling = row + 1 - 2 * core

    def doc_strip(r):
        return docs_ref.at[:, span(r, w_doc)]

    def qry_strip(r):
        return qrys_ref.at[span(r, n_qry), :]

    def meta_strip(r):
        return metas_ref.at[pl.ds(r * cols, cols)]

    strips = (meta_strip, doc_strip, qry_strip)

    def line_piece(kind, c):
        if kind == 0:
            return meta_ref, metas_ref.at[row * cols + c]
        if kind == 1:
            return doc_ref, docs_ref.at[span(c, n_doc), span(row, w_doc)]
        if kind == 2:
            return qry_ref, qrys_ref.at[span(row, n_qry), span(c, w_qry)]
        f = kind - 3
        part = pl.ds(f * step, step)
        return tok_ref.at[:, part], tokc.at[span(c, n_tok), part]

    def along_line(kind, s, origin, to):
        src, dst = line_piece(kind, origin)
        return remote(src, dst, zs.at[kind, s], zr.at[kind, origin], (row, to))

    own = []
    for kind in range(3 + CHUNKS):
        src, dst = line_piece(kind, col)
        own.append(pltpu.make_async_copy(src, dst, own_sem.at[kind]))
    loads = [
        pltpu.make_async_copy(wgu_ref.at[span(f, step)], w.at[span(f, step)], w_sem.at[f])
        for f in range(CHUNKS)
    ]
    for copy in own:
        copy.start()
    for copy in loads:
        copy.start()
    greet(rows, cols)
    for kind in range(3 + CHUNKS):
        for s in range(1, cols):
            along_line(kind, s, col, lax.rem(col + s, cols)).start()

    def line_arrived(kind):
        own[kind].wait()
        for s in range(1, cols):
            origin = lax.rem(col + s, cols)
            along_line(kind, s, origin, origin).wait_recv()

    def peer(s):
        return 2 * lax.rem(chip + s, chips) + core

    def direct(kind, s, origin, to):
        return remote(strips[kind](origin), strips[kind](origin), gs.at[kind, s],
                      gr.at[kind, origin], (to, col))

    def relay(kind, s, origin):
        return remote(strips[kind](origin), strips[kind](origin), rs.at[kind, s],
                      gr.at[kind, origin], (sibling, col))

    for kind in range(3):
        line_arrived(kind)
        for s in range(1, chips):
            direct(kind, s, row, peer(s)).start()
        direct(kind, 0, row, sibling).start()

    target = (
        lax.broadcasted_iota(jnp.int32, (rows, n_tok), 0) * cols + col
    ).astype(F32)
    before = (
        lax.broadcasted_iota(jnp.int32, (n_tok, n_tok), 0)
        < lax.broadcasted_iota(jnp.int32, (n_tok, n_tok), 1)
    ).astype(BF)
    slot = lax.broadcasted_iota(jnp.int32, (block, n_tok), 0).astype(F32)
    for c in range(cols):
        ids = metas_ref[row * cols + c]
        hit = jnp.zeros((rows, n_tok), F32)
        for k in range(top):
            hit = hit + (ids[k : k + 1, :] == target).astype(F32)
        rank = contract(hit.astype(BF), before, 1, 0)
        place = jnp.where(hit > 0.5, rank + float(c * cap), -1.0)
        for r in range(rows):
            dm_ref[r * block : (r + 1) * block, c * n_tok : (c + 1) * n_tok] = jnp.where(
                slot == place[r : r + 1, :], 1.0, 0.0
            ).astype(BF)

    def outgoing(f, s, origin, to):
        part = pl.ds(f * step, step)
        return remote(packed.at[span(to, block), part], x_ref.at[span(origin, block), part],
                      ds.at[f, s], dr.at[f, origin], (to, col))

    def kept(f):
        part = pl.ds(f * step, step)
        return pltpu.make_async_copy(
            packed.at[span(row, block), part], x_ref.at[span(row, block), part],
            own_sem.at[3 + CHUNKS + f],
        )

    pair = 2 * block
    for f in range(CHUNKS):
        line_arrived(3 + f)
        part = slice(f * step, (f + 1) * step)

        @pl.loop(0, rows // 2)
        def _(m):
            packed[span(m, pair), part] = contract(
                dm_ref[span(m, pair), :], tokc[:, part], 1, 0
            ).astype(BF)

        for s in range(1, rows):
            outgoing(f, s, row, lax.rem(row + s, rows)).start()
        kept(f).start()

    for kind in range(3):
        for s in range(1, chips):
            origin = peer(s)
            direct(kind, s, origin, origin).wait_recv()
            relay(kind, s, origin).start()

    hidden2 = proj_ref.shape[1]
    tile = 512
    for f in range(CHUNKS):
        loads[f].wait()
        kept(f).wait()
        for s in range(1, rows):
            origin = lax.rem(row + s, rows)
            outgoing(f, s, origin, origin).wait_recv()
        part = slice(f * step, (f + 1) * step)

        @pl.loop(0, hidden2 // tile)
        def _(n):
            term = contract(x_ref[:, part], w[part, span(n, tile)], 1, 0)
            if f == 0:
                proj_ref[:, span(n, tile)] = term
            else:
                proj_ref[:, span(n, tile)] += term

    for kind in range(3):
        direct(kind, 0, sibling, sibling).wait_recv()
        for s in range(1, chips):
            origin = 2 * lax.rem(chip + s, chips) + 1 - core
            relay(kind, s, origin).wait_recv()
    for kind in range(3):
        for s in range(1, chips):
            direct(kind, s, row, peer(s)).wait_send()
            relay(kind, s, peer(s)).wait_send()
        direct(kind, 0, row, sibling).wait_send()
    for kind in range(3 + CHUNKS):
        for s in range(1, cols):
            along_line(kind, s, col, lax.rem(col + s, cols)).wait_send()
    for f in range(CHUNKS):
        for s in range(1, rows):
            outgoing(f, s, row, lax.rem(row + s, rows)).wait_send()


def dispatch(rows, cols, cap, tokens, documents, questions, meta, gate_up):
    n_tok, width = tokens.shape
    n_doc, w_doc = documents.shape
    n_qry, w_qry = questions.shape
    slots = rows * cols * cap
    hidden2 = gate_up.shape[1]
    dma = pltpu.SemaphoreType.DMA
    vmem = pl.BlockSpec(memory_space=pltpu.VMEM)
    hbm = pl.BlockSpec(memory_space=pl.ANY)
    return pl.pallas_call(
        functools.partial(dispatch_kernel, rows, cols, cap),
        out_shape=(
            jax.ShapeDtypeStruct((slots, width), BF),
            jax.ShapeDtypeStruct((cols * n_doc, rows * w_doc), BF),
            jax.ShapeDtypeStruct((rows * n_qry, cols * w_qry), BF),
            jax.ShapeDtypeStruct((rows * cols,) + meta.shape, F32),
            jax.ShapeDtypeStruct((slots, hidden2), F32),
            jax.ShapeDtypeStruct((slots, cols * n_tok), BF),
        ),
        in_specs=[vmem] * 4 + [hbm],
        out_specs=[vmem, hbm, hbm, vmem, vmem, vmem],
        scratch_shapes=[
            pltpu.VMEM((cols * n_tok, width), BF),
            pltpu.VMEM((slots, width), BF),
            pltpu.VMEM((width, hidden2), BF),
            dma((3 + 2 * CHUNKS,)),
            dma((CHUNKS,)),
            dma((3 + CHUNKS, cols)),
            dma((3 + CHUNKS, cols)),
            dma((3, rows)),
            dma((3, rows)),
            dma((3, rows)),
            dma((CHUNKS, rows)),
            dma((CHUNKS, rows)),
        ],
        compiler_params=pltpu.CompilerParams(
            collective_id=0, has_side_effects=True, vmem_limit_bytes=VMEM_LIMIT
        ),
        name="dispatch",
    )(tokens, documents, questions, meta, gate_up)


def combine_kernel(
    rows, cols,
    pre_ref, dmt_ref, cot_ref, wgu_ref, xin_ref,
    tok_ref, gug_ref,
    w, x, back, ret, comb, parts, stage,
    load_sem, own_sem, es, er, fs, fr, out_sem,
):
    row, col = lax.axis_index("row"), lax.axis_index("col")
    slots = pre_ref.shape[0]
    block = slots // rows
    width = wgu_ref.shape[0]
    n_tok = cot_ref.shape[0]
    step = width // CHUNKS

    loads = [
        pltpu.make_async_copy(wgu_ref.at[span(f, step)], w.at[span(f, step)], load_sem.at[f])
        for f in range(CHUNKS)
    ]
    loads.append(pltpu.make_async_copy(xin_ref, x, load_sem.at[CHUNKS]))
    for copy in loads:
        copy.start()
    greet(rows, cols)

    def returning(f, s, origin, to):
        part = pl.ds(f * step, step)
        return remote(back.at[span(to, block), part], ret.at[span(origin, block), part],
                      es.at[f, s], er.at[f, origin], (to, col))

    def kept(f):
        part = pl.ds(f * step, step)
        return pltpu.make_async_copy(
            back.at[span(row, block), part], ret.at[span(row, block), part], own_sem.at[f]
        )

    def home(f, s, origin, to):
        part = pl.ds(f * step, step)
        return remote(comb.at[span(to, n_tok), part], parts.at[origin, :, part],
                      fs.at[f, s], fr.at[f, origin], (row, to))

    tile = 256
    for f in range(CHUNKS):
        loads[f].wait()

        @pl.loop(0, step // tile)
        def _(n):
            back[:, pl.ds(pl.multiple_of(f * step + n * tile, tile), tile)] = contract(
                pre_ref[...], w[pl.ds(pl.multiple_of(f * step + n * tile, tile), tile), :], 1, 1
            ).astype(BF)

        for s in range(1, rows):
            returning(f, s, row, lax.rem(row + s, rows)).start()
        kept(f).start()
    loads[CHUNKS].wait()

    def grad_tile(i):
        here = slice(i * step, (i + 1) * step)
        stage[i % 2] = contract(x[:, here], pre_ref[...], 0, 0).astype(BF)

    def grad_out(i):
        return pltpu.make_async_copy(
            stage.at[i % 2], gug_ref.at[pl.ds(i * step, step)], out_sem.at[i % 2]
        )

    def merge(f):
        kept(f).wait()
        for s in range(1, rows):
            origin = lax.rem(row + s, rows)
            returning(f, s, origin, origin).wait_recv()
        part = slice(f * step, (f + 1) * step)
        comb[:, part] = contract(dmt_ref[...], ret[:, part], 1, 0).astype(BF)
        for s in range(1, cols):
            home(f, s, col, lax.rem(col + s, cols)).start()

    def finish(f):
        part = slice(f * step, (f + 1) * step)
        total = cot_ref[:, part].astype(F32) + comb[span(col, n_tok), part].astype(F32)
        for s in range(1, cols):
            origin = lax.rem(col + s, cols)
            home(f, s, origin, origin).wait_recv()
            total = total + parts[origin, :, part].astype(F32)
        tok_ref[:, part] = total.astype(BF)

    for i in range(CHUNKS):
        if i >= 2:
            grad_out(i - 2).wait()
        grad_tile(i)
        grad_out(i).start()
        merge(i)
        if i >= 1:
            finish(i - 1)
    finish(CHUNKS - 1)
    for i in range(CHUNKS - 2, CHUNKS):
        grad_out(i).wait()
    for f in range(CHUNKS):
        for s in range(1, rows):
            returning(f, s, row, lax.rem(row + s, rows)).wait_send()
        for s in range(1, cols):
            home(f, s, col, lax.rem(col + s, cols)).wait_send()


def combine(rows, cols, pre_grad, dispatch_t, cot_tok, gate_up, slot_inputs):
    slots, hidden2 = pre_grad.shape
    n_tok, width = cot_tok.shape
    step = width // CHUNKS
    dma = pltpu.SemaphoreType.DMA
    vmem = pl.BlockSpec(memory_space=pltpu.VMEM)
    hbm = pl.BlockSpec(memory_space=pl.ANY)
    return pl.pallas_call(
        functools.partial(combine_kernel, rows, cols),
        out_shape=(
            jax.ShapeDtypeStruct((n_tok, width), BF),
            jax.ShapeDtypeStruct((width, hidden2), BF),
        ),
        in_specs=[vmem, vmem, vmem, hbm, hbm],
        out_specs=[vmem, hbm],
        scratch_shapes=[
            pltpu.VMEM((width, hidden2), BF),
            pltpu.VMEM((slots, width), BF),
            pltpu.VMEM((slots, width), BF),
            pltpu.VMEM((slots, width), BF),
            pltpu.VMEM((cols * n_tok, width), BF),
            pltpu.VMEM((cols, n_tok, width), BF),
            pltpu.VMEM((2, step, hidden2), BF),
            dma((CHUNKS + 1,)),
            dma((CHUNKS,)),
            dma((CHUNKS, rows)),
            dma((CHUNKS, rows)),
            dma((CHUNKS, cols)),
            dma((CHUNKS, cols)),
            dma((2,)),
        ],
        compiler_params=pltpu.CompilerParams(
            collective_id=1, has_side_effects=True, vmem_limit_bytes=VMEM_LIMIT
        ),
        name="combine",
    )(pre_grad, dispatch_t, cot_tok, gate_up, slot_inputs)


def shards(
    question_vectors,
    document_vectors,
    positive,
    tokens,
    expert_ids,
    route_weights,
    expert_gate_up,
    expert_down,
):
    rows = lax.axis_size("row")
    cols = lax.axis_size("col")
    row = lax.axis_index("row")
    col = lax.axis_index("col")
    devices_all = rows * cols
    me = row * cols + col
    n_tok, width = tokens.shape
    top = expert_ids.shape[1]
    experts_all = devices_all * expert_gate_up.shape[0]
    cap = max(2, (n_tok * top * 9 + 8 * experts_all - 1) // (8 * experts_all))
    block = cols * cap
    hidden_width = expert_down.shape[1]
    gate_up = expert_gate_up[0]
    down = expert_down[0]

    n_qry = positive.shape[0]
    pos_rows = -(-n_qry // (8 * LANES)) * 8
    pos = jnp.pad(positive, (0, pos_rows * LANES - n_qry)).astype(F32).reshape(pos_rows, LANES)
    meta = jnp.concatenate([expert_ids.T.astype(F32), route_weights.T, pos], axis=0)
    slot_inputs, docs, qrys, metas, projected, dm = dispatch(
        rows, cols, cap, tokens, document_vectors, question_vectors, meta, gate_up
    )

    ids = metas[:, :top].astype(jnp.int32)
    weights = metas[:, top : 2 * top]
    positive_all = metas.reshape(rows, cols, -1, LANES)[:, 0, 2 * top :].reshape(rows, -1)
    positive_all = positive_all[:, :n_qry].reshape(-1).astype(jnp.int32)

    scores = contract(qrys, docs, 1, 1) / sharpness_divisor
    peak = jnp.max(scores, axis=1, keepdims=True)
    grown = jnp.exp(scores - peak)
    total = jnp.sum(grown, axis=1, keepdims=True)
    onehot = (
        positive_all[:, None] == jnp.arange(docs.shape[0], dtype=jnp.int32)[None, :]
    ).astype(F32)
    dscore = ((grown / total - onehot) / sharpness_divisor).astype(BF)
    cot = (contract(dscore, docs, 1, 0) / SEQ_LEN).astype(BF)
    n_doc, w_doc = document_vectors.shape
    passage_grad = contract(
        lax.dynamic_slice_in_dim(dscore, col * n_doc, n_doc, 1),
        lax.dynamic_slice_in_dim(qrys, row * w_doc, w_doc, 1),
        0, 0,
    )

    mine = ids == me
    chosen = jnp.any(mine, axis=1)
    weight = jnp.sum(jnp.where(mine, weights, 0.0), axis=1)
    earlier = (
        lax.broadcasted_iota(jnp.int32, (n_tok, n_tok), 0)
        < lax.broadcasted_iota(jnp.int32, (n_tok, n_tok), 1)
    ).astype(BF)
    rank = contract(chosen.astype(BF), earlier, 1, 0).astype(jnp.int32)
    first = jnp.tile(jnp.arange(cols, dtype=jnp.int32) * cap, rows)[:, None]
    place = jnp.where(chosen, first + rank, -1).reshape(rows, 1, cols * n_tok)
    line_weight = weight.reshape(rows, 1, cols * n_tok)
    placed = jnp.where(
        place == jnp.arange(block, dtype=jnp.int32)[None, :, None], line_weight, 0.0
    ).astype(BF)
    line_q = cols * n_tok // SEQ_LEN
    grouped = (
        lax.broadcasted_iota(jnp.int32, (cols * n_tok, line_q), 0) // SEQ_LEN
        == lax.broadcasted_iota(jnp.int32, (cols * n_tok, line_q), 1)
    ).astype(BF)
    spread = contract(placed.reshape(-1, cols * n_tok), grouped, 1, 0).astype(BF)
    spread = spread.reshape(rows, block, line_q)

    gate_part = projected[:, :hidden_width]
    up_part = projected[:, hidden_width:]
    sigmoid_gate = jax.nn.sigmoid(gate_part)
    activated = gate_part * sigmoid_gate
    hidden = (activated * up_part).astype(BF)
    cot_down = contract(cot, down, 1, 1).astype(BF).reshape(rows, line_q, hidden_width)
    hidden_grad = lax.dot_general(
        spread, cot_down, (((2,), (1,)), ((0,), (0,))), preferred_element_type=F32
    ).reshape(-1, hidden_width)
    slope = sigmoid_gate * (1.0 + gate_part * (1.0 - sigmoid_gate))
    pre_grad = jnp.concatenate(
        [hidden_grad * up_part * slope, hidden_grad * activated], axis=1
    ).astype(BF)

    per_dev = n_tok // SEQ_LEN
    cot_own = lax.dynamic_slice_in_dim(cot, me * per_dev, per_dev, 0)
    cot_tok = jnp.repeat(cot_own, SEQ_LEN, axis=0)
    token_grad, gate_up_grad = combine(
        rows, cols, pre_grad, dm.T, cot_tok, gate_up, slot_inputs
    )

    hidden_by_query = lax.dot_general(
        spread, hidden.reshape(rows, block, hidden_width), (((1,), (1,)), ((0,), (0,))),
        preferred_element_type=F32,
    ).astype(BF).reshape(-1, hidden_width)
    down_grad = contract(hidden_by_query, cot, 0, 0).astype(BF)
    return (passage_grad, token_grad, gate_up_grad[None], down_grad[None])


def solution(mesh):
    in_specs = (
        P("row", "col"),
        P("col", "row"),
        P("row"),
        P(("row", "col"), None),
        P(("row", "col"), None),
        P(("row", "col"), None),
        P(("row", "col"), None, None),
        P(("row", "col"), None, None),
    )
    out_specs = (
        P("col", "row"),
        P(("row", "col"), None),
        P(("row", "col"), None, None),
        P(("row", "col"), None, None),
    )
    return jax.shard_map(shards, mesh=mesh, in_specs=in_specs, out_specs=out_specs, check_vma=False)
```

```python
import functools
import math

import jax
import jax.numpy as jnp
from jax import lax
from jax.experimental import pallas as pl
from jax.experimental.pallas import tpu as pltpu
from jax.sharding import PartitionSpec as P

SEQ_LEN = 8
LANES = 128
CHUNKS = 4
VMEM_LIMIT = 67_000_000

sharpness_divisor = 0.02

BF = jnp.bfloat16
F32 = jnp.float32
MESH = pl.DeviceIdType.MESH


def contract(a, b, da, db):
    return lax.dot_general(a, b, (((da,), (db,)), ((), ())), preferred_element_type=F32)


def span(index, size):
    return pl.ds(pl.multiple_of(index * size, size), size)


def remote(src, dst, send_sem, recv_sem, to):
    return pltpu.make_async_remote_copy(
        src_ref=src, dst_ref=dst, send_sem=send_sem, recv_sem=recv_sem,
        device_id=to, device_id_type=MESH,
    )


def greet(rows, cols):
    row, col = lax.axis_index("row"), lax.axis_index("col")
    barrier = pltpu.get_barrier_semaphore()
    for s in range(1, rows):
        pl.semaphore_signal(
            barrier, inc=1, device_id=(lax.rem(row + s, rows), col), device_id_type=MESH
        )
    for s in range(1, cols):
        pl.semaphore_signal(
            barrier, inc=1, device_id=(row, lax.rem(col + s, cols)), device_id_type=MESH
        )
    pl.semaphore_wait(barrier, rows + cols - 2)


def dispatch_kernel(
    rows, cols, cap, top,
    tok_ref, doc_ref, qry_ref, meta_ref, wgu_ref,
    x_ref, docs_ref, qrys_ref, metas_ref, proj_ref, dm_ref,
    tokc, packed, w, own_sem, w_sem, zs, zr, gs, gr, rs, ds, dr,
):
    row, col = lax.axis_index("row"), lax.axis_index("col")
    n_tok, width = tok_ref.shape
    n_doc, w_doc = doc_ref.shape
    n_qry, w_qry = qry_ref.shape
    step = width // CHUNKS
    block = cols * cap
    chips = rows // 2
    core = lax.rem(row, 2)
    chip = lax.div(row, 2)
    sibling = row + 1 - 2 * core

    def doc_strip(r):
        return docs_ref.at[:, span(r, w_doc)]

    def qry_strip(r):
        return qrys_ref.at[span(r, n_qry), :]

    def meta_strip(r):
        return metas_ref.at[pl.ds(r * cols, cols)]

    strips = (meta_strip, doc_strip, qry_strip)

    def line_piece(kind, c):
        if kind == 0:
            return meta_ref, metas_ref.at[row * cols + c]
        if kind == 1:
            return doc_ref, docs_ref.at[span(c, n_doc), span(row, w_doc)]
        if kind == 2:
            return qry_ref, qrys_ref.at[span(row, n_qry), span(c, w_qry)]
        f = kind - 3
        part = pl.ds(f * step, step)
        return tok_ref.at[:, part], tokc.at[span(c, n_tok), part]

    def along_line(kind, s, origin, to):
        src, dst = line_piece(kind, origin)
        return remote(src, dst, zs.at[kind, s], zr.at[kind, origin], (row, to))

    own = []
    for kind in range(3 + CHUNKS):
        src, dst = line_piece(kind, col)
        own.append(pltpu.make_async_copy(src, dst, own_sem.at[kind]))
    loads = [
        pltpu.make_async_copy(wgu_ref.at[span(f, step)], w.at[span(f, step)], w_sem.at[f])
        for f in range(CHUNKS)
    ]
    for copy in own:
        copy.start()
    for copy in loads:
        copy.start()
    greet(rows, cols)
    for kind in range(3 + CHUNKS):
        for s in range(1, cols):
            along_line(kind, s, col, lax.rem(col + s, cols)).start()

    def line_arrived(kind):
        own[kind].wait()
        for s in range(1, cols):
            origin = lax.rem(col + s, cols)
            along_line(kind, s, origin, origin).wait_recv()

    def peer(s):
        return 2 * lax.rem(chip + s, chips) + core

    def direct(kind, s, origin, to):
        return remote(strips[kind](origin), strips[kind](origin), gs.at[kind, s],
                      gr.at[kind, origin], (to, col))

    def relay(kind, s, origin):
        return remote(strips[kind](origin), strips[kind](origin), rs.at[kind, s],
                      gr.at[kind, origin], (sibling, col))

    for kind in range(3):
        line_arrived(kind)
        for s in range(1, chips):
            direct(kind, s, row, peer(s)).start()
        direct(kind, 0, row, sibling).start()

    target = (
        lax.broadcasted_iota(jnp.int32, (rows, n_tok), 0) * cols + col
    ).astype(F32)
    before = (
        lax.broadcasted_iota(jnp.int32, (n_tok, n_tok), 0)
        < lax.broadcasted_iota(jnp.int32, (n_tok, n_tok), 1)
    ).astype(BF)
    slot = lax.broadcasted_iota(jnp.int32, (block, n_tok), 0).astype(F32)
    for c in range(cols):
        ids = metas_ref[row * cols + c]
        hit = jnp.zeros((rows, n_tok), F32)
        for k in range(top):
            hit = hit + (ids[k : k + 1, :] == target).astype(F32)
        rank = contract(hit.astype(BF), before, 1, 0)
        place = jnp.where(hit > 0.5, rank + float(c * cap), -1.0)
        for r in range(rows):
            dm_ref[r * block : (r + 1) * block, c * n_tok : (c + 1) * n_tok] = jnp.where(
                slot == place[r : r + 1, :], 1.0, 0.0
            ).astype(BF)

    def outgoing(f, s, origin, to):
        part = pl.ds(f * step, step)
        return remote(packed.at[span(to, block), part], x_ref.at[span(origin, block), part],
                      ds.at[f, s], dr.at[f, origin], (to, col))

    def kept(f):
        part = pl.ds(f * step, step)
        return pltpu.make_async_copy(
            packed.at[span(row, block), part], x_ref.at[span(row, block), part],
            own_sem.at[3 + CHUNKS + f],
        )

    pair = 2 * block
    for f in range(CHUNKS):
        line_arrived(3 + f)
        part = slice(f * step, (f + 1) * step)

        @pl.loop(0, rows // 2)
        def _(m):
            packed[span(m, pair), part] = contract(
                dm_ref[span(m, pair), :], tokc[:, part], 1, 0
            ).astype(BF)

        for s in range(1, rows):
            outgoing(f, s, row, lax.rem(row + s, rows)).start()
        kept(f).start()

    for kind in range(3):
        for s in range(1, chips):
            origin = peer(s)
            direct(kind, s, origin, origin).wait_recv()
            relay(kind, s, origin).start()

    hidden2 = proj_ref.shape[1]
    tile = 512
    for f in range(CHUNKS):
        loads[f].wait()
        kept(f).wait()
        for s in range(1, rows):
            origin = lax.rem(row + s, rows)
            outgoing(f, s, origin, origin).wait_recv()
        part = slice(f * step, (f + 1) * step)

        @pl.loop(0, hidden2 // tile)
        def _(n):
            term = contract(x_ref[:, part], w[part, span(n, tile)], 1, 0)
            if f == 0:
                proj_ref[:, span(n, tile)] = term
            else:
                proj_ref[:, span(n, tile)] += term

    for kind in range(3):
        direct(kind, 0, sibling, sibling).wait_recv()
        for s in range(1, chips):
            origin = 2 * lax.rem(chip + s, chips) + 1 - core
            relay(kind, s, origin).wait_recv()
    for kind in range(3):
        for s in range(1, chips):
            direct(kind, s, row, peer(s)).wait_send()
            relay(kind, s, peer(s)).wait_send()
        direct(kind, 0, row, sibling).wait_send()
    for kind in range(3 + CHUNKS):
        for s in range(1, cols):
            along_line(kind, s, col, lax.rem(col + s, cols)).wait_send()
    for f in range(CHUNKS):
        for s in range(1, rows):
            outgoing(f, s, row, lax.rem(row + s, rows)).wait_send()


def dispatch(rows, cols, cap, top, tokens, documents, questions, meta, gate_up):
    n_tok, width = tokens.shape
    n_doc, w_doc = documents.shape
    n_qry, w_qry = questions.shape
    slots = rows * cols * cap
    hidden2 = gate_up.shape[1]
    dma = pltpu.SemaphoreType.DMA
    vmem = pl.BlockSpec(memory_space=pltpu.VMEM)
    hbm = pl.BlockSpec(memory_space=pl.ANY)
    return pl.pallas_call(
        functools.partial(dispatch_kernel, rows, cols, cap, top),
        out_shape=(
            jax.ShapeDtypeStruct((slots, width), BF),
            jax.ShapeDtypeStruct((cols * n_doc, rows * w_doc), BF),
            jax.ShapeDtypeStruct((rows * n_qry, cols * w_qry), BF),
            jax.ShapeDtypeStruct((rows * cols,) + meta.shape, F32),
            jax.ShapeDtypeStruct((slots, hidden2), F32),
            jax.ShapeDtypeStruct((slots, cols * n_tok), BF),
        ),
        in_specs=[vmem] * 4 + [hbm],
        out_specs=[vmem, hbm, hbm, vmem, vmem, vmem],
        scratch_shapes=[
            pltpu.VMEM((cols * n_tok, width), BF),
            pltpu.VMEM((slots, width), BF),
            pltpu.VMEM((width, hidden2), BF),
            dma((3 + 2 * CHUNKS,)),
            dma((CHUNKS,)),
            dma((3 + CHUNKS, cols)),
            dma((3 + CHUNKS, cols)),
            dma((3, rows)),
            dma((3, rows)),
            dma((3, rows)),
            dma((CHUNKS, rows)),
            dma((CHUNKS, rows)),
        ],
        compiler_params=pltpu.CompilerParams(
            collective_id=0, has_side_effects=True, vmem_limit_bytes=VMEM_LIMIT
        ),
        name="dispatch",
    )(tokens, documents, questions, meta, gate_up)


def combine_kernel(
    rows, cols,
    pre_ref, dmt_ref, cot_ref, wgu_ref, xin_ref,
    tok_ref, gug_ref,
    w, x, back, ret, comb, parts, stage,
    load_sem, own_sem, es, er, fs, fr, out_sem,
):
    row, col = lax.axis_index("row"), lax.axis_index("col")
    slots = pre_ref.shape[0]
    block = slots // rows
    width = wgu_ref.shape[0]
    n_tok = cot_ref.shape[0]
    step = width // CHUNKS

    loads = [
        pltpu.make_async_copy(wgu_ref.at[span(f, step)], w.at[span(f, step)], load_sem.at[f])
        for f in range(CHUNKS)
    ]
    loads.append(pltpu.make_async_copy(xin_ref, x, load_sem.at[CHUNKS]))
    for copy in loads:
        copy.start()
    greet(rows, cols)

    def returning(f, s, origin, to):
        part = pl.ds(f * step, step)
        return remote(back.at[span(to, block), part], ret.at[span(origin, block), part],
                      es.at[f, s], er.at[f, origin], (to, col))

    def kept(f):
        part = pl.ds(f * step, step)
        return pltpu.make_async_copy(
            back.at[span(row, block), part], ret.at[span(row, block), part], own_sem.at[f]
        )

    def home(f, s, origin, to):
        part = pl.ds(f * step, step)
        return remote(comb.at[span(to, n_tok), part], parts.at[origin, :, part],
                      fs.at[f, s], fr.at[f, origin], (row, to))

    tile = 256
    for f in range(CHUNKS):
        loads[f].wait()

        @pl.loop(0, step // tile)
        def _(n):
            back[:, pl.ds(pl.multiple_of(f * step + n * tile, tile), tile)] = contract(
                pre_ref[...], w[pl.ds(pl.multiple_of(f * step + n * tile, tile), tile), :], 1, 1
            ).astype(BF)

        for s in range(1, rows):
            returning(f, s, row, lax.rem(row + s, rows)).start()
        kept(f).start()
    loads[CHUNKS].wait()

    def grad_tile(i):
        here = slice(i * step, (i + 1) * step)
        stage[i % 2] = contract(x[:, here], pre_ref[...], 0, 0).astype(BF)

    def grad_out(i):
        return pltpu.make_async_copy(
            stage.at[i % 2], gug_ref.at[pl.ds(i * step, step)], out_sem.at[i % 2]
        )

    def merge(f):
        kept(f).wait()
        for s in range(1, rows):
            origin = lax.rem(row + s, rows)
            returning(f, s, origin, origin).wait_recv()
        part = slice(f * step, (f + 1) * step)
        comb[:, part] = contract(dmt_ref[...], ret[:, part], 1, 0).astype(BF)
        for s in range(1, cols):
            home(f, s, col, lax.rem(col + s, cols)).start()

    def finish(f):
        part = slice(f * step, (f + 1) * step)
        total = cot_ref[:, part].astype(F32) + comb[span(col, n_tok), part].astype(F32)
        for s in range(1, cols):
            origin = lax.rem(col + s, cols)
            home(f, s, origin, origin).wait_recv()
            total = total + parts[origin, :, part].astype(F32)
        tok_ref[:, part] = total.astype(BF)

    for i in range(CHUNKS):
        if i >= 2:
            grad_out(i - 2).wait()
        grad_tile(i)
        grad_out(i).start()
        merge(i)
        if i >= 1:
            finish(i - 1)
    finish(CHUNKS - 1)
    for i in range(CHUNKS - 2, CHUNKS):
        grad_out(i).wait()
    for f in range(CHUNKS):
        for s in range(1, rows):
            returning(f, s, row, lax.rem(row + s, rows)).wait_send()
        for s in range(1, cols):
            home(f, s, col, lax.rem(col + s, cols)).wait_send()


def combine(rows, cols, pre_grad, dispatch_t, cot_tok, gate_up, slot_inputs):
    slots, hidden2 = pre_grad.shape
    n_tok, width = cot_tok.shape
    step = width // CHUNKS
    dma = pltpu.SemaphoreType.DMA
    vmem = pl.BlockSpec(memory_space=pltpu.VMEM)
    hbm = pl.BlockSpec(memory_space=pl.ANY)
    return pl.pallas_call(
        functools.partial(combine_kernel, rows, cols),
        out_shape=(
            jax.ShapeDtypeStruct((n_tok, width), BF),
            jax.ShapeDtypeStruct((width, hidden2), BF),
        ),
        in_specs=[vmem, vmem, vmem, hbm, hbm],
        out_specs=[vmem, hbm],
        scratch_shapes=[
            pltpu.VMEM((width, hidden2), BF),
            pltpu.VMEM((slots, width), BF),
            pltpu.VMEM((slots, width), BF),
            pltpu.VMEM((slots, width), BF),
            pltpu.VMEM((cols * n_tok, width), BF),
            pltpu.VMEM((cols, n_tok, width), BF),
            pltpu.VMEM((2, step, hidden2), BF),
            dma((CHUNKS + 1,)),
            dma((CHUNKS,)),
            dma((CHUNKS, rows)),
            dma((CHUNKS, rows)),
            dma((CHUNKS, cols)),
            dma((CHUNKS, cols)),
            dma((2,)),
        ],
        compiler_params=pltpu.CompilerParams(
            collective_id=1, has_side_effects=True, vmem_limit_bytes=VMEM_LIMIT
        ),
        name="combine",
    )(pre_grad, dispatch_t, cot_tok, gate_up, slot_inputs)


def fused_kernel(
    rows, cols, cap, first_widths, last_widths,
    tok_ref, doc_ref, qry_ref, pos_ref, ids_ref, rw_ref, wgu_ref, down_ref,
    passage_ref, out_ref, gug_ref, dg_ref,
    meta, metas, tokc, packed, x, w, down, proj, dm, dmt, place, weight, placed, group,
    docs, qrow, qcols, dsc, cot, cot_down, spread, hgrad, hidden, pre, ret, comb, parts,
    hbq, stage,
    own_sem, load_sem, zs, zr, gs, gr, rs, ds, dr, qs, qr, ss, sr, es, er, fs, fr, out_sem,
):
    row, col = lax.axis_index("row"), lax.axis_index("col")
    me = row * cols + col
    n_tok, width = tok_ref.shape
    n_doc, w_doc = doc_ref.shape
    n_qry, w_qry = qry_ref.shape
    top = ids_ref.shape[1]
    ff = down.shape[0]
    slots = x.shape[0]
    block = slots // rows
    pair = 2 * block
    chips = rows // 2
    core = lax.rem(row, 2)
    chip = lax.div(row, 2)
    sibling = row + 1 - 2 * core
    line_q = cols * n_tok // SEQ_LEN

    def cuts(widths):
        edges, at = [], 0
        for size in widths:
            edges.append((at, size))
            at += size
        return edges

    first, last = cuts(first_widths), cuts(last_widths)
    n_first, n_last = len(first), len(last)

    def line_piece(kind, c):
        if kind == 0:
            return doc_ref, docs.at[span(c, n_doc), span(row, w_doc)]
        if kind == 1:
            return meta, metas.at[row * cols + c]
        if kind == 2:
            return qry_ref, qrow.at[:, span(c, w_qry)]
        at, size = first[kind - 3]
        return tok_ref.at[:, pl.ds(at, size)], tokc.at[span(c, n_tok), pl.ds(at, size)]

    def along_line(kind, s, origin, to):
        src, dst = line_piece(kind, origin)
        return remote(src, dst, zs.at[kind, s], zr.at[kind, origin], (row, to))

    def own(kind):
        src, dst = line_piece(kind, col)
        return pltpu.make_async_copy(src, dst, own_sem.at[kind])

    loads = [
        pltpu.make_async_copy(wgu_ref.at[pl.ds(at, size)], w.at[pl.ds(at, size)], load_sem.at[f])
        for f, (at, size) in enumerate(first)
    ]
    loads.append(pltpu.make_async_copy(down_ref, down, load_sem.at[n_first]))

    meta[:top] = ids_ref[...].astype(F32).T
    meta[top:] = rw_ref[...].T
    greet(rows, cols)
    order = [0, 1, 3, 2] + list(range(4, 3 + n_first))
    for kind in order:
        for s in range(1, cols):
            along_line(kind, s, col, lax.rem(col + s, cols)).start()
        own(kind).start()
    for copy in loads:
        copy.start()

    def line_arrived(kind):
        own(kind).wait()
        for s in range(1, cols):
            origin = lax.rem(col + s, cols)
            along_line(kind, s, origin, origin).wait_recv()

    def strip(kind, r):
        if kind == 0:
            return docs.at[:, span(r, w_doc)]
        return metas.at[pl.ds(r * cols, cols)]

    def peer(s):
        return 2 * lax.rem(chip + s, chips) + core

    def direct(kind, s, origin, to):
        return remote(strip(kind, origin), strip(kind, origin), gs.at[kind, s],
                      gr.at[kind, origin], (to, col))

    def relay(kind, s, origin):
        return remote(strip(kind, origin), strip(kind, origin), rs.at[kind, s],
                      gr.at[kind, origin], (sibling, col))

    def spread_out(kind):
        line_arrived(kind)
        for s in range(1, chips):
            direct(kind, s, row, peer(s)).start()
        direct(kind, 0, row, sibling).start()

    def pass_on(kind):
        for s in range(1, chips):
            origin = peer(s)
            direct(kind, s, origin, origin).wait_recv()
            relay(kind, s, origin).start()

    def all_here(kind):
        direct(kind, 0, sibling, sibling).wait_recv()
        for s in range(1, chips):
            relay(kind, s, 2 * lax.rem(chip + s, chips) + 1 - core).wait_recv()

    before = (
        lax.broadcasted_iota(jnp.int32, (n_tok, n_tok), 0)
        < lax.broadcasted_iota(jnp.int32, (n_tok, n_tok), 1)
    ).astype(BF)
    slot = lax.broadcasted_iota(jnp.int32, (block, n_tok), 0).astype(F32)

    def outgoing(f, s, origin, to):
        part = pl.ds(*first[f])
        return remote(packed.at[span(to, block), part], x.at[span(origin, block), part],
                      ds.at[f, s], dr.at[f, origin], (to, col))

    def kept(f):
        part = pl.ds(*first[f])
        return pltpu.make_async_copy(
            packed.at[span(row, block), part], x.at[span(row, block), part],
            own_sem.at[3 + n_first + f],
        )

    def pack(f):
        line_arrived(3 + f)
        part = pl.ds(*first[f])

        @pl.loop(0, chips)
        def _(m):
            packed[span(m, pair), part] = contract(
                dm[span(m, pair), :], tokc[:, part], 1, 0
            ).astype(BF)

        for s in range(1, rows):
            outgoing(f, s, row, lax.rem(row + s, rows)).start()
        kept(f).start()

    tile = 512

    def project(f):
        loads[f].wait()
        kept(f).wait()
        for s in range(1, rows):
            origin = lax.rem(row + s, rows)
            outgoing(f, s, origin, origin).wait_recv()
        part = pl.ds(*first[f])

        @pl.loop(0, 2 * ff // tile)
        def _(n):
            term = contract(x[:, part], w[part, span(n, tile)], 1, 0)
            if f == 0:
                proj[:, span(n, tile)] = term
            else:
                proj[:, span(n, tile)] += term

    def query_piece(origin, to):
        return qrow.at[:, span(to, w_doc)], qcols.at[span(origin, n_qry), :]

    def queries(s, origin, to):
        src, dst = query_piece(origin, to)
        return remote(src, dst, qs.at[s], qr.at[origin], (to, col))

    def own_queries():
        src, dst = query_piece(row, row)
        return pltpu.make_async_copy(src, dst, own_sem.at[3 + 2 * n_first])

    def scored(s, origin, to):
        rows_of = dsc.at[span(origin, n_qry), :]
        return remote(rows_of, rows_of, ss.at[s], sr.at[origin], (to, col))

    spread_out(0)
    spread_out(1)
    target = (
        lax.broadcasted_iota(jnp.int32, (rows, n_tok), 0) * cols + col
    ).astype(F32)
    for c in range(cols):
        ids = metas[row * cols + c, :top]
        hit = jnp.zeros((rows, n_tok), F32)
        for k in range(top):
            hit = hit + (ids[k : k + 1, :] == target).astype(F32)
        rank = contract(hit.astype(BF), before, 1, 0)
        spot = jnp.where(hit > 0.5, rank + float(c * cap), -1.0)
        for r in range(rows):
            dm[r * block : (r + 1) * block, c * n_tok : (c + 1) * n_tok] = jnp.where(
                slot == spot[r : r + 1, :], 1.0, 0.0
            ).astype(BF)
    pack(0)

    pass_on(0)
    pass_on(1)
    line_arrived(2)
    for s in range(1, rows):
        queries(s, row, lax.rem(row + s, rows)).start()
    own_queries().start()
    all_here(0)
    scores = contract(qrow[...], docs[...], 1, 1) / sharpness_divisor
    peak = jnp.max(scores, axis=1, keepdims=True)
    grown = jnp.exp(scores - peak)
    total = jnp.sum(grown, axis=1, keepdims=True)
    onehot = (
        pos_ref[...] == lax.broadcasted_iota(jnp.int32, scores.shape, 1)
    ).astype(F32)
    dsc[span(row, n_qry), :] = ((grown / total - onehot) / sharpness_divisor).astype(BF)
    for c in range(cols):
        here = slice(c * n_tok, (c + 1) * n_tok)
        dmt[here, :] = dm[:, here].astype(F32).T.astype(BF)
    for s in range(1, rows):
        scored(s, row, lax.rem(row + s, rows)).start()
    pack(1)

    all_here(1)
    lines = rows * cols
    each = lax.broadcasted_iota(jnp.int32, (lines, n_tok), 0)
    mine = me.astype(F32)
    chosen = jnp.zeros((lines, n_tok), F32)
    amount = jnp.zeros((lines, n_tok), F32)
    for b in range(lines):
        hit = (metas[b, :top] == mine).astype(F32)
        found = jnp.sum(hit, axis=0, keepdims=True)
        value = jnp.sum(hit * metas[b, top:], axis=0, keepdims=True)
        chosen = jnp.where(each == b, found, chosen)
        amount = jnp.where(each == b, value, amount)
    rank = contract(chosen.astype(BF), before, 1, 0)
    begin = (lax.rem(each, cols) * cap).astype(F32)
    place[...] = jnp.where(chosen > 0.5, rank + begin, -1.0)
    weight[...] = amount
    group[...] = (
        lax.broadcasted_iota(jnp.int32, (cols * n_tok, line_q), 0) // SEQ_LEN
        == lax.broadcasted_iota(jnp.int32, (cols * n_tok, line_q), 1)
    ).astype(BF)

    @pl.loop(0, rows)
    def _(r):
        for c in range(cols):
            here = pl.ds(r * cols + c, 1)
            placed[:, c * n_tok : (c + 1) * n_tok] = jnp.where(
                slot == place[here, :], weight[here, :], 0.0
            ).astype(BF)
        spread[span(r, block), :] = contract(placed[...], group[...], 1, 0).astype(BF)

    project(0)
    pack(2)

    for s in range(1, rows):
        origin = lax.rem(row + s, rows)
        scored(s, origin, origin).wait_recv()

    @pl.loop(0, width // tile)
    def _(n):
        cot[:, span(n, tile)] = (
            contract(dsc[...], docs[:, span(n, tile)], 1, 0) / SEQ_LEN
        ).astype(BF)

    loads[n_first].wait()
    small = 256

    @pl.loop(0, ff // small)
    def _(n):
        cot_down[:, span(n, small)] = contract(
            cot[...], down[span(n, small), :], 1, 1
        ).astype(BF)

    project(1)
    for f in range(3, n_first):
        pack(f)
        if f < n_first - 1 or f > 3:
            project(f - 1)
    for s in range(1, rows):
        origin = lax.rem(row + s, rows)
        queries(s, origin, origin).wait_recv()
    own_queries().wait()
    passage_ref[...] = contract(dsc[:, span(col, n_doc)], qcols[...], 0, 0)
    if n_first == 4:
        project(2)

    def returning(f, s, origin, to):
        part = pl.ds(*last[f])
        return remote(packed.at[span(to, block), part], ret.at[span(origin, block), part],
                      es.at[f, s], er.at[f, origin], (to, col))

    def held(f):
        part = pl.ds(*last[f])
        return pltpu.make_async_copy(
            packed.at[span(row, block), part], ret.at[span(row, block), part],
            own_sem.at[4 + 2 * n_first + f],
        )

    def home(f, s, origin, to):
        part = pl.ds(*last[f])
        return remote(comb.at[span(to, n_tok), part], parts.at[origin, :, part],
                      fs.at[f, s], fr.at[f, origin], (row, to))

    drained = set()

    def drain(g):
        low, size = last[g]
        for f, (at, wide) in enumerate(first):
            if f not in drained and at < low + size and low < at + wide:
                drained.add(f)
                for s in range(1, rows):
                    outgoing(f, s, row, lax.rem(row + s, rows)).wait_send()

    f_end = n_first - 1
    loads[f_end].wait()
    kept(f_end).wait()
    drain(0)
    end = pl.ds(*first[f_end])
    begin_cols = pl.ds(*last[0])
    lane = 128

    def offset_of(r):
        return lax.rem(r - row + rows, rows)

    for s in range(chips):
        other = lax.rem(chip + s, chips)
        two = (2 * other + core, 2 * other + 1 - core)
        for k, origin in enumerate(two):
            if s == 0 and k == 0:
                continue
            outgoing(f_end, offset_of(origin), origin, origin).wait_recv()
        here = span(other, pair)

        @pl.loop(0, 2 * ff // tile)
        def _(n):
            proj[here, span(n, tile)] += contract(x[here, end], w[end, span(n, tile)], 1, 0)

        for k in range(2):
            r = 2 * other + k
            at = span(r, block)
            hgrad[...] = contract(spread[at, :], cot_down[span(r, line_q), :], 1, 0)

            @pl.loop(0, ff // lane)
            def _(n):
                left = span(n, lane)
                right = pl.ds(pl.multiple_of(ff + n * lane, lane), lane)
                gate, up = proj[at, left], proj[at, right]
                sig = jax.nn.sigmoid(gate)
                act = gate * sig
                grad = hgrad[:, left]
                hidden[at, left] = (act * up).astype(BF)
                pre[at, left] = (grad * up * (sig * (1.0 + gate * (1.0 - sig)))).astype(BF)
                pre[at, right] = (grad * act).astype(BF)

        packed[here, begin_cols] = contract(pre[here, :], w[begin_cols, :], 1, 1).astype(BF)
        for k, to in enumerate(two):
            if s == 0 and k == 0:
                held(0).start()
            else:
                returning(0, offset_of(to), row, to).start()

    for f in range(1, n_last):
        at, size = last[f]
        drain(f)

        @pl.loop(0, size // small)
        def _(n):
            part = pl.ds(pl.multiple_of(at + n * small, small), small)
            packed[:, part] = contract(pre[...], w[part, :], 1, 1).astype(BF)

        for s in range(1, rows):
            returning(f, s, row, lax.rem(row + s, rows)).start()
        held(f).start()

    @pl.loop(0, rows)
    def _(r):
        hbq[span(r, line_q), :] = contract(
            spread[span(r, block), :], hidden[span(r, block), :], 0, 0
        ).astype(BF)

    n_gate, n_down = width // small, ff // small

    def gate_out(i):
        return pltpu.make_async_copy(
            stage.at[i % 2, :, pl.ds(0, 2 * ff)], gug_ref.at[pl.ds(i * small, small)],
            out_sem.at[i % 2],
        )

    def down_out(i):
        j = n_gate + i
        return pltpu.make_async_copy(
            stage.at[j % 2], dg_ref.at[pl.ds(i * small, small)], out_sem.at[j % 2]
        )

    def grad_out(i):
        return gate_out(i) if i < n_gate else down_out(i - n_gate)

    def grad_tile(i):
        if i >= 2:
            grad_out(i - 2).wait()
        if i < n_gate:
            stage[i % 2, :, : 2 * ff] = contract(
                x[:, i * small : (i + 1) * small], pre[...], 0, 0
            ).astype(BF)
        else:
            j = i - n_gate
            stage[i % 2] = contract(hbq[:, j * small : (j + 1) * small], cot[...], 0, 0).astype(BF)
        grad_out(i).start()

    def merge(f):
        held(f).wait()
        for s in range(1, rows):
            origin = lax.rem(row + s, rows)
            returning(f, s, origin, origin).wait_recv()
        part = pl.ds(*last[f])
        comb[:, part] = contract(dmt[...], ret[:, part], 1, 0).astype(BF)
        for s in range(1, cols):
            home(f, s, col, lax.rem(col + s, cols)).start()

    per_dev = n_tok // SEQ_LEN
    repeat = (
        lax.broadcasted_iota(jnp.int32, (n_tok, per_dev), 0) // SEQ_LEN
        == lax.broadcasted_iota(jnp.int32, (n_tok, per_dev), 1)
    ).astype(BF)

    def finish(f):
        part = pl.ds(*last[f])
        sums = contract(repeat, cot[span(me, per_dev), part], 1, 0)
        sums = sums + comb[span(col, n_tok), part].astype(F32)
        for s in range(1, cols):
            origin = lax.rem(col + s, cols)
            home(f, s, origin, origin).wait_recv()
            sums = sums + parts[origin, :, part].astype(F32)
        out_ref[:, part] = sums.astype(BF)

    tiles = n_gate + n_down
    done = 0
    for f in range(n_last):
        merge(f)
        if f >= 1:
            finish(f - 1)
        until = tiles * (f + 1) // n_last
        for i in range(done, until):
            grad_tile(i)
        done = until
    finish(n_last - 1)
    for i in range(tiles - 2, tiles):
        grad_out(i).wait()

    for kind in range(2):
        for s in range(1, chips):
            direct(kind, s, row, peer(s)).wait_send()
            relay(kind, s, peer(s)).wait_send()
        direct(kind, 0, row, sibling).wait_send()
    for kind in range(3 + n_first):
        for s in range(1, cols):
            along_line(kind, s, col, lax.rem(col + s, cols)).wait_send()
    for s in range(1, rows):
        to = lax.rem(row + s, rows)
        queries(s, row, to).wait_send()
        scored(s, row, to).wait_send()
        for f in range(n_last):
            returning(f, s, row, to).wait_send()
    for f in range(n_last):
        for s in range(1, cols):
            home(f, s, col, lax.rem(col + s, cols)).wait_send()


def fused_plan(rows, cols, cap, top, tokens, documents, questions, down):
    n_tok, width = tokens.shape
    n_doc, w_doc = documents.shape
    n_qry = questions.shape[0]
    ff = down.shape[0]
    block = cols * cap
    slots = rows * block
    line = cols * n_tok
    line_q = line // SEQ_LEN
    n_all = rows * n_qry
    stage_rows = 256
    return [
        ((2 * top, n_tok), F32),
        ((rows * cols, 2 * top, n_tok), F32),
        ((line, width), BF),
        ((slots, width), BF),
        ((slots, width), BF),
        ((width, 2 * ff), BF),
        ((ff, width), BF),
        ((slots, 2 * ff), F32),
        ((slots, line), BF),
        ((line, slots), BF),
        ((rows * cols, n_tok), F32),
        ((rows * cols, n_tok), F32),
        ((block, line), BF),
        ((line, line_q), BF),
        ((cols * n_doc, width), BF),
        ((n_qry, width), BF),
        ((n_all, w_doc), BF),
        ((n_all, cols * n_doc), BF),
        ((n_all, width), BF),
        ((n_all, ff), BF),
        ((slots, line_q), BF),
        ((block, ff), F32),
        ((slots, ff), BF),
        ((slots, 2 * ff), BF),
        ((slots, width), BF),
        ((line, width), BF),
        ((cols, n_tok, width), BF),
        ((n_all, ff), BF),
        ((2, stage_rows, max(width, 2 * ff)), BF),
    ]


def plan_bytes(plan):
    return sum(math.prod(shape) * jnp.dtype(kind).itemsize for shape, kind in plan)


def fused(rows, cols, cap, plan, tokens, documents, questions, positive, ids, weights, gate_up, down):
    n_tok, width = tokens.shape
    n_doc, w_doc = documents.shape
    hidden2 = gate_up.shape[1]
    first = [width // 4] * 4
    last = [width // 4] * 3 + [width // 8] * 2
    dma = pltpu.SemaphoreType.DMA
    vmem = pl.BlockSpec(memory_space=pltpu.VMEM)
    hbm = pl.BlockSpec(memory_space=pl.ANY)
    n_first, n_last = len(first), len(last)
    return pl.pallas_call(
        functools.partial(fused_kernel, rows, cols, cap, first, last),
        out_shape=(
            jax.ShapeDtypeStruct((n_doc, w_doc), F32),
            jax.ShapeDtypeStruct((n_tok, width), BF),
            jax.ShapeDtypeStruct((width, hidden2), BF),
            jax.ShapeDtypeStruct(down.shape, BF),
        ),
        in_specs=[vmem] * 6 + [hbm] * 2,
        out_specs=[vmem, vmem, hbm, hbm],
        scratch_shapes=[pltpu.VMEM(shape, kind) for shape, kind in plan]
        + [
            dma((4 + 2 * n_first + n_last,)),
            dma((n_first + 1,)),
            dma((3 + n_first, cols)),
            dma((3 + n_first, cols)),
            dma((2, rows)),
            dma((2, rows)),
            dma((2, rows)),
            dma((n_first, rows)),
            dma((n_first, rows)),
            dma((rows,)),
            dma((rows,)),
            dma((rows,)),
            dma((rows,)),
            dma((n_last, rows)),
            dma((n_last, rows)),
            dma((n_last, cols)),
            dma((n_last, cols)),
            dma((2,)),
        ],
        compiler_params=pltpu.CompilerParams(
            collective_id=2, has_side_effects=True, vmem_limit_bytes=VMEM_LIMIT
        ),
        name="fused",
    )(tokens, documents, questions, positive[:, None], ids, weights, gate_up, down)


def shards(
    question_vectors,
    document_vectors,
    positive,
    tokens,
    expert_ids,
    route_weights,
    expert_gate_up,
    expert_down,
):
    rows = lax.axis_size("row")
    cols = lax.axis_size("col")
    row = lax.axis_index("row")
    col = lax.axis_index("col")
    devices_all = rows * cols
    me = row * cols + col
    n_tok, width = tokens.shape
    top = expert_ids.shape[1]
    experts_all = devices_all * expert_gate_up.shape[0]
    cap = max(2, (n_tok * top * 9 + 8 * experts_all - 1) // (8 * experts_all))
    block = cols * cap
    hidden_width = expert_down.shape[1]
    gate_up = expert_gate_up[0]
    down = expert_down[0]

    plan = fused_plan(rows, cols, cap, top, tokens, document_vectors, question_vectors, down)
    if plan_bytes(plan) < VMEM_LIMIT - 6_000_000:
        passage_grad, token_grad, gate_up_grad, down_grad = fused(
            rows, cols, cap, plan, tokens, document_vectors, question_vectors, positive,
            expert_ids, route_weights, gate_up, down,
        )
        return (passage_grad, token_grad, gate_up_grad[None], down_grad[None])

    n_qry = positive.shape[0]
    pos_rows = -(-n_qry // (8 * LANES)) * 8
    pos = jnp.pad(positive, (0, pos_rows * LANES - n_qry)).astype(F32).reshape(pos_rows, LANES)
    meta = jnp.concatenate([expert_ids.T.astype(F32), route_weights.T, pos], axis=0)
    slot_inputs, docs, qrys, metas, projected, dm = dispatch(
        rows, cols, cap, top, tokens, document_vectors, question_vectors, meta, gate_up
    )

    ids = metas[:, :top].astype(jnp.int32)
    weights = metas[:, top : 2 * top]
    positive_all = metas.reshape(rows, cols, -1, LANES)[:, 0, 2 * top :].reshape(rows, -1)
    positive_all = positive_all[:, :n_qry].reshape(-1).astype(jnp.int32)

    scores = contract(qrys, docs, 1, 1) / sharpness_divisor
    peak = jnp.max(scores, axis=1, keepdims=True)
    grown = jnp.exp(scores - peak)
    total = jnp.sum(grown, axis=1, keepdims=True)
    onehot = (
        positive_all[:, None] == jnp.arange(docs.shape[0], dtype=jnp.int32)[None, :]
    ).astype(F32)
    dscore = ((grown / total - onehot) / sharpness_divisor).astype(BF)
    cot = (contract(dscore, docs, 1, 0) / SEQ_LEN).astype(BF)
    n_doc, w_doc = document_vectors.shape
    passage_grad = contract(
        lax.dynamic_slice_in_dim(dscore, col * n_doc, n_doc, 1),
        lax.dynamic_slice_in_dim(qrys, row * w_doc, w_doc, 1),
        0, 0,
    )

    mine = ids == me
    chosen = jnp.any(mine, axis=1)
    weight = jnp.sum(jnp.where(mine, weights, 0.0), axis=1)
    earlier = (
        lax.broadcasted_iota(jnp.int32, (n_tok, n_tok), 0)
        < lax.broadcasted_iota(jnp.int32, (n_tok, n_tok), 1)
    ).astype(BF)
    rank = contract(chosen.astype(BF), earlier, 1, 0).astype(jnp.int32)
    first = jnp.tile(jnp.arange(cols, dtype=jnp.int32) * cap, rows)[:, None]
    place = jnp.where(chosen, first + rank, -1).reshape(rows, 1, cols * n_tok)
    line_weight = weight.reshape(rows, 1, cols * n_tok)
    placed = jnp.where(
        place == jnp.arange(block, dtype=jnp.int32)[None, :, None], line_weight, 0.0
    ).astype(BF)
    line_q = cols * n_tok // SEQ_LEN
    grouped = (
        lax.broadcasted_iota(jnp.int32, (cols * n_tok, line_q), 0) // SEQ_LEN
        == lax.broadcasted_iota(jnp.int32, (cols * n_tok, line_q), 1)
    ).astype(BF)
    spread = contract(placed.reshape(-1, cols * n_tok), grouped, 1, 0).astype(BF)
    spread = spread.reshape(rows, block, line_q)

    gate_part = projected[:, :hidden_width]
    up_part = projected[:, hidden_width:]
    sigmoid_gate = jax.nn.sigmoid(gate_part)
    activated = gate_part * sigmoid_gate
    hidden = (activated * up_part).astype(BF)
    cot_down = contract(cot, down, 1, 1).astype(BF).reshape(rows, line_q, hidden_width)
    hidden_grad = lax.dot_general(
        spread, cot_down, (((2,), (1,)), ((0,), (0,))), preferred_element_type=F32
    ).reshape(-1, hidden_width)
    slope = sigmoid_gate * (1.0 + gate_part * (1.0 - sigmoid_gate))
    pre_grad = jnp.concatenate(
        [hidden_grad * up_part * slope, hidden_grad * activated], axis=1
    ).astype(BF)

    per_dev = n_tok // SEQ_LEN
    cot_own = lax.dynamic_slice_in_dim(cot, me * per_dev, per_dev, 0)
    cot_tok = jnp.repeat(cot_own, SEQ_LEN, axis=0)
    token_grad, gate_up_grad = combine(
        rows, cols, pre_grad, dm.T, cot_tok, gate_up, slot_inputs
    )

    hidden_by_query = lax.dot_general(
        spread, hidden.reshape(rows, block, hidden_width), (((1,), (1,)), ((0,), (0,))),
        preferred_element_type=F32,
    ).astype(BF).reshape(-1, hidden_width)
    down_grad = contract(hidden_by_query, cot, 0, 0).astype(BF)
    return (passage_grad, token_grad, gate_up_grad[None], down_grad[None])


def solution(mesh):
    in_specs = (
        P("row", "col"),
        P("col", "row"),
        P("row"),
        P(("row", "col"), None),
        P(("row", "col"), None),
        P(("row", "col"), None),
        P(("row", "col"), None, None),
        P(("row", "col"), None, None),
    )
    out_specs = (
        P("col", "row"),
        P(("row", "col"), None),
        P(("row", "col"), None, None),
        P(("row", "col"), None, None),
    )
    return jax.shard_map(shards, mesh=mesh, in_specs=in_specs, out_specs=out_specs, check_vma=False)
```

```python
import functools
import math

import jax
import jax.numpy as jnp
from jax import lax
from jax.experimental import pallas as pl
from jax.experimental.pallas import tpu as pltpu
from jax.sharding import PartitionSpec as P

SEQ_LEN = 8
LANES = 128
CHUNKS = 4
VMEM_LIMIT = 67_000_000

sharpness_divisor = 0.02

BF = jnp.bfloat16
F32 = jnp.float32
MESH = pl.DeviceIdType.MESH


def contract(a, b, da, db):
    return lax.dot_general(a, b, (((da,), (db,)), ((), ())), preferred_element_type=F32)


def span(index, size):
    return pl.ds(pl.multiple_of(index * size, size), size)


def remote(src, dst, send_sem, recv_sem, to):
    return pltpu.make_async_remote_copy(
        src_ref=src, dst_ref=dst, send_sem=send_sem, recv_sem=recv_sem,
        device_id=to, device_id_type=MESH,
    )


def greet(rows, cols):
    row, col = lax.axis_index("row"), lax.axis_index("col")
    barrier = pltpu.get_barrier_semaphore()
    for s in range(1, rows):
        pl.semaphore_signal(
            barrier, inc=1, device_id=(lax.rem(row + s, rows), col), device_id_type=MESH
        )
    for s in range(1, cols):
        pl.semaphore_signal(
            barrier, inc=1, device_id=(row, lax.rem(col + s, cols)), device_id_type=MESH
        )
    pl.semaphore_wait(barrier, rows + cols - 2)


def dispatch_kernel(
    rows, cols, cap, top,
    tok_ref, doc_ref, qry_ref, meta_ref, wgu_ref,
    x_ref, docs_ref, qrys_ref, metas_ref, proj_ref, dm_ref,
    tokc, packed, w, own_sem, w_sem, zs, zr, gs, gr, rs, ds, dr,
):
    row, col = lax.axis_index("row"), lax.axis_index("col")
    n_tok, width = tok_ref.shape
    n_doc, w_doc = doc_ref.shape
    n_qry, w_qry = qry_ref.shape
    step = width // CHUNKS
    block = cols * cap
    chips = rows // 2
    core = lax.rem(row, 2)
    chip = lax.div(row, 2)
    sibling = row + 1 - 2 * core

    def doc_strip(r):
        return docs_ref.at[:, span(r, w_doc)]

    def qry_strip(r):
        return qrys_ref.at[span(r, n_qry), :]

    def meta_strip(r):
        return metas_ref.at[pl.ds(r * cols, cols)]

    strips = (meta_strip, doc_strip, qry_strip)

    def line_piece(kind, c):
        if kind == 0:
            return meta_ref, metas_ref.at[row * cols + c]
        if kind == 1:
            return doc_ref, docs_ref.at[span(c, n_doc), span(row, w_doc)]
        if kind == 2:
            return qry_ref, qrys_ref.at[span(row, n_qry), span(c, w_qry)]
        f = kind - 3
        part = pl.ds(f * step, step)
        return tok_ref.at[:, part], tokc.at[span(c, n_tok), part]

    def along_line(kind, s, origin, to):
        src, dst = line_piece(kind, origin)
        return remote(src, dst, zs.at[kind, s], zr.at[kind, origin], (row, to))

    own = []
    for kind in range(3 + CHUNKS):
        src, dst = line_piece(kind, col)
        own.append(pltpu.make_async_copy(src, dst, own_sem.at[kind]))
    loads = [
        pltpu.make_async_copy(wgu_ref.at[span(f, step)], w.at[span(f, step)], w_sem.at[f])
        for f in range(CHUNKS)
    ]
    for copy in own:
        copy.start()
    for copy in loads:
        copy.start()
    greet(rows, cols)
    for kind in range(3 + CHUNKS):
        for s in range(1, cols):
            along_line(kind, s, col, lax.rem(col + s, cols)).start()

    def line_arrived(kind):
        own[kind].wait()
        for s in range(1, cols):
            origin = lax.rem(col + s, cols)
            along_line(kind, s, origin, origin).wait_recv()

    def peer(s):
        return 2 * lax.rem(chip + s, chips) + core

    def direct(kind, s, origin, to):
        return remote(strips[kind](origin), strips[kind](origin), gs.at[kind, s],
                      gr.at[kind, origin], (to, col))

    def relay(kind, s, origin):
        return remote(strips[kind](origin), strips[kind](origin), rs.at[kind, s],
                      gr.at[kind, origin], (sibling, col))

    for kind in range(3):
        line_arrived(kind)
        for s in range(1, chips):
            direct(kind, s, row, peer(s)).start()
        direct(kind, 0, row, sibling).start()

    target = (
        lax.broadcasted_iota(jnp.int32, (rows, n_tok), 0) * cols + col
    ).astype(F32)
    before = (
        lax.broadcasted_iota(jnp.int32, (n_tok, n_tok), 0)
        < lax.broadcasted_iota(jnp.int32, (n_tok, n_tok), 1)
    ).astype(BF)
    slot = lax.broadcasted_iota(jnp.int32, (block, n_tok), 0).astype(F32)
    for c in range(cols):
        ids = metas_ref[row * cols + c]
        hit = jnp.zeros((rows, n_tok), F32)
        for k in range(top):
            hit = hit + (ids[k : k + 1, :] == target).astype(F32)
        rank = contract(hit.astype(BF), before, 1, 0)
        place = jnp.where(hit > 0.5, rank + float(c * cap), -1.0)
        for r in range(rows):
            dm_ref[r * block : (r + 1) * block, c * n_tok : (c + 1) * n_tok] = jnp.where(
                slot == place[r : r + 1, :], 1.0, 0.0
            ).astype(BF)

    def outgoing(f, s, origin, to):
        part = pl.ds(f * step, step)
        return remote(packed.at[span(to, block), part], x_ref.at[span(origin, block), part],
                      ds.at[f, s], dr.at[f, origin], (to, col))

    def kept(f):
        part = pl.ds(f * step, step)
        return pltpu.make_async_copy(
            packed.at[span(row, block), part], x_ref.at[span(row, block), part],
            own_sem.at[3 + CHUNKS + f],
        )

    pair = 2 * block
    for f in range(CHUNKS):
        line_arrived(3 + f)
        part = slice(f * step, (f + 1) * step)

        @pl.loop(0, rows // 2)
        def _(m):
            packed[span(m, pair), part] = contract(
                dm_ref[span(m, pair), :], tokc[:, part], 1, 0
            ).astype(BF)

        for s in range(1, rows):
            outgoing(f, s, row, lax.rem(row + s, rows)).start()
        kept(f).start()

    for kind in range(3):
        for s in range(1, chips):
            origin = peer(s)
            direct(kind, s, origin, origin).wait_recv()
            relay(kind, s, origin).start()

    hidden2 = proj_ref.shape[1]
    tile = 512
    for f in range(CHUNKS):
        loads[f].wait()
        kept(f).wait()
        for s in range(1, rows):
            origin = lax.rem(row + s, rows)
            outgoing(f, s, origin, origin).wait_recv()
        part = slice(f * step, (f + 1) * step)

        @pl.loop(0, hidden2 // tile)
        def _(n):
            term = contract(x_ref[:, part], w[part, span(n, tile)], 1, 0)
            if f == 0:
                proj_ref[:, span(n, tile)] = term
            else:
                proj_ref[:, span(n, tile)] += term

    for kind in range(3):
        direct(kind, 0, sibling, sibling).wait_recv()
        for s in range(1, chips):
            origin = 2 * lax.rem(chip + s, chips) + 1 - core
            relay(kind, s, origin).wait_recv()
    for kind in range(3):
        for s in range(1, chips):
            direct(kind, s, row, peer(s)).wait_send()
            relay(kind, s, peer(s)).wait_send()
        direct(kind, 0, row, sibling).wait_send()
    for kind in range(3 + CHUNKS):
        for s in range(1, cols):
            along_line(kind, s, col, lax.rem(col + s, cols)).wait_send()
    for f in range(CHUNKS):
        for s in range(1, rows):
            outgoing(f, s, row, lax.rem(row + s, rows)).wait_send()


def dispatch(rows, cols, cap, top, tokens, documents, questions, meta, gate_up):
    n_tok, width = tokens.shape
    n_doc, w_doc = documents.shape
    n_qry, w_qry = questions.shape
    slots = rows * cols * cap
    hidden2 = gate_up.shape[1]
    dma = pltpu.SemaphoreType.DMA
    vmem = pl.BlockSpec(memory_space=pltpu.VMEM)
    hbm = pl.BlockSpec(memory_space=pl.ANY)
    return pl.pallas_call(
        functools.partial(dispatch_kernel, rows, cols, cap, top),
        out_shape=(
            jax.ShapeDtypeStruct((slots, width), BF),
            jax.ShapeDtypeStruct((cols * n_doc, rows * w_doc), BF),
            jax.ShapeDtypeStruct((rows * n_qry, cols * w_qry), BF),
            jax.ShapeDtypeStruct((rows * cols,) + meta.shape, F32),
            jax.ShapeDtypeStruct((slots, hidden2), F32),
            jax.ShapeDtypeStruct((slots, cols * n_tok), BF),
        ),
        in_specs=[vmem] * 4 + [hbm],
        out_specs=[vmem, hbm, hbm, vmem, vmem, vmem],
        scratch_shapes=[
            pltpu.VMEM((cols * n_tok, width), BF),
            pltpu.VMEM((slots, width), BF),
            pltpu.VMEM((width, hidden2), BF),
            dma((3 + 2 * CHUNKS,)),
            dma((CHUNKS,)),
            dma((3 + CHUNKS, cols)),
            dma((3 + CHUNKS, cols)),
            dma((3, rows)),
            dma((3, rows)),
            dma((3, rows)),
            dma((CHUNKS, rows)),
            dma((CHUNKS, rows)),
        ],
        compiler_params=pltpu.CompilerParams(
            collective_id=0, has_side_effects=True, vmem_limit_bytes=VMEM_LIMIT
        ),
        name="dispatch",
    )(tokens, documents, questions, meta, gate_up)


def combine_kernel(
    rows, cols,
    pre_ref, dmt_ref, cot_ref, wgu_ref, xin_ref,
    tok_ref, gug_ref,
    w, x, back, ret, comb, parts, stage,
    load_sem, own_sem, es, er, fs, fr, out_sem,
):
    row, col = lax.axis_index("row"), lax.axis_index("col")
    slots = pre_ref.shape[0]
    block = slots // rows
    width = wgu_ref.shape[0]
    n_tok = cot_ref.shape[0]
    step = width // CHUNKS

    loads = [
        pltpu.make_async_copy(wgu_ref.at[span(f, step)], w.at[span(f, step)], load_sem.at[f])
        for f in range(CHUNKS)
    ]
    loads.append(pltpu.make_async_copy(xin_ref, x, load_sem.at[CHUNKS]))
    for copy in loads:
        copy.start()
    greet(rows, cols)

    def returning(f, s, origin, to):
        part = pl.ds(f * step, step)
        return remote(back.at[span(to, block), part], ret.at[span(origin, block), part],
                      es.at[f, s], er.at[f, origin], (to, col))

    def kept(f):
        part = pl.ds(f * step, step)
        return pltpu.make_async_copy(
            back.at[span(row, block), part], ret.at[span(row, block), part], own_sem.at[f]
        )

    def home(f, s, origin, to):
        part = pl.ds(f * step, step)
        return remote(comb.at[span(to, n_tok), part], parts.at[origin, :, part],
                      fs.at[f, s], fr.at[f, origin], (row, to))

    tile = 256
    for f in range(CHUNKS):
        loads[f].wait()

        @pl.loop(0, step // tile)
        def _(n):
            back[:, pl.ds(pl.multiple_of(f * step + n * tile, tile), tile)] = contract(
                pre_ref[...], w[pl.ds(pl.multiple_of(f * step + n * tile, tile), tile), :], 1, 1
            ).astype(BF)

        for s in range(1, rows):
            returning(f, s, row, lax.rem(row + s, rows)).start()
        kept(f).start()
    loads[CHUNKS].wait()

    def grad_tile(i):
        here = slice(i * step, (i + 1) * step)
        stage[i % 2] = contract(x[:, here], pre_ref[...], 0, 0).astype(BF)

    def grad_out(i):
        return pltpu.make_async_copy(
            stage.at[i % 2], gug_ref.at[pl.ds(i * step, step)], out_sem.at[i % 2]
        )

    def merge(f):
        kept(f).wait()
        for s in range(1, rows):
            origin = lax.rem(row + s, rows)
            returning(f, s, origin, origin).wait_recv()
        part = slice(f * step, (f + 1) * step)
        comb[:, part] = contract(dmt_ref[...], ret[:, part], 1, 0).astype(BF)
        for s in range(1, cols):
            home(f, s, col, lax.rem(col + s, cols)).start()

    def finish(f):
        part = slice(f * step, (f + 1) * step)
        total = cot_ref[:, part].astype(F32) + comb[span(col, n_tok), part].astype(F32)
        for s in range(1, cols):
            origin = lax.rem(col + s, cols)
            home(f, s, origin, origin).wait_recv()
            total = total + parts[origin, :, part].astype(F32)
        tok_ref[:, part] = total.astype(BF)

    for i in range(CHUNKS):
        if i >= 2:
            grad_out(i - 2).wait()
        grad_tile(i)
        grad_out(i).start()
        merge(i)
        if i >= 1:
            finish(i - 1)
    finish(CHUNKS - 1)
    for i in range(CHUNKS - 2, CHUNKS):
        grad_out(i).wait()
    for f in range(CHUNKS):
        for s in range(1, rows):
            returning(f, s, row, lax.rem(row + s, rows)).wait_send()
        for s in range(1, cols):
            home(f, s, col, lax.rem(col + s, cols)).wait_send()


def combine(rows, cols, pre_grad, dispatch_t, cot_tok, gate_up, slot_inputs):
    slots, hidden2 = pre_grad.shape
    n_tok, width = cot_tok.shape
    step = width // CHUNKS
    dma = pltpu.SemaphoreType.DMA
    vmem = pl.BlockSpec(memory_space=pltpu.VMEM)
    hbm = pl.BlockSpec(memory_space=pl.ANY)
    return pl.pallas_call(
        functools.partial(combine_kernel, rows, cols),
        out_shape=(
            jax.ShapeDtypeStruct((n_tok, width), BF),
            jax.ShapeDtypeStruct((width, hidden2), BF),
        ),
        in_specs=[vmem, vmem, vmem, hbm, hbm],
        out_specs=[vmem, hbm],
        scratch_shapes=[
            pltpu.VMEM((width, hidden2), BF),
            pltpu.VMEM((slots, width), BF),
            pltpu.VMEM((slots, width), BF),
            pltpu.VMEM((slots, width), BF),
            pltpu.VMEM((cols * n_tok, width), BF),
            pltpu.VMEM((cols, n_tok, width), BF),
            pltpu.VMEM((2, step, hidden2), BF),
            dma((CHUNKS + 1,)),
            dma((CHUNKS,)),
            dma((CHUNKS, rows)),
            dma((CHUNKS, rows)),
            dma((CHUNKS, cols)),
            dma((CHUNKS, cols)),
            dma((2,)),
        ],
        compiler_params=pltpu.CompilerParams(
            collective_id=1, has_side_effects=True, vmem_limit_bytes=VMEM_LIMIT
        ),
        name="combine",
    )(pre_grad, dispatch_t, cot_tok, gate_up, slot_inputs)


def fused_kernel(
    rows, cols, cap, first_widths, last_widths,
    tok_ref, doc_ref, qry_ref, pos_ref, ids_ref, rw_ref, wgu_ref, down_ref,
    passage_ref, out_ref, gug_ref, dg_ref,
    meta, metas, tokc, packed, x, w, down, proj, dm, dmt, place, weight, placed, group,
    docs, qrow, qcols, dsc, cot, cot_down, spread, hgrad, hidden, pre, ret, comb, parts,
    hbq, stage,
    own_sem, load_sem, zs, zr, gs, gr, rs, ds, dr, qs, qr, ss, sr, es, er, fs, fr, out_sem,
):
    row, col = lax.axis_index("row"), lax.axis_index("col")
    me = row * cols + col
    n_tok, width = tok_ref.shape
    n_doc, w_doc = doc_ref.shape
    n_qry, w_qry = qry_ref.shape
    top = ids_ref.shape[0]
    ff = down.shape[0]
    slots = x.shape[0]
    block = slots // rows
    pair = 2 * block
    chips = rows // 2
    core = lax.rem(row, 2)
    chip = lax.div(row, 2)
    sibling = row + 1 - 2 * core

    def flip(index, k, count):
        total, bit = 0, 1
        while bit < count:
            digit = lax.rem(lax.div(index, bit), 2)
            total = total + bit * (1 - digit if k & bit else digit)
            bit *= 2
        return total

    mates = list(range(2, rows)) + [1]
    line_q = cols * n_tok // SEQ_LEN

    def cuts(widths):
        edges, at = [], 0
        for size in widths:
            edges.append((at, size))
            at += size
        return edges

    first, last = cuts(first_widths), cuts(last_widths)
    n_first, n_last = len(first), len(last)

    def line_piece(kind, c):
        if kind == 0:
            return doc_ref, docs.at[span(c, n_doc), span(row, w_doc)]
        if kind == 1:
            return meta, metas.at[row * cols + c]
        if kind == 2:
            return qry_ref, qrow.at[:, span(c, w_qry)]
        at, size = first[kind - 3]
        return tok_ref.at[:, pl.ds(at, size)], tokc.at[span(c, n_tok), pl.ds(at, size)]

    ways = ((0, 1), (1, -1))

    def can_send(way):
        return col < cols - 1 if way == 0 else col > 0

    def hop(kind, step, way, block, to):
        src, dst = line_piece(kind, block)
        return remote(src if step == 0 else dst, dst, zs.at[kind, way, step],
                      zr.at[kind, block], (row, to))

    def advance(kinds, step):
        for kind in kinds:
            for way, d in ways:
                origin = col - d * step
                came = origin >= 0 if way == 0 else origin < cols
                if step:
                    @pl.when(came)
                    def _():
                        hop(kind, step, way, origin, col).wait_recv()

                @pl.when(jnp.logical_and(came, can_send(way)))
                def _():
                    hop(kind, step, way, origin, col + d).start()

    def settle(kind):
        for step in range(cols):
            for way, d in ways:
                origin = col - d * step
                came = origin >= 0 if way == 0 else origin < cols

                @pl.when(jnp.logical_and(came, can_send(way)))
                def _():
                    hop(kind, step, way, origin, col + d).wait_send()

    def own(kind):
        src, dst = line_piece(kind, col)
        return pltpu.make_async_copy(src, dst, own_sem.at[kind])

    loads = [
        pltpu.make_async_copy(wgu_ref.at[pl.ds(at, size)], w.at[pl.ds(at, size)], load_sem.at[f])
        for f, (at, size) in enumerate(first)
    ]
    loads.append(pltpu.make_async_copy(down_ref, down, load_sem.at[n_first]))

    meta[:top] = ids_ref[...].astype(F32)
    meta[top:] = rw_ref[...]
    for kind in range(3 + n_first):
        own(kind).start()
    greet(rows, cols)
    queue = [(0, 1), (3,), (4,), (2,)] + [(kind,) for kind in range(5, 3 + n_first)]
    advance(queue[0], 0)
    advance(queue[1], 0)
    for copy in loads:
        copy.start()

    def gathered(i):
        for step in range(1, cols):
            advance(queue[i], step)
        for kind in queue[i]:
            own(kind).wait()
        if i + 2 < len(queue):
            advance(queue[i + 2], 0)

    def strip(kind, r):
        if kind == 0:
            return docs.at[:, span(r, w_doc)]
        return metas.at[pl.ds(r * cols, cols)]

    def peer(s):
        return 2 * flip(chip, s, chips) + core

    def direct(kind, s, origin, to):
        return remote(strip(kind, origin), strip(kind, origin), gs.at[kind, s],
                      gr.at[kind, origin], (to, col))

    def relay(kind, s, origin):
        return remote(strip(kind, origin), strip(kind, origin), rs.at[kind, s],
                      gr.at[kind, origin], (sibling, col))

    def spread_out(kind):
        for s in range(1, chips):
            direct(kind, s, row, peer(s)).start()
        direct(kind, 0, row, sibling).start()

    def pass_on(kind):
        for s in range(1, chips):
            origin = peer(s)
            direct(kind, s, origin, origin).wait_recv()
            relay(kind, s, origin).start()

    def all_here(kind):
        direct(kind, 0, sibling, sibling).wait_recv()
        for s in range(1, chips):
            relay(kind, s, peer(s) + 1 - 2 * core).wait_recv()

    before = (
        lax.broadcasted_iota(jnp.int32, (n_tok, n_tok), 0)
        < lax.broadcasted_iota(jnp.int32, (n_tok, n_tok), 1)
    ).astype(BF)
    slot = lax.broadcasted_iota(jnp.int32, (block, n_tok), 0).astype(F32)

    def outgoing(f, s, origin, to):
        part = pl.ds(*first[f])
        return remote(packed.at[span(to, block), part], x.at[span(origin, block), part],
                      ds.at[f, s], dr.at[f, origin], (to, col))

    def kept(f):
        part = pl.ds(*first[f])
        return pltpu.make_async_copy(
            packed.at[span(row, block), part], x.at[span(row, block), part],
            own_sem.at[3 + n_first + f],
        )

    def send(f, offsets):
        for s in offsets:
            outgoing(f, s, row, flip(row, s, rows)).start()

    def sent(f, offsets):
        for s in offsets:
            outgoing(f, s, row, flip(row, s, rows)).wait_send()

    near = tuple(k for k in mates if k < 6)
    far = tuple(k for k in mates if k >= 6)
    final = n_first - 1

    def pack(f):
        part = pl.ds(*first[f])

        @pl.loop(0, chips)
        def _(m):
            packed[span(m, pair), part] = contract(
                dm[span(m, pair), :], tokc[:, part], 1, 0
            ).astype(BF)

        kept(f).start()

    tile = 512

    def project(f):
        loads[f].wait()
        kept(f).wait()
        for s in range(1, rows):
            origin = flip(row, s, rows)
            outgoing(f, s, origin, origin).wait_recv()
        part = pl.ds(*first[f])

        @pl.loop(0, 2 * ff // tile)
        def _(n):
            term = contract(x[:, part], w[part, span(n, tile)], 1, 0)
            if f == 0:
                proj[:, span(n, tile)] = term
            else:
                proj[:, span(n, tile)] += term

    def query_piece(origin, to):
        return qrow.at[:, span(to, w_doc)], qcols.at[span(origin, n_qry), :]

    def queries(s, origin, to):
        src, dst = query_piece(origin, to)
        return remote(src, dst, qs.at[s], qr.at[origin], (to, col))

    def own_queries():
        src, dst = query_piece(row, row)
        return pltpu.make_async_copy(src, dst, own_sem.at[3 + 2 * n_first])

    def scored(s, origin, to):
        rows_of = dsc.at[span(origin, n_qry), :]
        return remote(rows_of, rows_of, ss.at[s], sr.at[origin], (to, col))

    gathered(0)
    spread_out(0)
    spread_out(1)
    target = (
        lax.broadcasted_iota(jnp.int32, (rows, n_tok), 0) * cols + col
    ).astype(F32)
    for c in range(cols):
        ids = metas[row * cols + c, :top]
        hit = jnp.zeros((rows, n_tok), F32)
        for k in range(top):
            hit = hit + (ids[k : k + 1, :] == target).astype(F32)
        rank = contract(hit.astype(BF), before, 1, 0)
        spot = jnp.where(hit > 0.5, rank + float(c * cap), -1.0)
        for r in range(rows):
            dm[r * block : (r + 1) * block, c * n_tok : (c + 1) * n_tok] = jnp.where(
                slot == spot[r : r + 1, :], 1.0, 0.0
            ).astype(BF)
    gathered(1)
    pack(0)
    send(0, mates)
    gathered(2)
    pack(1)
    for kind in range(2):
        for s in range(1, chips):
            direct(kind, s, row, peer(s)).wait_send()
    send(1, mates)
    pass_on(0)
    pass_on(1)
    gathered(3)
    for s in mates:
        queries(s, row, flip(row, s, rows)).start()
    own_queries().start()
    all_here(0)
    scores = contract(qrow[...], docs[...], 1, 1) / sharpness_divisor
    peak = jnp.max(scores, axis=1, keepdims=True)
    grown = jnp.exp(scores - peak)
    total = jnp.sum(grown, axis=1, keepdims=True)
    square = (n_qry, n_qry)
    diagonal = lax.broadcasted_iota(jnp.int32, square, 0) == lax.broadcasted_iota(jnp.int32, square, 1)
    wanted = jnp.sum(
        jnp.where(diagonal, pos_ref[...].astype(F32), 0.0), axis=1, keepdims=True
    )
    onehot = (
        wanted == lax.broadcasted_iota(jnp.int32, scores.shape, 1).astype(F32)
    ).astype(F32)
    dsc[span(row, n_qry), :] = ((grown / total - onehot) / sharpness_divisor).astype(BF)
    for c in range(cols):
        here = slice(c * n_tok, (c + 1) * n_tok)
        dmt[here, :] = dm[:, here].astype(F32).T.astype(BF)
    gathered(4)
    pack(2)
    for s in mates:
        scored(s, row, flip(row, s, rows)).start()
    sent(0, mates)
    send(2, mates)

    all_here(1)
    lines = rows * cols
    each = lax.broadcasted_iota(jnp.int32, (lines, n_tok), 0)
    mine = me.astype(F32)
    chosen = jnp.zeros((lines, n_tok), F32)
    amount = jnp.zeros((lines, n_tok), F32)
    for b in range(lines):
        hit = (metas[b, :top] == mine).astype(F32)
        found = jnp.sum(hit, axis=0, keepdims=True)
        value = jnp.sum(hit * metas[b, top:], axis=0, keepdims=True)
        chosen = jnp.where(each == b, found, chosen)
        amount = jnp.where(each == b, value, amount)
    rank = contract(chosen.astype(BF), before, 1, 0)
    begin = (lax.rem(each, cols) * cap).astype(F32)
    place[...] = jnp.where(chosen > 0.5, rank + begin, -1.0)
    weight[...] = amount
    group[...] = (
        lax.broadcasted_iota(jnp.int32, (cols * n_tok, line_q), 0) // SEQ_LEN
        == lax.broadcasted_iota(jnp.int32, (cols * n_tok, line_q), 1)
    ).astype(BF)

    @pl.loop(0, rows)
    def _(r):
        for c in range(cols):
            here = pl.ds(r * cols + c, 1)
            placed[:, c * n_tok : (c + 1) * n_tok] = jnp.where(
                slot == place[here, :], weight[here, :], 0.0
            ).astype(BF)
        spread[span(r, block), :] = contract(placed[...], group[...], 1, 0).astype(BF)

    gathered(5)
    pack(3)
    project(0)
    sent(1, mates)
    send(3, near)
    project(1)
    for s in mates:
        origin = flip(row, s, rows)
        scored(s, origin, origin).wait_recv()

    @pl.loop(0, width // tile)
    def _(n):
        cot[:, span(n, tile)] = (
            contract(dsc[...], docs[:, span(n, tile)], 1, 0) / SEQ_LEN
        ).astype(BF)

    loads[n_first].wait()
    small = 256

    @pl.loop(0, ff // small)
    def _(n):
        cot_down[:, span(n, small)] = contract(
            cot[...], down[span(n, small), :], 1, 1
        ).astype(BF)

    for s in mates:
        origin = flip(row, s, rows)
        queries(s, origin, origin).wait_recv()
    own_queries().wait()
    passage_ref[...] = contract(dsc[:, span(col, n_doc)], qcols[...], 0, 0)
    sent(2, mates)
    send(3, far)
    project(2)

    def returning(f, s, origin, to):
        part = pl.ds(*last[f])
        return remote(packed.at[span(to, block), part], ret.at[span(origin, block), part],
                      es.at[f, s], er.at[f, origin], (to, col))

    def held(f):
        part = pl.ds(*last[f])
        return pltpu.make_async_copy(
            packed.at[span(row, block), part], ret.at[span(row, block), part],
            own_sem.at[4 + 2 * n_first + f],
        )

    def home(f, s, origin, to):
        part = pl.ds(*last[f])
        return remote(comb.at[span(to, n_tok), part], parts.at[origin, :, part],
                      fs.at[f, s], fr.at[f, origin], (row, to))

    f_end = n_first - 1
    loads[f_end].wait()
    kept(f_end).wait()
    end = pl.ds(*first[f_end])
    begin_cols = pl.ds(*last[0])
    lane = 128

    for s in range(chips):
        other = flip(chip, s, chips)
        for k in (2 * s, 2 * s + 1):
            if k:
                origin = flip(row, k, rows)
                outgoing(f_end, k, origin, origin).wait_recv()
        here = span(other, pair)

        @pl.loop(0, 2 * ff // tile)
        def _(n):
            proj[here, span(n, tile)] += contract(x[here, end], w[end, span(n, tile)], 1, 0)

        for k in range(2):
            r = 2 * other + k
            at = span(r, block)
            hgrad[...] = contract(spread[at, :], cot_down[span(r, line_q), :], 1, 0)

            @pl.loop(0, ff // lane)
            def _(n):
                left = span(n, lane)
                right = pl.ds(pl.multiple_of(ff + n * lane, lane), lane)
                gate, up = proj[at, left], proj[at, right]
                sig = jax.nn.sigmoid(gate)
                act = gate * sig
                grad = hgrad[:, left]
                hidden[at, left] = (act * up).astype(BF)
                pre[at, left] = (grad * up * (sig * (1.0 + gate * (1.0 - sig)))).astype(BF)
                pre[at, right] = (grad * act).astype(BF)

        packed[here, begin_cols] = contract(pre[here, :], w[begin_cols, :], 1, 1).astype(BF)
        for k in (2 * s, 2 * s + 1):
            if k:
                returning(0, k, row, flip(row, k, rows)).start()
            else:
                held(0).start()

    flushed = False
    for f in range(1, n_last):
        at, size = last[f]
        if at + size > first[final][0] and not flushed:
            flushed = True
            sent(final, near + far)
        bit = math.gcd(size, small)

        @pl.loop(0, size // bit)
        def _(n):
            part = pl.ds(pl.multiple_of(at + n * bit, bit), bit)
            packed[:, part] = contract(pre[...], w[part, :], 1, 1).astype(BF)

        for s in mates:
            returning(f, s, row, flip(row, s, rows)).start()
        held(f).start()

    @pl.loop(0, rows)
    def _(r):
        hbq[span(r, line_q), :] = contract(
            spread[span(r, block), :], hidden[span(r, block), :], 0, 0
        ).astype(BF)

    n_gate, n_down = width // small, ff // small

    def gate_out(i):
        return pltpu.make_async_copy(
            stage.at[i % 2, :, pl.ds(0, 2 * ff)], gug_ref.at[pl.ds(i * small, small)],
            out_sem.at[i % 2],
        )

    def down_out(i):
        j = n_gate + i
        return pltpu.make_async_copy(
            stage.at[j % 2], dg_ref.at[pl.ds(i * small, small)], out_sem.at[j % 2]
        )

    def grad_out(i):
        return gate_out(i) if i < n_gate else down_out(i - n_gate)

    def grad_tile(i):
        if i >= 2:
            grad_out(i - 2).wait()
        if i < n_gate:
            stage[i % 2, :, : 2 * ff] = contract(
                x[:, i * small : (i + 1) * small], pre[...], 0, 0
            ).astype(BF)
        else:
            j = i - n_gate
            stage[i % 2] = contract(hbq[:, j * small : (j + 1) * small], cot[...], 0, 0).astype(BF)
        grad_out(i).start()

    def merge(f):
        held(f).wait()
        for s in range(1, rows):
            origin = flip(row, s, rows)
            returning(f, s, origin, origin).wait_recv()
        part = pl.ds(*last[f])
        comb[:, part] = contract(dmt[...], ret[:, part], 1, 0).astype(BF)
        for s in range(1, cols):
            home(f, s, col, lax.rem(col + s, cols)).start()

    per_dev = n_tok // SEQ_LEN
    repeat = (
        lax.broadcasted_iota(jnp.int32, (n_tok, per_dev), 0) // SEQ_LEN
        == lax.broadcasted_iota(jnp.int32, (n_tok, per_dev), 1)
    ).astype(BF)

    def finish(f):
        part = pl.ds(*last[f])
        sums = contract(repeat, cot[span(me, per_dev), part], 1, 0)
        sums = sums + comb[span(col, n_tok), part].astype(F32)
        for s in range(1, cols):
            origin = lax.rem(col + s, cols)
            home(f, s, origin, origin).wait_recv()
            sums = sums + parts[origin, :, part].astype(F32)
        out_ref[:, part] = sums.astype(BF)

    tiles = n_gate + n_down
    done = 0
    for f in range(n_last):
        merge(f)
        if f >= 1:
            finish(f - 1)
        if f == 0:
            for kind in range(2):
                for s in range(1, chips):
                    relay(kind, s, peer(s)).wait_send()
                direct(kind, 0, row, sibling).wait_send()
            for kind in range(3 + n_first):
                settle(kind)
            for s in mates:
                to = flip(row, s, rows)
                queries(s, row, to).wait_send()
                scored(s, row, to).wait_send()
        until = min(tiles, -(-tiles * (f + 1) // 3))
        for i in range(done, until):
            grad_tile(i)
        done = until
    finish(n_last - 1)
    for i in range(tiles - 2, tiles):
        grad_out(i).wait()

    for f in range(n_last):
        for s in mates:
            returning(f, s, row, flip(row, s, rows)).wait_send()
    for f in range(n_last):
        for s in range(1, cols):
            home(f, s, col, lax.rem(col + s, cols)).wait_send()


def fused_plan(rows, cols, cap, top, tokens, documents, questions, down):
    n_tok, width = tokens.shape
    n_doc, w_doc = documents.shape
    n_qry = questions.shape[0]
    ff = down.shape[0]
    block = cols * cap
    slots = rows * block
    line = cols * n_tok
    line_q = line // SEQ_LEN
    n_all = rows * n_qry
    stage_rows = 256
    return [
        ((2 * top, n_tok), F32),
        ((rows * cols, 2 * top, n_tok), F32),
        ((line, width), BF),
        ((slots, width), BF),
        ((slots, width), BF),
        ((width, 2 * ff), BF),
        ((ff, width), BF),
        ((slots, 2 * ff), F32),
        ((slots, line), BF),
        ((line, slots), BF),
        ((rows * cols, n_tok), F32),
        ((rows * cols, n_tok), F32),
        ((block, line), BF),
        ((line, line_q), BF),
        ((cols * n_doc, width), BF),
        ((n_qry, width), BF),
        ((n_all, w_doc), BF),
        ((n_all, cols * n_doc), BF),
        ((n_all, width), BF),
        ((n_all, ff), BF),
        ((slots, line_q), BF),
        ((block, ff), F32),
        ((slots, ff), BF),
        ((slots, 2 * ff), BF),
        ((slots, width), BF),
        ((line, width), BF),
        ((cols, n_tok, width), BF),
        ((n_all, ff), BF),
        ((2, stage_rows, max(width, 2 * ff)), BF),
    ]


def plan_bytes(plan):
    return sum(math.prod(shape) * jnp.dtype(kind).itemsize for shape, kind in plan)


def fused(rows, cols, cap, plan, tokens, documents, questions, positive, ids, weights, gate_up, down):
    n_tok, width = tokens.shape
    n_doc, w_doc = documents.shape
    hidden2 = gate_up.shape[1]
    first = [width // 4] * 4
    last = [width // 4] * 3 + [width // 8] * 2
    dma = pltpu.SemaphoreType.DMA
    vmem = pl.BlockSpec(memory_space=pltpu.VMEM)
    hbm = pl.BlockSpec(memory_space=pl.ANY)
    n_first, n_last = len(first), len(last)
    return pl.pallas_call(
        functools.partial(fused_kernel, rows, cols, cap, first, last),
        out_shape=(
            jax.ShapeDtypeStruct((n_doc, w_doc), F32),
            jax.ShapeDtypeStruct((n_tok, width), BF),
            jax.ShapeDtypeStruct((width, hidden2), BF),
            jax.ShapeDtypeStruct(down.shape, BF),
        ),
        in_specs=[vmem] * 6 + [hbm] * 2,
        out_specs=[vmem, vmem, hbm, hbm],
        scratch_shapes=[pltpu.VMEM(shape, kind) for shape, kind in plan]
        + [
            dma((4 + 2 * n_first + n_last,)),
            dma((n_first + 1,)),
            dma((3 + n_first, 2, cols)),
            dma((3 + n_first, cols)),
            dma((2, rows)),
            dma((2, rows)),
            dma((2, rows)),
            dma((n_first, rows)),
            dma((n_first, rows)),
            dma((rows,)),
            dma((rows,)),
            dma((rows,)),
            dma((rows,)),
            dma((n_last, rows)),
            dma((n_last, rows)),
            dma((n_last, cols)),
            dma((n_last, cols)),
            dma((2,)),
        ],
        compiler_params=pltpu.CompilerParams(
            collective_id=2, has_side_effects=True, vmem_limit_bytes=VMEM_LIMIT
        ),
        name="fused",
    )(tokens, documents, questions, positive.reshape(1, -1), ids.T, weights.T, gate_up, down)


def settle_kernel(pieces, *refs):
    count = len(pieces)
    sources, targets = refs[:count], refs[count : 2 * count]
    buffers, in_sem, out_sem = refs[2 * count : 3 * count], refs[-2], refs[-1]
    todo = []
    for i, parts in enumerate(pieces):
        size = sources[i].shape[0] // parts
        for p in range(parts):
            todo.append((i, pl.ds(p * size, size)))
    ins = [
        pltpu.make_async_copy(sources[i].at[at], buffers[i].at[at], in_sem.at[n])
        for n, (i, at) in enumerate(todo)
    ]
    outs = [
        pltpu.make_async_copy(buffers[i].at[at], targets[i].at[at], out_sem.at[n])
        for n, (i, at) in enumerate(todo)
    ]
    for copy in ins:
        copy.start()
    for arrived, leave in zip(ins, outs):
        arrived.wait()
        leave.start()
    for copy in outs:
        copy.wait()


def settled(*arrays):
    halves = [a.size * a.dtype.itemsize // (1 << 19) for a in arrays]
    pieces = [1 << max(0, n.bit_length() - 1) for n in halves]
    dma = pltpu.SemaphoreType.DMA
    hbm = pl.BlockSpec(memory_space=pl.ANY)
    return pl.pallas_call(
        functools.partial(settle_kernel, pieces),
        out_shape=tuple(jax.ShapeDtypeStruct(a.shape, a.dtype) for a in arrays),
        in_specs=[hbm] * len(arrays),
        out_specs=[hbm] * len(arrays),
        scratch_shapes=[pltpu.VMEM(a.shape, a.dtype) for a in arrays]
        + [dma((sum(pieces),)), dma((sum(pieces),))],
        compiler_params=pltpu.CompilerParams(vmem_limit_bytes=VMEM_LIMIT),
        name="settle",
    )(*arrays)


def shards(
    question_vectors,
    document_vectors,
    positive,
    tokens,
    expert_ids,
    route_weights,
    expert_gate_up,
    expert_down,
):
    rows = lax.axis_size("row")
    cols = lax.axis_size("col")
    row = lax.axis_index("row")
    col = lax.axis_index("col")
    devices_all = rows * cols
    me = row * cols + col
    n_tok, width = tokens.shape
    top = expert_ids.shape[1]
    experts_all = devices_all * expert_gate_up.shape[0]
    cap = max(2, (n_tok * top * 9 + 8 * experts_all - 1) // (8 * experts_all))
    block = cols * cap
    hidden_width = expert_down.shape[1]
    gate_up = expert_gate_up[0]
    down = expert_down[0]

    plan = fused_plan(rows, cols, cap, top, tokens, document_vectors, question_vectors, down)
    if rows == 8 and plan_bytes(plan) < VMEM_LIMIT - 6_000_000:
        passage_grad, token_grad, gate_up_grad, down_grad = fused(
            rows, cols, cap, plan, tokens, document_vectors, question_vectors, positive,
            expert_ids, route_weights, gate_up, down,
        )
        passage_grad, token_grad, gate_up_grad, down_grad = settled(
            passage_grad, token_grad, gate_up_grad, down_grad
        )
        return (passage_grad, token_grad, gate_up_grad[None], down_grad[None])

    n_qry = positive.shape[0]
    pos_rows = -(-n_qry // (8 * LANES)) * 8
    pos = jnp.pad(positive, (0, pos_rows * LANES - n_qry)).astype(F32).reshape(pos_rows, LANES)
    meta = jnp.concatenate([expert_ids.T.astype(F32), route_weights.T, pos], axis=0)
    slot_inputs, docs, qrys, metas, projected, dm = dispatch(
        rows, cols, cap, top, tokens, document_vectors, question_vectors, meta, gate_up
    )

    ids = metas[:, :top].astype(jnp.int32)
    weights = metas[:, top : 2 * top]
    positive_all = metas.reshape(rows, cols, -1, LANES)[:, 0, 2 * top :].reshape(rows, -1)
    positive_all = positive_all[:, :n_qry].reshape(-1).astype(jnp.int32)

    scores = contract(qrys, docs, 1, 1) / sharpness_divisor
    peak = jnp.max(scores, axis=1, keepdims=True)
    grown = jnp.exp(scores - peak)
    total = jnp.sum(grown, axis=1, keepdims=True)
    onehot = (
        positive_all[:, None] == jnp.arange(docs.shape[0], dtype=jnp.int32)[None, :]
    ).astype(F32)
    dscore = ((grown / total - onehot) / sharpness_divisor).astype(BF)
    cot = (contract(dscore, docs, 1, 0) / SEQ_LEN).astype(BF)
    n_doc, w_doc = document_vectors.shape
    passage_grad = contract(
        lax.dynamic_slice_in_dim(dscore, col * n_doc, n_doc, 1),
        lax.dynamic_slice_in_dim(qrys, row * w_doc, w_doc, 1),
        0, 0,
    )

    mine = ids == me
    chosen = jnp.any(mine, axis=1)
    weight = jnp.sum(jnp.where(mine, weights, 0.0), axis=1)
    earlier = (
        lax.broadcasted_iota(jnp.int32, (n_tok, n_tok), 0)
        < lax.broadcasted_iota(jnp.int32, (n_tok, n_tok), 1)
    ).astype(BF)
    rank = contract(chosen.astype(BF), earlier, 1, 0).astype(jnp.int32)
    first = jnp.tile(jnp.arange(cols, dtype=jnp.int32) * cap, rows)[:, None]
    place = jnp.where(chosen, first + rank, -1).reshape(rows, 1, cols * n_tok)
    line_weight = weight.reshape(rows, 1, cols * n_tok)
    placed = jnp.where(
        place == jnp.arange(block, dtype=jnp.int32)[None, :, None], line_weight, 0.0
    ).astype(BF)
    line_q = cols * n_tok // SEQ_LEN
    grouped = (
        lax.broadcasted_iota(jnp.int32, (cols * n_tok, line_q), 0) // SEQ_LEN
        == lax.broadcasted_iota(jnp.int32, (cols * n_tok, line_q), 1)
    ).astype(BF)
    spread = contract(placed.reshape(-1, cols * n_tok), grouped, 1, 0).astype(BF)
    spread = spread.reshape(rows, block, line_q)

    gate_part = projected[:, :hidden_width]
    up_part = projected[:, hidden_width:]
    sigmoid_gate = jax.nn.sigmoid(gate_part)
    activated = gate_part * sigmoid_gate
    hidden = (activated * up_part).astype(BF)
    cot_down = contract(cot, down, 1, 1).astype(BF).reshape(rows, line_q, hidden_width)
    hidden_grad = lax.dot_general(
        spread, cot_down, (((2,), (1,)), ((0,), (0,))), preferred_element_type=F32
    ).reshape(-1, hidden_width)
    slope = sigmoid_gate * (1.0 + gate_part * (1.0 - sigmoid_gate))
    pre_grad = jnp.concatenate(
        [hidden_grad * up_part * slope, hidden_grad * activated], axis=1
    ).astype(BF)

    per_dev = n_tok // SEQ_LEN
    cot_own = lax.dynamic_slice_in_dim(cot, me * per_dev, per_dev, 0)
    cot_tok = jnp.repeat(cot_own, SEQ_LEN, axis=0)
    token_grad, gate_up_grad = combine(
        rows, cols, pre_grad, dm.T, cot_tok, gate_up, slot_inputs
    )

    hidden_by_query = lax.dot_general(
        spread, hidden.reshape(rows, block, hidden_width), (((1,), (1,)), ((0,), (0,))),
        preferred_element_type=F32,
    ).astype(BF).reshape(-1, hidden_width)
    down_grad = contract(hidden_by_query, cot, 0, 0).astype(BF)
    return (passage_grad, token_grad, gate_up_grad[None], down_grad[None])


def solution(mesh):
    in_specs = (
        P("row", "col"),
        P("col", "row"),
        P("row"),
        P(("row", "col"), None),
        P(("row", "col"), None),
        P(("row", "col"), None),
        P(("row", "col"), None, None),
        P(("row", "col"), None, None),
    )
    out_specs = (
        P("col", "row"),
        P(("row", "col"), None),
        P(("row", "col"), None, None),
        P(("row", "col"), None, None),
    )
    return jax.shard_map(shards, mesh=mesh, in_specs=in_specs, out_specs=out_specs, check_vma=False)
```

```python
import functools
import math

import jax
import jax.numpy as jnp
from jax import lax
from jax.experimental import pallas as pl
from jax.experimental.pallas import tpu as pltpu
from jax.sharding import PartitionSpec as P

SEQ_LEN = 8
LANES = 128
CHUNKS = 4
VMEM_LIMIT = 67_000_000

sharpness_divisor = 0.02

BF = jnp.bfloat16
F32 = jnp.float32
MESH = pl.DeviceIdType.MESH


def contract(a, b, da, db):
    return lax.dot_general(a, b, (((da,), (db,)), ((), ())), preferred_element_type=F32)


def span(index, size):
    return pl.ds(pl.multiple_of(index * size, size), size)


def remote(src, dst, send_sem, recv_sem, to):
    return pltpu.make_async_remote_copy(
        src_ref=src, dst_ref=dst, send_sem=send_sem, recv_sem=recv_sem,
        device_id=to, device_id_type=MESH,
    )


def greet(rows, cols):
    row, col = lax.axis_index("row"), lax.axis_index("col")
    barrier = pltpu.get_barrier_semaphore()
    for s in range(1, rows):
        pl.semaphore_signal(
            barrier, inc=1, device_id=(lax.rem(row + s, rows), col), device_id_type=MESH
        )
    for s in range(1, cols):
        pl.semaphore_signal(
            barrier, inc=1, device_id=(row, lax.rem(col + s, cols)), device_id_type=MESH
        )
    pl.semaphore_wait(barrier, rows + cols - 2)


def dispatch_kernel(
    rows, cols, cap, top,
    tok_ref, doc_ref, qry_ref, meta_ref, wgu_ref,
    x_ref, docs_ref, qrys_ref, metas_ref, proj_ref, dm_ref,
    tokc, packed, w, own_sem, w_sem, zs, zr, gs, gr, rs, ds, dr,
):
    row, col = lax.axis_index("row"), lax.axis_index("col")
    n_tok, width = tok_ref.shape
    n_doc, w_doc = doc_ref.shape
    n_qry, w_qry = qry_ref.shape
    step = width // CHUNKS
    block = cols * cap
    chips = rows // 2
    core = lax.rem(row, 2)
    chip = lax.div(row, 2)
    sibling = row + 1 - 2 * core

    def doc_strip(r):
        return docs_ref.at[:, span(r, w_doc)]

    def qry_strip(r):
        return qrys_ref.at[span(r, n_qry), :]

    def meta_strip(r):
        return metas_ref.at[pl.ds(r * cols, cols)]

    strips = (meta_strip, doc_strip, qry_strip)

    def line_piece(kind, c):
        if kind == 0:
            return meta_ref, metas_ref.at[row * cols + c]
        if kind == 1:
            return doc_ref, docs_ref.at[span(c, n_doc), span(row, w_doc)]
        if kind == 2:
            return qry_ref, qrys_ref.at[span(row, n_qry), span(c, w_qry)]
        f = kind - 3
        part = pl.ds(f * step, step)
        return tok_ref.at[:, part], tokc.at[span(c, n_tok), part]

    def along_line(kind, s, origin, to):
        src, dst = line_piece(kind, origin)
        return remote(src, dst, zs.at[kind, s], zr.at[kind, origin], (row, to))

    own = []
    for kind in range(3 + CHUNKS):
        src, dst = line_piece(kind, col)
        own.append(pltpu.make_async_copy(src, dst, own_sem.at[kind]))
    loads = [
        pltpu.make_async_copy(wgu_ref.at[span(f, step)], w.at[span(f, step)], w_sem.at[f])
        for f in range(CHUNKS)
    ]
    for copy in own:
        copy.start()
    for copy in loads:
        copy.start()
    greet(rows, cols)
    for kind in range(3 + CHUNKS):
        for s in range(1, cols):
            along_line(kind, s, col, lax.rem(col + s, cols)).start()

    def line_arrived(kind):
        own[kind].wait()
        for s in range(1, cols):
            origin = lax.rem(col + s, cols)
            along_line(kind, s, origin, origin).wait_recv()

    def peer(s):
        return 2 * lax.rem(chip + s, chips) + core

    def direct(kind, s, origin, to):
        return remote(strips[kind](origin), strips[kind](origin), gs.at[kind, s],
                      gr.at[kind, origin], (to, col))

    def relay(kind, s, origin):
        return remote(strips[kind](origin), strips[kind](origin), rs.at[kind, s],
                      gr.at[kind, origin], (sibling, col))

    for kind in range(3):
        line_arrived(kind)
        for s in range(1, chips):
            direct(kind, s, row, peer(s)).start()
        direct(kind, 0, row, sibling).start()

    target = (
        lax.broadcasted_iota(jnp.int32, (rows, n_tok), 0) * cols + col
    ).astype(F32)
    before = (
        lax.broadcasted_iota(jnp.int32, (n_tok, n_tok), 0)
        < lax.broadcasted_iota(jnp.int32, (n_tok, n_tok), 1)
    ).astype(BF)
    slot = lax.broadcasted_iota(jnp.int32, (block, n_tok), 0).astype(F32)
    for c in range(cols):
        ids = metas_ref[row * cols + c]
        hit = jnp.zeros((rows, n_tok), F32)
        for k in range(top):
            hit = hit + (ids[k : k + 1, :] == target).astype(F32)
        rank = contract(hit.astype(BF), before, 1, 0)
        place = jnp.where(hit > 0.5, rank + float(c * cap), -1.0)
        for r in range(rows):
            dm_ref[r * block : (r + 1) * block, c * n_tok : (c + 1) * n_tok] = jnp.where(
                slot == place[r : r + 1, :], 1.0, 0.0
            ).astype(BF)

    def outgoing(f, s, origin, to):
        part = pl.ds(f * step, step)
        return remote(packed.at[span(to, block), part], x_ref.at[span(origin, block), part],
                      ds.at[f, s], dr.at[f, origin], (to, col))

    def kept(f):
        part = pl.ds(f * step, step)
        return pltpu.make_async_copy(
            packed.at[span(row, block), part], x_ref.at[span(row, block), part],
            own_sem.at[3 + CHUNKS + f],
        )

    pair = 2 * block
    for f in range(CHUNKS):
        line_arrived(3 + f)
        part = slice(f * step, (f + 1) * step)

        @pl.loop(0, rows // 2)
        def _(m):
            packed[span(m, pair), part] = contract(
                dm_ref[span(m, pair), :], tokc[:, part], 1, 0
            ).astype(BF)

        for s in range(1, rows):
            outgoing(f, s, row, lax.rem(row + s, rows)).start()
        kept(f).start()

    for kind in range(3):
        for s in range(1, chips):
            origin = peer(s)
            direct(kind, s, origin, origin).wait_recv()
            relay(kind, s, origin).start()

    hidden2 = proj_ref.shape[1]
    tile = 512
    for f in range(CHUNKS):
        loads[f].wait()
        kept(f).wait()
        for s in range(1, rows):
            origin = lax.rem(row + s, rows)
            outgoing(f, s, origin, origin).wait_recv()
        part = slice(f * step, (f + 1) * step)

        @pl.loop(0, hidden2 // tile)
        def _(n):
            term = contract(x_ref[:, part], w[part, span(n, tile)], 1, 0)
            if f == 0:
                proj_ref[:, span(n, tile)] = term
            else:
                proj_ref[:, span(n, tile)] += term

    for kind in range(3):
        direct(kind, 0, sibling, sibling).wait_recv()
        for s in range(1, chips):
            origin = 2 * lax.rem(chip + s, chips) + 1 - core
            relay(kind, s, origin).wait_recv()
    for kind in range(3):
        for s in range(1, chips):
            direct(kind, s, row, peer(s)).wait_send()
            relay(kind, s, peer(s)).wait_send()
        direct(kind, 0, row, sibling).wait_send()
    for kind in range(3 + CHUNKS):
        for s in range(1, cols):
            along_line(kind, s, col, lax.rem(col + s, cols)).wait_send()
    for f in range(CHUNKS):
        for s in range(1, rows):
            outgoing(f, s, row, lax.rem(row + s, rows)).wait_send()


def dispatch(rows, cols, cap, top, tokens, documents, questions, meta, gate_up):
    n_tok, width = tokens.shape
    n_doc, w_doc = documents.shape
    n_qry, w_qry = questions.shape
    slots = rows * cols * cap
    hidden2 = gate_up.shape[1]
    dma = pltpu.SemaphoreType.DMA
    vmem = pl.BlockSpec(memory_space=pltpu.VMEM)
    hbm = pl.BlockSpec(memory_space=pl.ANY)
    return pl.pallas_call(
        functools.partial(dispatch_kernel, rows, cols, cap, top),
        out_shape=(
            jax.ShapeDtypeStruct((slots, width), BF),
            jax.ShapeDtypeStruct((cols * n_doc, rows * w_doc), BF),
            jax.ShapeDtypeStruct((rows * n_qry, cols * w_qry), BF),
            jax.ShapeDtypeStruct((rows * cols,) + meta.shape, F32),
            jax.ShapeDtypeStruct((slots, hidden2), F32),
            jax.ShapeDtypeStruct((slots, cols * n_tok), BF),
        ),
        in_specs=[vmem] * 4 + [hbm],
        out_specs=[vmem, hbm, hbm, vmem, vmem, vmem],
        scratch_shapes=[
            pltpu.VMEM((cols * n_tok, width), BF),
            pltpu.VMEM((slots, width), BF),
            pltpu.VMEM((width, hidden2), BF),
            dma((3 + 2 * CHUNKS,)),
            dma((CHUNKS,)),
            dma((3 + CHUNKS, cols)),
            dma((3 + CHUNKS, cols)),
            dma((3, rows)),
            dma((3, rows)),
            dma((3, rows)),
            dma((CHUNKS, rows)),
            dma((CHUNKS, rows)),
        ],
        compiler_params=pltpu.CompilerParams(
            collective_id=0, has_side_effects=True, vmem_limit_bytes=VMEM_LIMIT
        ),
        name="dispatch",
    )(tokens, documents, questions, meta, gate_up)


def combine_kernel(
    rows, cols,
    pre_ref, dmt_ref, cot_ref, wgu_ref, xin_ref,
    tok_ref, gug_ref,
    w, x, back, ret, comb, parts, stage,
    load_sem, own_sem, es, er, fs, fr, out_sem,
):
    row, col = lax.axis_index("row"), lax.axis_index("col")
    slots = pre_ref.shape[0]
    block = slots // rows
    width = wgu_ref.shape[0]
    n_tok = cot_ref.shape[0]
    step = width // CHUNKS

    loads = [
        pltpu.make_async_copy(wgu_ref.at[span(f, step)], w.at[span(f, step)], load_sem.at[f])
        for f in range(CHUNKS)
    ]
    loads.append(pltpu.make_async_copy(xin_ref, x, load_sem.at[CHUNKS]))
    for copy in loads:
        copy.start()
    greet(rows, cols)

    def returning(f, s, origin, to):
        part = pl.ds(f * step, step)
        return remote(back.at[span(to, block), part], ret.at[span(origin, block), part],
                      es.at[f, s], er.at[f, origin], (to, col))

    def kept(f):
        part = pl.ds(f * step, step)
        return pltpu.make_async_copy(
            back.at[span(row, block), part], ret.at[span(row, block), part], own_sem.at[f]
        )

    def home(f, s, origin, to):
        part = pl.ds(f * step, step)
        return remote(comb.at[span(to, n_tok), part], parts.at[origin, :, part],
                      fs.at[f, s], fr.at[f, origin], (row, to))

    tile = 256
    for f in range(CHUNKS):
        loads[f].wait()

        @pl.loop(0, step // tile)
        def _(n):
            back[:, pl.ds(pl.multiple_of(f * step + n * tile, tile), tile)] = contract(
                pre_ref[...], w[pl.ds(pl.multiple_of(f * step + n * tile, tile), tile), :], 1, 1
            ).astype(BF)

        for s in range(1, rows):
            returning(f, s, row, lax.rem(row + s, rows)).start()
        kept(f).start()
    loads[CHUNKS].wait()

    def grad_tile(i):
        here = slice(i * step, (i + 1) * step)
        stage[i % 2] = contract(x[:, here], pre_ref[...], 0, 0).astype(BF)

    def grad_out(i):
        return pltpu.make_async_copy(
            stage.at[i % 2], gug_ref.at[pl.ds(i * step, step)], out_sem.at[i % 2]
        )

    def merge(f):
        kept(f).wait()
        for s in range(1, rows):
            origin = lax.rem(row + s, rows)
            returning(f, s, origin, origin).wait_recv()
        part = slice(f * step, (f + 1) * step)
        comb[:, part] = contract(dmt_ref[...], ret[:, part], 1, 0).astype(BF)
        for s in range(1, cols):
            home(f, s, col, lax.rem(col + s, cols)).start()

    def finish(f):
        part = slice(f * step, (f + 1) * step)
        total = cot_ref[:, part].astype(F32) + comb[span(col, n_tok), part].astype(F32)
        for s in range(1, cols):
            origin = lax.rem(col + s, cols)
            home(f, s, origin, origin).wait_recv()
            total = total + parts[origin, :, part].astype(F32)
        tok_ref[:, part] = total.astype(BF)

    for i in range(CHUNKS):
        if i >= 2:
            grad_out(i - 2).wait()
        grad_tile(i)
        grad_out(i).start()
        merge(i)
        if i >= 1:
            finish(i - 1)
    finish(CHUNKS - 1)
    for i in range(CHUNKS - 2, CHUNKS):
        grad_out(i).wait()
    for f in range(CHUNKS):
        for s in range(1, rows):
            returning(f, s, row, lax.rem(row + s, rows)).wait_send()
        for s in range(1, cols):
            home(f, s, col, lax.rem(col + s, cols)).wait_send()


def combine(rows, cols, pre_grad, dispatch_t, cot_tok, gate_up, slot_inputs):
    slots, hidden2 = pre_grad.shape
    n_tok, width = cot_tok.shape
    step = width // CHUNKS
    dma = pltpu.SemaphoreType.DMA
    vmem = pl.BlockSpec(memory_space=pltpu.VMEM)
    hbm = pl.BlockSpec(memory_space=pl.ANY)
    return pl.pallas_call(
        functools.partial(combine_kernel, rows, cols),
        out_shape=(
            jax.ShapeDtypeStruct((n_tok, width), BF),
            jax.ShapeDtypeStruct((width, hidden2), BF),
        ),
        in_specs=[vmem, vmem, vmem, hbm, hbm],
        out_specs=[vmem, hbm],
        scratch_shapes=[
            pltpu.VMEM((width, hidden2), BF),
            pltpu.VMEM((slots, width), BF),
            pltpu.VMEM((slots, width), BF),
            pltpu.VMEM((slots, width), BF),
            pltpu.VMEM((cols * n_tok, width), BF),
            pltpu.VMEM((cols, n_tok, width), BF),
            pltpu.VMEM((2, step, hidden2), BF),
            dma((CHUNKS + 1,)),
            dma((CHUNKS,)),
            dma((CHUNKS, rows)),
            dma((CHUNKS, rows)),
            dma((CHUNKS, cols)),
            dma((CHUNKS, cols)),
            dma((2,)),
        ],
        compiler_params=pltpu.CompilerParams(
            collective_id=1, has_side_effects=True, vmem_limit_bytes=VMEM_LIMIT
        ),
        name="combine",
    )(pre_grad, dispatch_t, cot_tok, gate_up, slot_inputs)


def fused_kernel(
    rows, cols, cap, first_widths, plane_width, last_widths,
    tok_ref, doc_ref, qry_ref, pos_ref, ids_ref, rw_ref, wgu_ref, down_ref,
    passage_ref, out_ref, gug_ref, dg_ref,
    meta, metas, tokc, packed, x, w, down, proj, dm, dmt, place, weight, placed, group,
    docs, qrow, qcols, dsc, cot, cot_down, spread, hgrad, hidden, pre, ret, comb, parts,
    hbq, stage, plane, drops, sums_out,
    own_sem, load_sem, zs, zr, gs, gr, rs, ds, dr, qs, qr, ps, pr, es, er, fs, fr, out_sem,
    leave_sem,
):
    row, col = lax.axis_index("row"), lax.axis_index("col")
    me = row * cols + col
    n_tok, width = tok_ref.shape
    n_doc, w_doc = doc_ref.shape
    n_qry, w_qry = qry_ref.shape
    top = ids_ref.shape[0]
    ff = down.shape[0]
    slots = x.shape[0]
    block = slots // rows
    pair = 2 * block
    chips = rows // 2
    core = lax.rem(row, 2)
    chip = lax.div(row, 2)
    sibling = row + 1 - 2 * core

    def flip(index, k, count):
        total, bit = 0, 1
        while bit < count:
            digit = lax.rem(lax.div(index, bit), 2)
            total = total + bit * (1 - digit if k & bit else digit)
            bit *= 2
        return total

    mates = list(range(2, rows)) + [1]
    line_q = cols * n_tok // SEQ_LEN

    def cuts(widths):
        edges, at = [], 0
        for size in widths:
            edges.append((at, size))
            at += size
        return edges

    first, last = cuts(first_widths), cuts(last_widths)
    n_first, n_last = len(first), len(last)

    def line_piece(kind, c):
        if kind == 0:
            return doc_ref, docs.at[span(c, n_doc), span(row, w_doc)]
        if kind == 1:
            return meta, metas.at[row * cols + c]
        if kind == 2:
            return qry_ref, qrow.at[:, span(c, w_qry)]
        at, size = first[kind - 3]
        return tok_ref.at[:, pl.ds(at, size)], tokc.at[span(c, n_tok), pl.ds(at, size)]

    ways = ((0, 1), (1, -1))

    def can_send(way):
        return col < cols - 1 if way == 0 else col > 0

    def hop(kind, step, way, block, to):
        src, dst = line_piece(kind, block)
        return remote(src if step == 0 else dst, dst, zs.at[kind, way],
                      zr.at[kind, block], (row, to))

    def advance(kinds, step):
        for kind in kinds:
            for way, d in ways:
                origin = col - d * step
                came = origin >= 0 if way == 0 else origin < cols
                if step:
                    @pl.when(came)
                    def _():
                        hop(kind, step, way, origin, col).wait_recv()

                    @pl.when(jnp.logical_and(came, can_send(way)))
                    def _():
                        hop(kind, step - 1, way, col, col + d).wait_send()

                @pl.when(jnp.logical_and(came, can_send(way)))
                def _():
                    hop(kind, step, way, origin, col + d).start()

    def settle(kind):
        for way, d in ways:
            @pl.when(can_send(way))
            def _():
                hop(kind, 0, way, col, col + d).wait_send()

    def own(kind):
        src, dst = line_piece(kind, col)
        return pltpu.make_async_copy(src, dst, own_sem.at[kind])

    plane_cut = (sum(first_widths), plane_width)
    plane_cols = pl.ds(*plane_cut)
    loads = [
        pltpu.make_async_copy(wgu_ref.at[pl.ds(at, size)], w.at[pl.ds(at, size)], load_sem.at[f])
        for f, (at, size) in enumerate(first + [plane_cut])
    ]
    loads.append(pltpu.make_async_copy(down_ref, down, load_sem.at[n_first + 1]))

    meta[:top] = ids_ref[...].astype(F32)
    meta[top:] = rw_ref[...]
    for kind in range(3 + n_first):
        own(kind).start()
    greet(rows, cols)
    queue = [(0, 1), (3,), (4,), (2,)] + [(kind,) for kind in range(5, 3 + n_first)]
    advance(queue[0], 0)
    advance(queue[1], 0)

    def gathered(i):
        for step in range(1, cols):
            advance(queue[i], step)
        for kind in queue[i]:
            own(kind).wait()
        if i + 2 < len(queue):
            advance(queue[i + 2], 0)

    def strip(kind, r):
        if kind == 0:
            return docs.at[:, span(r, w_doc)]
        if kind == 1:
            return metas.at[pl.ds(r * cols, cols)]
        if kind == 2:
            return plane.at[span(r, n_tok), :]
        return dsc.at[span(r, n_qry), :]

    def peer(s):
        return 2 * flip(chip, s, chips) + core

    def direct(kind, s, origin, to):
        src = tok_ref.at[:, plane_cols] if kind == 2 else strip(kind, origin)
        return remote(src, strip(kind, origin), gs.at[kind], gr.at[kind, 0 if s else 1], (to, col))

    def relay(kind, origin):
        return remote(strip(kind, origin), strip(kind, origin), rs.at[kind], gr.at[kind, 1],
                      (sibling, col))

    def several(kind, count, send_sem, recv_sem):
        if kind == 0:
            part = docs.at[:, pl.ds(0, count * w_doc)]
        elif kind == 1:
            part = metas.at[pl.ds(0, count * cols)]
        elif kind == 2:
            part = plane.at[pl.ds(0, count * n_tok), :]
        else:
            part = dsc.at[pl.ds(0, count * n_qry), :]
        return remote(part, part, send_sem, recv_sem, (sibling, col))

    def spread_out(kind):
        for s in range(1, chips):
            direct(kind, s, row, peer(s)).start()
        direct(kind, 0, row, sibling).start()

    def pass_on(kind):
        several(kind, chips - 1, rs.at[kind], gr.at[kind, 0]).wait_recv()
        for s in range(1, chips):
            relay(kind, peer(s)).start()

    def all_here(kind):
        several(kind, chips, rs.at[kind], gr.at[kind, 1]).wait_recv()

    def all_out(kind):
        several(kind, chips, gs.at[kind], gr.at[kind, 0]).wait_send()

    def passed(kind):
        several(kind, chips - 1, rs.at[kind], gr.at[kind, 1]).wait_send()

    own_plane = pltpu.make_async_copy(
        tok_ref.at[:, plane_cols], strip(2, row), own_sem.at[4 + 2 * n_first + n_last]
    )
    spread_out(2)
    own_plane.start()
    for copy in loads:
        copy.start()

    before = (
        lax.broadcasted_iota(jnp.int32, (n_tok, n_tok), 0)
        < lax.broadcasted_iota(jnp.int32, (n_tok, n_tok), 1)
    ).astype(BF)
    slot = lax.broadcasted_iota(jnp.int32, (block, n_tok), 0).astype(F32)

    near = tuple(k for k in mates if k < 6)
    far = tuple(k for k in mates if k >= 6)
    final = n_first - 1

    def outgoing(f, k, origin, to):
        part = pl.ds(*first[f])
        late = f == final
        return remote(
            packed.at[span(to, block), part], x.at[span(origin, block), part],
            ds.at[f + 1 if late and k in far else f], dr.at[f + k // 2 if late else f], (to, col),
        )

    def batch(f, count, send_sem, recv_sem):
        part = pl.ds(*first[f])
        here = pl.ds(0, count * block)
        return remote(packed.at[here, part], x.at[here, part], send_sem, recv_sem, (row, col))

    def sent(f, late=False):
        if f < final:
            batch(f, rows - 1, ds.at[f], dr.at[f]).wait_send()
        elif late:
            batch(f, len(far), ds.at[f + 1], dr.at[f]).wait_send()
        else:
            batch(f, len(near), ds.at[f], dr.at[f]).wait_send()

    def kept(f):
        part = pl.ds(*first[f])
        return pltpu.make_async_copy(
            packed.at[span(row, block), part], x.at[span(row, block), part],
            own_sem.at[3 + n_first + f],
        )

    def send(f, offsets):
        for s in offsets:
            outgoing(f, s, row, flip(row, s, rows)).start()

    def pack(f):
        part = pl.ds(*first[f])

        @pl.loop(0, chips)
        def _(m):
            packed[span(m, pair), part] = contract(
                dm[span(m, pair), :], tokc[:, part], 1, 0
            ).astype(BF)

        kept(f).start()

    tile = 512

    def project(f):
        loads[f].wait()
        kept(f).wait()
        batch(f, rows - 1, ds.at[f], dr.at[f]).wait_recv()
        part = pl.ds(*first[f])

        @pl.loop(0, 2 * ff // tile)
        def _(n):
            term = contract(x[:, part], w[part, span(n, tile)], 1, 0)
            if f == 0:
                proj[:, span(n, tile)] = term
            else:
                proj[:, span(n, tile)] += term

    def query_piece(origin, to):
        return qrow.at[:, span(to, w_doc)], qcols.at[span(origin, n_qry), :]

    def queries(s, origin, to):
        src, dst = query_piece(origin, to)
        return remote(src, dst, qs.at[0], qr.at[0], (to, col))

    def all_queries():
        part = qcols.at[pl.ds(0, (rows - 1) * n_qry), :]
        return remote(part, part, qs.at[0], qr.at[0], (sibling, col))

    def own_queries():
        src, dst = query_piece(row, row)
        return pltpu.make_async_copy(src, dst, own_sem.at[3 + 2 * n_first])

    share = rows * cap

    def dropped(s, origin, to):
        return remote(packed.at[span(to, share), plane_cols], drops.at[span(origin, share), :],
                      ps.at[0], pr.at[0], (row, to))

    def all_dropped():
        part = drops.at[pl.ds(0, (cols - 1) * share), :]
        return remote(part, part, ps.at[0], pr.at[0], (row, col))

    def own_drop():
        return pltpu.make_async_copy(
            packed.at[span(col, share), plane_cols], drops.at[span(col, share), :],
            own_sem.at[5 + 2 * n_first + n_last],
        )

    def pack_plane():
        wanted_by = (
            lax.broadcasted_iota(jnp.int32, (cols, n_tok), 0) + row * cols
        ).astype(F32)
        spots = lax.broadcasted_iota(jnp.int32, (share, n_tok), 0).astype(F32)
        for r in range(rows):
            ids = metas[r * cols + col, :top]
            hit = jnp.zeros((cols, n_tok), F32)
            for k in range(top):
                hit = hit + (ids[k : k + 1, :] == wanted_by).astype(F32)
            rank = contract(hit.astype(BF), before, 1, 0)
            spot = jnp.where(hit > 0.5, rank + float(r * cap), -1.0)
            for c in range(cols):
                pre[c * share : (c + 1) * share, r * n_tok : (r + 1) * n_tok] = jnp.where(
                    spots == spot[c : c + 1, :], 1.0, 0.0
                ).astype(BF)

        @pl.loop(0, cols)
        def _(c):
            packed[span(c, share), plane_cols] = contract(
                pre[span(c, share), : rows * n_tok], plane[...], 1, 0
            ).astype(BF)

        for s in range(1, cols):
            dropped(s, col, lax.rem(col + s, cols)).start()
        own_drop().start()

    def order_rows():
        at = lax.broadcasted_iota(jnp.int32, (slots, LANES), 0).astype(F32)
        lane_at = lax.broadcasted_iota(jnp.int32, (slots, LANES), 1).astype(F32)
        line_of = jnp.floor((at + 0.5) * (1.0 / block))
        rest = at - line_of * block
        plane_of = jnp.floor((rest + 0.5) * (1.0 / cap))
        source = plane_of * share + line_of * cap + (rest - plane_of * cap)
        for n in range(slots // LANES):
            pre[:, n * LANES : (n + 1) * LANES] = jnp.where(
                lane_at + float(n * LANES) == source, 1.0, 0.0
            ).astype(BF)

    def project_plane():
        loads[n_first].wait()
        own_drop().wait()
        all_dropped().wait_recv()
        x[:, plane_cols] = contract(pre[:, :slots], drops[...], 1, 0).astype(BF)

        @pl.loop(0, 2 * ff // tile)
        def _(n):
            proj[:, span(n, tile)] += contract(
                x[:, plane_cols], w[plane_cols, span(n, tile)], 1, 0
            )

    gathered(0)
    spread_out(0)
    spread_out(1)
    target = (
        lax.broadcasted_iota(jnp.int32, (rows, n_tok), 0) * cols + col
    ).astype(F32)
    for c in range(cols):
        ids = metas[row * cols + c, :top]
        hit = jnp.zeros((rows, n_tok), F32)
        for k in range(top):
            hit = hit + (ids[k : k + 1, :] == target).astype(F32)
        rank = contract(hit.astype(BF), before, 1, 0)
        spot = jnp.where(hit > 0.5, rank + float(c * cap), -1.0)
        for r in range(rows):
            dm[r * block : (r + 1) * block, c * n_tok : (c + 1) * n_tok] = jnp.where(
                slot == spot[r : r + 1, :], 1.0, 0.0
            ).astype(BF)
    gathered(1)
    pack(0)
    send(0, mates)
    pass_on(2)
    gathered(2)
    pack(1)
    pass_on(1)
    pass_on(0)
    gathered(3)
    for s in mates:
        queries(s, row, flip(row, s, rows)).start()
    own_queries().start()
    all_here(0)
    scores = contract(qrow[...], docs[...], 1, 1) / sharpness_divisor
    peak = jnp.max(scores, axis=1, keepdims=True)
    grown = jnp.exp(scores - peak)
    total = jnp.sum(grown, axis=1, keepdims=True)
    square = (n_qry, n_qry)
    diagonal = lax.broadcasted_iota(jnp.int32, square, 0) == lax.broadcasted_iota(jnp.int32, square, 1)
    wanted = jnp.sum(
        jnp.where(diagonal, pos_ref[...].astype(F32), 0.0), axis=1, keepdims=True
    )
    onehot = (
        wanted == lax.broadcasted_iota(jnp.int32, scores.shape, 1).astype(F32)
    ).astype(F32)
    dsc[span(row, n_qry), :] = ((grown / total - onehot) / sharpness_divisor).astype(BF)
    for c in range(cols):
        here = slice(c * n_tok, (c + 1) * n_tok)
        dmt[here, :] = dm[:, here].astype(F32).T.astype(BF)
    spread_out(3)
    send(1, mates)
    gathered(4)
    pack(2)
    all_here(1)
    all_here(2)
    own_plane.wait()
    pack_plane()
    sent(0)
    send(2, near)
    order_rows()

    lines = rows * cols
    each = lax.broadcasted_iota(jnp.int32, (lines, n_tok), 0)
    mine = me.astype(F32)
    chosen = jnp.zeros((lines, n_tok), F32)
    amount = jnp.zeros((lines, n_tok), F32)
    for b in range(lines):
        hit = (metas[b, :top] == mine).astype(F32)
        found = jnp.sum(hit, axis=0, keepdims=True)
        value = jnp.sum(hit * metas[b, top:], axis=0, keepdims=True)
        chosen = jnp.where(each == b, found, chosen)
        amount = jnp.where(each == b, value, amount)
    rank = contract(chosen.astype(BF), before, 1, 0)
    begin = (lax.rem(each, cols) * cap).astype(F32)
    place[...] = jnp.where(chosen > 0.5, rank + begin, -1.0)
    weight[...] = amount
    group[...] = (
        lax.broadcasted_iota(jnp.int32, (cols * n_tok, line_q), 0) // SEQ_LEN
        == lax.broadcasted_iota(jnp.int32, (cols * n_tok, line_q), 1)
    ).astype(BF)

    @pl.loop(0, rows)
    def _(r):
        for c in range(cols):
            here = pl.ds(r * cols + c, 1)
            placed[:, c * n_tok : (c + 1) * n_tok] = jnp.where(
                slot == place[here, :], weight[here, :], 0.0
            ).astype(BF)
        spread[span(r, block), :] = contract(placed[...], group[...], 1, 0).astype(BF)

    project(0)
    pass_on(3)
    all_here(3)

    @pl.loop(0, width // tile)
    def _(n):
        cot[:, span(n, tile)] = (
            contract(dsc[...], docs[:, span(n, tile)], 1, 0) / SEQ_LEN
        ).astype(BF)

    loads[n_first + 1].wait()
    small = 256

    @pl.loop(0, ff // small)
    def _(n):
        cot_down[:, span(n, small)] = contract(
            cot[...], down[span(n, small), :], 1, 1
        ).astype(BF)

    all_queries().wait_recv()
    own_queries().wait()
    passage_ref[...] = contract(dsc[:, span(col, n_doc)], qcols[...], 0, 0)
    sent(1)
    send(2, far)
    project(1)
    project_plane()

    def returning(f, s, origin, to):
        part = pl.ds(*last[f])
        return remote(packed.at[span(to, block), part], ret.at[span(origin, block), part],
                      es.at[f], er.at[f], (to, col))

    def all_returned(f):
        part = pl.ds(*last[f])
        here = pl.ds(0, (rows - 1) * block)
        return remote(packed.at[here, part], ret.at[here, part], es.at[f], er.at[f], (row, col))

    def held(f):
        part = pl.ds(*last[f])
        return pltpu.make_async_copy(
            packed.at[span(row, block), part], ret.at[span(row, block), part],
            own_sem.at[4 + 2 * n_first + f],
        )

    def home(f, s, origin, to):
        part = pl.ds(*last[f])
        return remote(comb.at[span(to, n_tok), part], parts.at[origin, :, part],
                      fs.at[f], fr.at[f], (row, to))

    def all_home(f):
        part = pl.ds(*last[f])
        here = pl.ds(0, cols - 1)
        return remote(parts.at[here, :, part], parts.at[here, :, part], fs.at[f], fr.at[f], (row, col))

    f_end = n_first - 1
    loads[f_end].wait()
    kept(f_end).wait()
    end = pl.ds(*first[f_end])
    lead = 2
    begin_cols = pl.ds(0, last[0][1] + last[1][1])
    lane = 128

    for s in [k for k in (1, 2, 0, 3) if k < chips]:
        other = flip(chip, s, chips)
        count = 2 if s else 1
        batch(f_end, count, ds.at[f_end], dr.at[f_end + s]).wait_recv()
        here = span(other, pair)

        @pl.loop(0, 2 * ff // tile)
        def _(n):
            proj[here, span(n, tile)] += contract(x[here, end], w[end, span(n, tile)], 1, 0)

        for k in range(2):
            r = 2 * other + k
            at = span(r, block)
            hgrad[...] = contract(spread[at, :], cot_down[span(r, line_q), :], 1, 0)

            @pl.loop(0, ff // lane)
            def _(n):
                left = span(n, lane)
                right = pl.ds(pl.multiple_of(ff + n * lane, lane), lane)
                gate, up = proj[at, left], proj[at, right]
                sig = jax.nn.sigmoid(gate)
                act = gate * sig
                grad = hgrad[:, left]
                hidden[at, left] = (act * up).astype(BF)
                pre[at, left] = (grad * up * (sig * (1.0 + gate * (1.0 - sig)))).astype(BF)
                pre[at, right] = (grad * act).astype(BF)

        packed[here, begin_cols] = contract(pre[here, :], w[begin_cols, :], 1, 1).astype(BF)
        for f in range(lead):
            for k in (2 * s, 2 * s + 1):
                if k:
                    returning(f, k, row, flip(row, k, rows)).start()
                else:
                    held(f).start()

    def give_back(f):
        at, size = last[f]
        bit = math.gcd(size, small)

        @pl.loop(0, size // bit)
        def _(n):
            part = pl.ds(pl.multiple_of(at + n * bit, bit), bit)
            packed[:, part] = contract(pre[...], w[part, :], 1, 1).astype(BF)

        for s in mates:
            returning(f, s, row, flip(row, s, rows)).start()
        held(f).start()

    ahead = lead + 3
    sent(final)
    sent(final, late=True)
    all_dropped().wait_send()
    for f in range(lead, ahead):
        give_back(f)

    n_gate, n_down = width // small, ff // small

    def gate_out(i):
        return pltpu.make_async_copy(
            stage.at[i % 2, :, pl.ds(0, 2 * ff)], gug_ref.at[pl.ds(i * small, small)],
            out_sem.at[i % 2],
        )

    def down_out(i):
        j = n_gate + i
        return pltpu.make_async_copy(
            stage.at[j % 2], dg_ref.at[pl.ds(i * small, small)], out_sem.at[j % 2]
        )

    def grad_out(i):
        return gate_out(i) if i < n_gate else down_out(i - n_gate)

    def grad_tile(i):
        if i >= 2:
            grad_out(i - 2).wait()
        if i < n_gate:
            stage[i % 2, :, : 2 * ff] = contract(
                x[:, i * small : (i + 1) * small], pre[...], 0, 0
            ).astype(BF)
        else:
            j = i - n_gate
            stage[i % 2] = contract(hbq[:, j * small : (j + 1) * small], cot[...], 0, 0).astype(BF)
        grad_out(i).start()

    def merge(f):
        held(f).wait()
        all_returned(f).wait_recv()
        part = pl.ds(*last[f])
        comb[:, part] = contract(dmt[...], ret[:, part], 1, 0).astype(BF)
        for s in range(1, cols):
            home(f, s, col, lax.rem(col + s, cols)).start()

    per_dev = n_tok // SEQ_LEN
    repeat = (
        lax.broadcasted_iota(jnp.int32, (n_tok, per_dev), 0) // SEQ_LEN
        == lax.broadcasted_iota(jnp.int32, (n_tok, per_dev), 1)
    ).astype(BF)

    def leaving(f):
        part = pl.ds(*last[f])
        return pltpu.make_async_copy(sums_out.at[:, part], out_ref.at[:, part], leave_sem.at[f])

    def finish(f):
        part = pl.ds(*last[f])
        sums = contract(repeat, cot[span(me, per_dev), part], 1, 0)
        sums = sums + comb[span(col, n_tok), part].astype(F32)
        all_home(f).wait_recv()
        for s in range(1, cols):
            origin = lax.rem(col + s, cols)
            sums = sums + parts[origin, :, part].astype(F32)
        sums_out[:, part] = sums.astype(BF)
        leaving(f).start()

    tiles = n_gate + n_down
    done = 0
    for f in range(n_last):
        merge(f)
        if f + ahead < n_last:
            give_back(f + ahead)
        if f >= 1:
            finish(f - 1)
        if f == 0:
            @pl.loop(0, rows)
            def _(r):
                hbq[span(r, line_q), :] = contract(
                    spread[span(r, block), :], hidden[span(r, block), :], 0, 0
                ).astype(BF)

            for kind in range(4):
                all_out(kind)
                passed(kind)
            for kind in range(3 + n_first):
                settle(kind)
            all_queries().wait_send()
        until = min(tiles, 2 * f)
        for i in range(done, until):
            grad_tile(i)
        done = until
    for i in range(tiles - 2, tiles):
        grad_out(i).wait()
    finish(n_last - 1)

    for f in range(n_last):
        all_returned(f).wait_send()
        all_home(f).wait_send()
        leaving(f).wait()


def fused_plan(rows, cols, cap, top, plane_width, tokens, documents, questions, down):
    n_tok, width = tokens.shape
    n_doc, w_doc = documents.shape
    n_qry = questions.shape[0]
    ff = down.shape[0]
    block = cols * cap
    slots = rows * block
    line = cols * n_tok
    line_q = line // SEQ_LEN
    n_all = rows * n_qry
    stage_rows = 256
    return [
        ((2 * top, n_tok), F32),
        ((rows * cols, 2 * top, n_tok), F32),
        ((line, width - plane_width), BF),
        ((slots, width), BF),
        ((slots, width), BF),
        ((width, 2 * ff), BF),
        ((ff, width), BF),
        ((slots, 2 * ff), F32),
        ((slots, line), BF),
        ((line, slots), BF),
        ((rows * cols, n_tok), F32),
        ((rows * cols, n_tok), F32),
        ((block, line), BF),
        ((line, line_q), BF),
        ((cols * n_doc, width), BF),
        ((n_qry, width), BF),
        ((n_all, w_doc), BF),
        ((n_all, cols * n_doc), BF),
        ((n_all, width), BF),
        ((n_all, ff), BF),
        ((slots, line_q), BF),
        ((block, ff), F32),
        ((slots, ff), BF),
        ((slots, 2 * ff), BF),
        ((slots, width), BF),
        ((line, width), BF),
        ((cols, n_tok, width), BF),
        ((n_all, ff), BF),
        ((2, stage_rows, max(width, 2 * ff)), BF),
        ((rows * n_tok, plane_width), BF),
        ((slots, plane_width), BF),
        ((n_tok, width), BF),
    ]


def plan_bytes(plan):
    return sum(math.prod(shape) * jnp.dtype(kind).itemsize for shape, kind in plan)


def fused(rows, cols, cap, plan, tokens, documents, questions, positive, ids, weights, gate_up, down):
    n_tok, width = tokens.shape
    n_doc, w_doc = documents.shape
    hidden2 = gate_up.shape[1]
    first = [width // 4] * 3
    plane_width = width - sum(first)
    last = [width // 8] * 7 + [width // 16] * 2
    dma = pltpu.SemaphoreType.DMA
    vmem = pl.BlockSpec(memory_space=pltpu.VMEM)
    hbm = pl.BlockSpec(memory_space=pl.ANY)
    n_first, n_last = len(first), len(last)
    return pl.pallas_call(
        functools.partial(fused_kernel, rows, cols, cap, first, plane_width, last),
        out_shape=(
            jax.ShapeDtypeStruct((n_doc, w_doc), F32),
            jax.ShapeDtypeStruct((n_tok, width), BF),
            jax.ShapeDtypeStruct((width, hidden2), BF),
            jax.ShapeDtypeStruct(down.shape, BF),
        ),
        in_specs=[vmem] * 6 + [hbm] * 2,
        out_specs=[vmem, hbm, hbm, hbm],
        scratch_shapes=[pltpu.VMEM(shape, kind) for shape, kind in plan]
        + [
            dma((6 + 2 * n_first + n_last,)),
            dma((n_first + 2,)),
            dma((3 + n_first, 2)),
            dma((3 + n_first, cols)),
            dma((4,)),
            dma((4, 2)),
            dma((4,)),
            dma((n_first + 1,)),
            dma((n_first + rows // 2,)),
            dma((1,)),
            dma((1,)),
            dma((1,)),
            dma((1,)),
            dma((n_last,)),
            dma((n_last,)),
            dma((n_last,)),
            dma((n_last,)),
            dma((2,)),
            dma((n_last,)),
        ],
        compiler_params=pltpu.CompilerParams(
            collective_id=2, has_side_effects=True, vmem_limit_bytes=VMEM_LIMIT
        ),
        name="fused",
    )(tokens, documents, questions, positive.reshape(1, -1), ids.T, weights.T, gate_up, down)


def settle_kernel(pieces, *refs):
    count = len(pieces)
    sources, targets = refs[:count], refs[count : 2 * count]
    buffers, in_sem, out_sem = refs[2 * count : 3 * count], refs[-2], refs[-1]
    todo = []
    for i, parts in enumerate(pieces):
        size = sources[i].shape[0] // parts
        for p in range(parts):
            todo.append((i, pl.ds(p * size, size)))
    ins = [
        pltpu.make_async_copy(sources[i].at[at], buffers[i].at[at], in_sem.at[n])
        for n, (i, at) in enumerate(todo)
    ]
    outs = [
        pltpu.make_async_copy(buffers[i].at[at], targets[i].at[at], out_sem.at[n])
        for n, (i, at) in enumerate(todo)
    ]
    for copy in ins:
        copy.start()
    for arrived, leave in zip(ins, outs):
        arrived.wait()
        leave.start()
    for copy in outs:
        copy.wait()


def settled(*arrays):
    halves = [a.size * a.dtype.itemsize // (1 << 18) for a in arrays]
    pieces = [1 << max(0, n.bit_length() - 1) for n in halves]
    dma = pltpu.SemaphoreType.DMA
    hbm = pl.BlockSpec(memory_space=pl.ANY)
    return pl.pallas_call(
        functools.partial(settle_kernel, pieces),
        out_shape=tuple(jax.ShapeDtypeStruct(a.shape, a.dtype) for a in arrays),
        in_specs=[hbm] * len(arrays),
        out_specs=[hbm] * len(arrays),
        scratch_shapes=[pltpu.VMEM(a.shape, a.dtype) for a in arrays]
        + [dma((sum(pieces),)), dma((sum(pieces),))],
        compiler_params=pltpu.CompilerParams(vmem_limit_bytes=VMEM_LIMIT),
        name="settle",
    )(*arrays)


def shards(
    question_vectors,
    document_vectors,
    positive,
    tokens,
    expert_ids,
    route_weights,
    expert_gate_up,
    expert_down,
):
    rows = lax.axis_size("row")
    cols = lax.axis_size("col")
    row = lax.axis_index("row")
    col = lax.axis_index("col")
    devices_all = rows * cols
    me = row * cols + col
    n_tok, width = tokens.shape
    top = expert_ids.shape[1]
    experts_all = devices_all * expert_gate_up.shape[0]
    cap = max(2, (n_tok * top * 9 + 8 * experts_all - 1) // (8 * experts_all))
    block = cols * cap
    hidden_width = expert_down.shape[1]
    gate_up = expert_gate_up[0]
    down = expert_down[0]

    plan = fused_plan(rows, cols, cap, top, width // 4, tokens, document_vectors, question_vectors, down)
    if rows == 8 and plan_bytes(plan) < VMEM_LIMIT - 6_000_000:
        passage_grad, token_grad, gate_up_grad, down_grad = fused(
            rows, cols, cap, plan, tokens, document_vectors, question_vectors, positive,
            expert_ids, route_weights, gate_up, down,
        )
        passage_grad, token_grad, gate_up_grad, down_grad = settled(
            passage_grad, token_grad, gate_up_grad, down_grad
        )
        return (passage_grad, token_grad, gate_up_grad[None], down_grad[None])

    n_qry = positive.shape[0]
    pos_rows = -(-n_qry // (8 * LANES)) * 8
    pos = jnp.pad(positive, (0, pos_rows * LANES - n_qry)).astype(F32).reshape(pos_rows, LANES)
    meta = jnp.concatenate([expert_ids.T.astype(F32), route_weights.T, pos], axis=0)
    slot_inputs, docs, qrys, metas, projected, dm = dispatch(
        rows, cols, cap, top, tokens, document_vectors, question_vectors, meta, gate_up
    )

    ids = metas[:, :top].astype(jnp.int32)
    weights = metas[:, top : 2 * top]
    positive_all = metas.reshape(rows, cols, -1, LANES)[:, 0, 2 * top :].reshape(rows, -1)
    positive_all = positive_all[:, :n_qry].reshape(-1).astype(jnp.int32)

    scores = contract(qrys, docs, 1, 1) / sharpness_divisor
    peak = jnp.max(scores, axis=1, keepdims=True)
    grown = jnp.exp(scores - peak)
    total = jnp.sum(grown, axis=1, keepdims=True)
    onehot = (
        positive_all[:, None] == jnp.arange(docs.shape[0], dtype=jnp.int32)[None, :]
    ).astype(F32)
    dscore = ((grown / total - onehot) / sharpness_divisor).astype(BF)
    cot = (contract(dscore, docs, 1, 0) / SEQ_LEN).astype(BF)
    n_doc, w_doc = document_vectors.shape
    passage_grad = contract(
        lax.dynamic_slice_in_dim(dscore, col * n_doc, n_doc, 1),
        lax.dynamic_slice_in_dim(qrys, row * w_doc, w_doc, 1),
        0, 0,
    )

    mine = ids == me
    chosen = jnp.any(mine, axis=1)
    weight = jnp.sum(jnp.where(mine, weights, 0.0), axis=1)
    earlier = (
        lax.broadcasted_iota(jnp.int32, (n_tok, n_tok), 0)
        < lax.broadcasted_iota(jnp.int32, (n_tok, n_tok), 1)
    ).astype(BF)
    rank = contract(chosen.astype(BF), earlier, 1, 0).astype(jnp.int32)
    first = jnp.tile(jnp.arange(cols, dtype=jnp.int32) * cap, rows)[:, None]
    place = jnp.where(chosen, first + rank, -1).reshape(rows, 1, cols * n_tok)
    line_weight = weight.reshape(rows, 1, cols * n_tok)
    placed = jnp.where(
        place == jnp.arange(block, dtype=jnp.int32)[None, :, None], line_weight, 0.0
    ).astype(BF)
    line_q = cols * n_tok // SEQ_LEN
    grouped = (
        lax.broadcasted_iota(jnp.int32, (cols * n_tok, line_q), 0) // SEQ_LEN
        == lax.broadcasted_iota(jnp.int32, (cols * n_tok, line_q), 1)
    ).astype(BF)
    spread = contract(placed.reshape(-1, cols * n_tok), grouped, 1, 0).astype(BF)
    spread = spread.reshape(rows, block, line_q)

    gate_part = projected[:, :hidden_width]
    up_part = projected[:, hidden_width:]
    sigmoid_gate = jax.nn.sigmoid(gate_part)
    activated = gate_part * sigmoid_gate
    hidden = (activated * up_part).astype(BF)
    cot_down = contract(cot, down, 1, 1).astype(BF).reshape(rows, line_q, hidden_width)
    hidden_grad = lax.dot_general(
        spread, cot_down, (((2,), (1,)), ((0,), (0,))), preferred_element_type=F32
    ).reshape(-1, hidden_width)
    slope = sigmoid_gate * (1.0 + gate_part * (1.0 - sigmoid_gate))
    pre_grad = jnp.concatenate(
        [hidden_grad * up_part * slope, hidden_grad * activated], axis=1
    ).astype(BF)

    per_dev = n_tok // SEQ_LEN
    cot_own = lax.dynamic_slice_in_dim(cot, me * per_dev, per_dev, 0)
    cot_tok = jnp.repeat(cot_own, SEQ_LEN, axis=0)
    token_grad, gate_up_grad = combine(
        rows, cols, pre_grad, dm.T, cot_tok, gate_up, slot_inputs
    )

    hidden_by_query = lax.dot_general(
        spread, hidden.reshape(rows, block, hidden_width), (((1,), (1,)), ((0,), (0,))),
        preferred_element_type=F32,
    ).astype(BF).reshape(-1, hidden_width)
    down_grad = contract(hidden_by_query, cot, 0, 0).astype(BF)
    return (passage_grad, token_grad, gate_up_grad[None], down_grad[None])


def solution(mesh):
    in_specs = (
        P("row", "col"),
        P("col", "row"),
        P("row"),
        P(("row", "col"), None),
        P(("row", "col"), None),
        P(("row", "col"), None),
        P(("row", "col"), None, None),
        P(("row", "col"), None, None),
    )
    out_specs = (
        P("col", "row"),
        P(("row", "col"), None),
        P(("row", "col"), None, None),
        P(("row", "col"), None, None),
    )
    return jax.shard_map(shards, mesh=mesh, in_specs=in_specs, out_specs=out_specs, check_vma=False)
```

```python
import functools
import math

import jax
import jax.numpy as jnp
from jax import lax
from jax.experimental import pallas as pl
from jax.experimental.pallas import tpu as pltpu
from jax.sharding import PartitionSpec as P

SEQ_LEN = 8
LANES = 128
CHUNKS = 4
VMEM_LIMIT = 67_000_000
FUSED_LIMIT = 56_600_000

sharpness_divisor = 0.02

BF = jnp.bfloat16
F32 = jnp.float32
MESH = pl.DeviceIdType.MESH


def contract(a, b, da, db):
    return lax.dot_general(a, b, (((da,), (db,)), ((), ())), preferred_element_type=F32)


def span(index, size):
    return pl.ds(pl.multiple_of(index * size, size), size)


def remote(src, dst, send_sem, recv_sem, to):
    return pltpu.make_async_remote_copy(
        src_ref=src, dst_ref=dst, send_sem=send_sem, recv_sem=recv_sem,
        device_id=to, device_id_type=MESH,
    )


def greet(rows, cols):
    row, col = lax.axis_index("row"), lax.axis_index("col")
    barrier = pltpu.get_barrier_semaphore()
    for s in range(1, rows):
        pl.semaphore_signal(
            barrier, inc=1, device_id=(lax.rem(row + s, rows), col), device_id_type=MESH
        )
    for s in range(1, cols):
        pl.semaphore_signal(
            barrier, inc=1, device_id=(row, lax.rem(col + s, cols)), device_id_type=MESH
        )
    pl.semaphore_wait(barrier, rows + cols - 2)


def dispatch_kernel(
    rows, cols, cap, top,
    tok_ref, doc_ref, qry_ref, meta_ref, wgu_ref,
    x_ref, docs_ref, qrys_ref, metas_ref, proj_ref, dm_ref,
    tokc, packed, w, own_sem, w_sem, zs, zr, gs, gr, rs, ds, dr,
):
    row, col = lax.axis_index("row"), lax.axis_index("col")
    n_tok, width = tok_ref.shape
    n_doc, w_doc = doc_ref.shape
    n_qry, w_qry = qry_ref.shape
    step = width // CHUNKS
    block = cols * cap
    chips = rows // 2
    core = lax.rem(row, 2)
    chip = lax.div(row, 2)
    sibling = row + 1 - 2 * core

    def doc_strip(r):
        return docs_ref.at[:, span(r, w_doc)]

    def qry_strip(r):
        return qrys_ref.at[span(r, n_qry), :]

    def meta_strip(r):
        return metas_ref.at[pl.ds(r * cols, cols)]

    strips = (meta_strip, doc_strip, qry_strip)

    def line_piece(kind, c):
        if kind == 0:
            return meta_ref, metas_ref.at[row * cols + c]
        if kind == 1:
            return doc_ref, docs_ref.at[span(c, n_doc), span(row, w_doc)]
        if kind == 2:
            return qry_ref, qrys_ref.at[span(row, n_qry), span(c, w_qry)]
        f = kind - 3
        part = pl.ds(f * step, step)
        return tok_ref.at[:, part], tokc.at[span(c, n_tok), part]

    def along_line(kind, s, origin, to):
        src, dst = line_piece(kind, origin)
        return remote(src, dst, zs.at[kind, s], zr.at[kind, origin], (row, to))

    own = []
    for kind in range(3 + CHUNKS):
        src, dst = line_piece(kind, col)
        own.append(pltpu.make_async_copy(src, dst, own_sem.at[kind]))
    loads = [
        pltpu.make_async_copy(wgu_ref.at[span(f, step)], w.at[span(f, step)], w_sem.at[f])
        for f in range(CHUNKS)
    ]
    for copy in own:
        copy.start()
    for copy in loads:
        copy.start()
    greet(rows, cols)
    for kind in range(3 + CHUNKS):
        for s in range(1, cols):
            along_line(kind, s, col, lax.rem(col + s, cols)).start()

    def line_arrived(kind):
        own[kind].wait()
        for s in range(1, cols):
            origin = lax.rem(col + s, cols)
            along_line(kind, s, origin, origin).wait_recv()

    def peer(s):
        return 2 * lax.rem(chip + s, chips) + core

    def direct(kind, s, origin, to):
        return remote(strips[kind](origin), strips[kind](origin), gs.at[kind, s],
                      gr.at[kind, origin], (to, col))

    def relay(kind, s, origin):
        return remote(strips[kind](origin), strips[kind](origin), rs.at[kind, s],
                      gr.at[kind, origin], (sibling, col))

    for kind in range(3):
        line_arrived(kind)
        for s in range(1, chips):
            direct(kind, s, row, peer(s)).start()
        direct(kind, 0, row, sibling).start()

    target = (
        lax.broadcasted_iota(jnp.int32, (rows, n_tok), 0) * cols + col
    ).astype(F32)
    before = (
        lax.broadcasted_iota(jnp.int32, (n_tok, n_tok), 0)
        < lax.broadcasted_iota(jnp.int32, (n_tok, n_tok), 1)
    ).astype(BF)
    slot = lax.broadcasted_iota(jnp.int32, (block, n_tok), 0).astype(F32)
    for c in range(cols):
        ids = metas_ref[row * cols + c]
        hit = jnp.zeros((rows, n_tok), F32)
        for k in range(top):
            hit = hit + (ids[k : k + 1, :] == target).astype(F32)
        rank = contract(hit.astype(BF), before, 1, 0)
        place = jnp.where(hit > 0.5, rank + float(c * cap), -1.0)
        for r in range(rows):
            dm_ref[r * block : (r + 1) * block, c * n_tok : (c + 1) * n_tok] = jnp.where(
                slot == place[r : r + 1, :], 1.0, 0.0
            ).astype(BF)

    def outgoing(f, s, origin, to):
        part = pl.ds(f * step, step)
        return remote(packed.at[span(to, block), part], x_ref.at[span(origin, block), part],
                      ds.at[f, s], dr.at[f, origin], (to, col))

    def kept(f):
        part = pl.ds(f * step, step)
        return pltpu.make_async_copy(
            packed.at[span(row, block), part], x_ref.at[span(row, block), part],
            own_sem.at[3 + CHUNKS + f],
        )

    pair = 2 * block
    for f in range(CHUNKS):
        line_arrived(3 + f)
        part = slice(f * step, (f + 1) * step)

        @pl.loop(0, rows // 2)
        def _(m):
            packed[span(m, pair), part] = contract(
                dm_ref[span(m, pair), :], tokc[:, part], 1, 0
            ).astype(BF)

        for s in range(1, rows):
            outgoing(f, s, row, lax.rem(row + s, rows)).start()
        kept(f).start()

    for kind in range(3):
        for s in range(1, chips):
            origin = peer(s)
            direct(kind, s, origin, origin).wait_recv()
            relay(kind, s, origin).start()

    hidden2 = proj_ref.shape[1]
    tile = 512
    for f in range(CHUNKS):
        loads[f].wait()
        kept(f).wait()
        for s in range(1, rows):
            origin = lax.rem(row + s, rows)
            outgoing(f, s, origin, origin).wait_recv()
        part = slice(f * step, (f + 1) * step)

        @pl.loop(0, hidden2 // tile)
        def _(n):
            term = contract(x_ref[:, part], w[part, span(n, tile)], 1, 0)
            if f == 0:
                proj_ref[:, span(n, tile)] = term
            else:
                proj_ref[:, span(n, tile)] += term

    for kind in range(3):
        direct(kind, 0, sibling, sibling).wait_recv()
        for s in range(1, chips):
            origin = 2 * lax.rem(chip + s, chips) + 1 - core
            relay(kind, s, origin).wait_recv()
    for kind in range(3):
        for s in range(1, chips):
            direct(kind, s, row, peer(s)).wait_send()
            relay(kind, s, peer(s)).wait_send()
        direct(kind, 0, row, sibling).wait_send()
    for kind in range(3 + CHUNKS):
        for s in range(1, cols):
            along_line(kind, s, col, lax.rem(col + s, cols)).wait_send()
    for f in range(CHUNKS):
        for s in range(1, rows):
            outgoing(f, s, row, lax.rem(row + s, rows)).wait_send()


def dispatch(rows, cols, cap, top, tokens, documents, questions, meta, gate_up):
    n_tok, width = tokens.shape
    n_doc, w_doc = documents.shape
    n_qry, w_qry = questions.shape
    slots = rows * cols * cap
    hidden2 = gate_up.shape[1]
    dma = pltpu.SemaphoreType.DMA
    vmem = pl.BlockSpec(memory_space=pltpu.VMEM)
    hbm = pl.BlockSpec(memory_space=pl.ANY)
    return pl.pallas_call(
        functools.partial(dispatch_kernel, rows, cols, cap, top),
        out_shape=(
            jax.ShapeDtypeStruct((slots, width), BF),
            jax.ShapeDtypeStruct((cols * n_doc, rows * w_doc), BF),
            jax.ShapeDtypeStruct((rows * n_qry, cols * w_qry), BF),
            jax.ShapeDtypeStruct((rows * cols,) + meta.shape, F32),
            jax.ShapeDtypeStruct((slots, hidden2), F32),
            jax.ShapeDtypeStruct((slots, cols * n_tok), BF),
        ),
        in_specs=[vmem] * 4 + [hbm],
        out_specs=[vmem, hbm, hbm, vmem, vmem, vmem],
        scratch_shapes=[
            pltpu.VMEM((cols * n_tok, width), BF),
            pltpu.VMEM((slots, width), BF),
            pltpu.VMEM((width, hidden2), BF),
            dma((3 + 2 * CHUNKS,)),
            dma((CHUNKS,)),
            dma((3 + CHUNKS, cols)),
            dma((3 + CHUNKS, cols)),
            dma((3, rows)),
            dma((3, rows)),
            dma((3, rows)),
            dma((CHUNKS, rows)),
            dma((CHUNKS, rows)),
        ],
        compiler_params=pltpu.CompilerParams(
            collective_id=0, has_side_effects=True, vmem_limit_bytes=VMEM_LIMIT
        ),
        name="dispatch",
    )(tokens, documents, questions, meta, gate_up)


def combine_kernel(
    rows, cols,
    pre_ref, dmt_ref, cot_ref, wgu_ref, xin_ref,
    tok_ref, gug_ref,
    w, x, back, ret, comb, parts, stage,
    load_sem, own_sem, es, er, fs, fr, out_sem,
):
    row, col = lax.axis_index("row"), lax.axis_index("col")
    slots = pre_ref.shape[0]
    block = slots // rows
    width = wgu_ref.shape[0]
    n_tok = cot_ref.shape[0]
    step = width // CHUNKS

    loads = [
        pltpu.make_async_copy(wgu_ref.at[span(f, step)], w.at[span(f, step)], load_sem.at[f])
        for f in range(CHUNKS)
    ]
    loads.append(pltpu.make_async_copy(xin_ref, x, load_sem.at[CHUNKS]))
    for copy in loads:
        copy.start()
    greet(rows, cols)

    def returning(f, s, origin, to):
        part = pl.ds(f * step, step)
        return remote(back.at[span(to, block), part], ret.at[span(origin, block), part],
                      es.at[f, s], er.at[f, origin], (to, col))

    def kept(f):
        part = pl.ds(f * step, step)
        return pltpu.make_async_copy(
            back.at[span(row, block), part], ret.at[span(row, block), part], own_sem.at[f]
        )

    def home(f, s, origin, to):
        part = pl.ds(f * step, step)
        return remote(comb.at[span(to, n_tok), part], parts.at[origin, :, part],
                      fs.at[f, s], fr.at[f, origin], (row, to))

    tile = 256
    for f in range(CHUNKS):
        loads[f].wait()

        @pl.loop(0, step // tile)
        def _(n):
            back[:, pl.ds(pl.multiple_of(f * step + n * tile, tile), tile)] = contract(
                pre_ref[...], w[pl.ds(pl.multiple_of(f * step + n * tile, tile), tile), :], 1, 1
            ).astype(BF)

        for s in range(1, rows):
            returning(f, s, row, lax.rem(row + s, rows)).start()
        kept(f).start()
    loads[CHUNKS].wait()

    def grad_tile(i):
        here = slice(i * step, (i + 1) * step)
        stage[i % 2] = contract(x[:, here], pre_ref[...], 0, 0).astype(BF)

    def grad_out(i):
        return pltpu.make_async_copy(
            stage.at[i % 2], gug_ref.at[pl.ds(i * step, step)], out_sem.at[i % 2]
        )

    def merge(f):
        kept(f).wait()
        for s in range(1, rows):
            origin = lax.rem(row + s, rows)
            returning(f, s, origin, origin).wait_recv()
        part = slice(f * step, (f + 1) * step)
        comb[:, part] = contract(dmt_ref[...], ret[:, part], 1, 0).astype(BF)
        for s in range(1, cols):
            home(f, s, col, lax.rem(col + s, cols)).start()

    def finish(f):
        part = slice(f * step, (f + 1) * step)
        total = cot_ref[:, part].astype(F32) + comb[span(col, n_tok), part].astype(F32)
        for s in range(1, cols):
            origin = lax.rem(col + s, cols)
            home(f, s, origin, origin).wait_recv()
            total = total + parts[origin, :, part].astype(F32)
        tok_ref[:, part] = total.astype(BF)

    for i in range(CHUNKS):
        if i >= 2:
            grad_out(i - 2).wait()
        grad_tile(i)
        grad_out(i).start()
        merge(i)
        if i >= 1:
            finish(i - 1)
    finish(CHUNKS - 1)
    for i in range(CHUNKS - 2, CHUNKS):
        grad_out(i).wait()
    for f in range(CHUNKS):
        for s in range(1, rows):
            returning(f, s, row, lax.rem(row + s, rows)).wait_send()
        for s in range(1, cols):
            home(f, s, col, lax.rem(col + s, cols)).wait_send()


def combine(rows, cols, pre_grad, dispatch_t, cot_tok, gate_up, slot_inputs):
    slots, hidden2 = pre_grad.shape
    n_tok, width = cot_tok.shape
    step = width // CHUNKS
    dma = pltpu.SemaphoreType.DMA
    vmem = pl.BlockSpec(memory_space=pltpu.VMEM)
    hbm = pl.BlockSpec(memory_space=pl.ANY)
    return pl.pallas_call(
        functools.partial(combine_kernel, rows, cols),
        out_shape=(
            jax.ShapeDtypeStruct((n_tok, width), BF),
            jax.ShapeDtypeStruct((width, hidden2), BF),
        ),
        in_specs=[vmem, vmem, vmem, hbm, hbm],
        out_specs=[vmem, hbm],
        scratch_shapes=[
            pltpu.VMEM((width, hidden2), BF),
            pltpu.VMEM((slots, width), BF),
            pltpu.VMEM((slots, width), BF),
            pltpu.VMEM((slots, width), BF),
            pltpu.VMEM((cols * n_tok, width), BF),
            pltpu.VMEM((cols, n_tok, width), BF),
            pltpu.VMEM((2, step, hidden2), BF),
            dma((CHUNKS + 1,)),
            dma((CHUNKS,)),
            dma((CHUNKS, rows)),
            dma((CHUNKS, rows)),
            dma((CHUNKS, cols)),
            dma((CHUNKS, cols)),
            dma((2,)),
        ],
        compiler_params=pltpu.CompilerParams(
            collective_id=1, has_side_effects=True, vmem_limit_bytes=VMEM_LIMIT
        ),
        name="combine",
    )(pre_grad, dispatch_t, cot_tok, gate_up, slot_inputs)


def fused_kernel(
    rows, cols, cap, first_widths, plane_width, last_widths,
    tok_ref, doc_ref, qry_ref, pos_ref, ids_ref, rw_ref, wgu_ref, down_ref,
    passage_ref, out_ref, w, down,
    meta, metas, tokc, packed, x, proj, dm, dmt, place, weight, placed, group,
    docs, qrow, qcols, dsc, cot, cot_down, spread, hgrad, hidden, pre, ret, comb, parts,
    hbq, plane, drops,
    own_sem, load_sem, zs, zr, gs, gr, rs, ds, dr, qs, qr, ps, pr, es, er, fs, fr,
):
    row, col = lax.axis_index("row"), lax.axis_index("col")
    me = row * cols + col
    n_tok, width = tok_ref.shape
    n_doc, w_doc = doc_ref.shape
    n_qry, w_qry = qry_ref.shape
    top = ids_ref.shape[0]
    ff = down.shape[0]
    slots = x.shape[0]
    block = slots // rows
    pair = 2 * block
    chips = rows // 2
    core = lax.rem(row, 2)
    chip = lax.div(row, 2)
    sibling = row + 1 - 2 * core

    def flip(index, k, count):
        total, bit = 0, 1
        while bit < count:
            digit = lax.rem(lax.div(index, bit), 2)
            total = total + bit * (1 - digit if k & bit else digit)
            bit *= 2
        return total

    mates = list(range(2, rows)) + [1]
    line_q = cols * n_tok // SEQ_LEN

    def cuts(widths):
        edges, at = [], 0
        for size in widths:
            edges.append((at, size))
            at += size
        return edges

    first, last = cuts(first_widths), cuts(last_widths)
    n_first, n_last = len(first), len(last)

    def line_piece(kind, c):
        if kind == 0:
            return doc_ref, docs.at[span(c, n_doc), span(row, w_doc)]
        if kind == 1:
            return meta, metas.at[row * cols + c]
        if kind == 2:
            return qry_ref, qrow.at[:, span(c, w_qry)]
        at, size = first[kind - 3]
        return tok_ref.at[:, pl.ds(at, size)], tokc.at[span(c, n_tok), pl.ds(at, size)]

    ways = ((0, 1), (1, -1))

    def can_send(way):
        return col < cols - 1 if way == 0 else col > 0

    def hop(kind, step, way, block, to):
        src, dst = line_piece(kind, block)
        return remote(src if step == 0 else dst, dst, zs.at[kind, way],
                      zr.at[kind, block], (row, to))

    def advance(kinds, step):
        for kind in kinds:
            for way, d in ways:
                origin = col - d * step
                came = origin >= 0 if way == 0 else origin < cols
                if step:
                    @pl.when(came)
                    def _():
                        hop(kind, step, way, origin, col).wait_recv()

                    @pl.when(jnp.logical_and(came, can_send(way)))
                    def _():
                        hop(kind, step - 1, way, col, col + d).wait_send()

                @pl.when(jnp.logical_and(came, can_send(way)))
                def _():
                    hop(kind, step, way, origin, col + d).start()

    def settle(kind):
        for way, d in ways:
            @pl.when(can_send(way))
            def _():
                hop(kind, 0, way, col, col + d).wait_send()

    def own(kind):
        src, dst = line_piece(kind, col)
        return pltpu.make_async_copy(src, dst, own_sem.at[kind])

    plane_cut = (sum(first_widths), plane_width)
    plane_cols = pl.ds(*plane_cut)
    loads = [
        pltpu.make_async_copy(wgu_ref.at[pl.ds(at, size)], w.at[pl.ds(at, size)], load_sem.at[f])
        for f, (at, size) in enumerate(first + [plane_cut])
    ]
    loads.append(pltpu.make_async_copy(down_ref, down, load_sem.at[n_first + 1]))

    meta[:top] = ids_ref[...].astype(F32)
    meta[top:] = rw_ref[...]
    for kind in range(3 + n_first):
        own(kind).start()
    greet(rows, cols)
    queue = [(0, 1), (3,), (4,), (2,)] + [(kind,) for kind in range(5, 3 + n_first)]
    advance(queue[0], 0)
    advance(queue[1], 0)

    def gathered(i):
        for step in range(1, cols):
            advance(queue[i], step)
        for kind in queue[i]:
            own(kind).wait()
        if i + 2 < len(queue):
            advance(queue[i + 2], 0)

    def strip(kind, r):
        if kind == 0:
            return docs.at[:, span(r, w_doc)]
        if kind == 1:
            return metas.at[pl.ds(r * cols, cols)]
        if kind == 2:
            return plane.at[span(r, n_tok), :]
        return dsc.at[span(r, n_qry), :]

    def peer(s):
        return 2 * flip(chip, s, chips) + core

    def direct(kind, s, origin, to):
        src = tok_ref.at[:, plane_cols] if kind == 2 else strip(kind, origin)
        return remote(src, strip(kind, origin), gs.at[kind], gr.at[kind, 0 if s else 1], (to, col))

    def relay(kind, origin):
        return remote(strip(kind, origin), strip(kind, origin), rs.at[kind], gr.at[kind, 1],
                      (sibling, col))

    def several(kind, count, send_sem, recv_sem):
        if kind == 0:
            part = docs.at[:, pl.ds(0, count * w_doc)]
        elif kind == 1:
            part = metas.at[pl.ds(0, count * cols)]
        elif kind == 2:
            part = plane.at[pl.ds(0, count * n_tok), :]
        else:
            part = dsc.at[pl.ds(0, count * n_qry), :]
        return remote(part, part, send_sem, recv_sem, (sibling, col))

    def spread_out(kind):
        for s in range(1, chips):
            direct(kind, s, row, peer(s)).start()
        direct(kind, 0, row, sibling).start()

    def pass_on(kind):
        several(kind, chips - 1, rs.at[kind], gr.at[kind, 0]).wait_recv()
        for s in range(1, chips):
            relay(kind, peer(s)).start()

    def all_here(kind):
        several(kind, chips, rs.at[kind], gr.at[kind, 1]).wait_recv()

    def all_out(kind):
        several(kind, chips, gs.at[kind], gr.at[kind, 0]).wait_send()

    def passed(kind):
        several(kind, chips - 1, rs.at[kind], gr.at[kind, 1]).wait_send()

    own_plane = pltpu.make_async_copy(
        tok_ref.at[:, plane_cols], strip(2, row), own_sem.at[4 + 2 * n_first + n_last]
    )
    spread_out(2)
    own_plane.start()
    for copy in loads:
        copy.start()

    before = (
        lax.broadcasted_iota(jnp.int32, (n_tok, n_tok), 0)
        < lax.broadcasted_iota(jnp.int32, (n_tok, n_tok), 1)
    ).astype(BF)
    slot = lax.broadcasted_iota(jnp.int32, (block, n_tok), 0).astype(F32)

    near = tuple(k for k in mates if k < 6)
    far = tuple(k for k in mates if k >= 6)
    final = n_first - 1

    def outgoing(f, k, origin, to):
        part = pl.ds(*first[f])
        late = f == final
        return remote(
            packed.at[span(to, block), part], x.at[span(origin, block), part],
            ds.at[f + 1 if late and k in far else f], dr.at[f + k // 2 if late else f], (to, col),
        )

    def batch(f, count, send_sem, recv_sem):
        part = pl.ds(*first[f])
        here = pl.ds(0, count * block)
        return remote(packed.at[here, part], x.at[here, part], send_sem, recv_sem, (row, col))

    def sent(f, late=False):
        if f < final:
            batch(f, rows - 1, ds.at[f], dr.at[f]).wait_send()
        elif late:
            batch(f, len(far), ds.at[f + 1], dr.at[f]).wait_send()
        else:
            batch(f, len(near), ds.at[f], dr.at[f]).wait_send()

    def kept(f):
        part = pl.ds(*first[f])
        return pltpu.make_async_copy(
            packed.at[span(row, block), part], x.at[span(row, block), part],
            own_sem.at[3 + n_first + f],
        )

    def send(f, offsets):
        for s in offsets:
            outgoing(f, s, row, flip(row, s, rows)).start()

    def pack(f):
        part = pl.ds(*first[f])

        @pl.loop(0, chips)
        def _(m):
            packed[span(m, pair), part] = contract(
                dm[span(m, pair), :], tokc[:, part], 1, 0
            ).astype(BF)

        kept(f).start()

    tile = 512

    def project(f):
        loads[f].wait()
        kept(f).wait()
        batch(f, rows - 1, ds.at[f], dr.at[f]).wait_recv()
        part = pl.ds(*first[f])

        @pl.loop(0, 2 * ff // tile)
        def _(n):
            term = contract(x[:, part], w[part, span(n, tile)], 1, 0)
            if f == 0:
                proj[:, span(n, tile)] = term
            else:
                proj[:, span(n, tile)] += term

    def query_piece(origin, to):
        return qrow.at[:, span(to, w_doc)], qcols.at[span(origin, n_qry), :]

    def queries(s, origin, to):
        src, dst = query_piece(origin, to)
        return remote(src, dst, qs.at[0], qr.at[0], (to, col))

    def all_queries():
        part = qcols.at[pl.ds(0, (rows - 1) * n_qry), :]
        return remote(part, part, qs.at[0], qr.at[0], (sibling, col))

    def own_queries():
        src, dst = query_piece(row, row)
        return pltpu.make_async_copy(src, dst, own_sem.at[3 + 2 * n_first])

    share = rows * cap

    def dropped(s, origin, to):
        return remote(packed.at[span(to, share), plane_cols], drops.at[span(origin, share), :],
                      ps.at[0], pr.at[0], (row, to))

    def all_dropped():
        part = drops.at[pl.ds(0, (cols - 1) * share), :]
        return remote(part, part, ps.at[0], pr.at[0], (row, col))

    def own_drop():
        return pltpu.make_async_copy(
            packed.at[span(col, share), plane_cols], drops.at[span(col, share), :],
            own_sem.at[5 + 2 * n_first + n_last],
        )

    def pack_plane():
        wanted_by = (
            lax.broadcasted_iota(jnp.int32, (cols, n_tok), 0) + row * cols
        ).astype(F32)
        spots = lax.broadcasted_iota(jnp.int32, (share, n_tok), 0).astype(F32)
        for r in range(rows):
            ids = metas[r * cols + col, :top]
            hit = jnp.zeros((cols, n_tok), F32)
            for k in range(top):
                hit = hit + (ids[k : k + 1, :] == wanted_by).astype(F32)
            rank = contract(hit.astype(BF), before, 1, 0)
            spot = jnp.where(hit > 0.5, rank + float(r * cap), -1.0)
            for c in range(cols):
                pre[c * share : (c + 1) * share, r * n_tok : (r + 1) * n_tok] = jnp.where(
                    spots == spot[c : c + 1, :], 1.0, 0.0
                ).astype(BF)

        @pl.loop(0, cols)
        def _(c):
            packed[span(c, share), plane_cols] = contract(
                pre[span(c, share), : rows * n_tok], plane[...], 1, 0
            ).astype(BF)

        settle(2 + n_first)
        for s in range(1, cols):
            dropped(s, col, lax.rem(col + s, cols)).start()
        own_drop().start()

    def order_rows():
        at = lax.broadcasted_iota(jnp.int32, (slots, LANES), 0).astype(F32)
        lane_at = lax.broadcasted_iota(jnp.int32, (slots, LANES), 1).astype(F32)
        line_of = jnp.floor((at + 0.5) * (1.0 / block))
        rest = at - line_of * block
        plane_of = jnp.floor((rest + 0.5) * (1.0 / cap))
        source = plane_of * share + line_of * cap + (rest - plane_of * cap)
        for n in range(slots // LANES):
            pre[:, n * LANES : (n + 1) * LANES] = jnp.where(
                lane_at + float(n * LANES) == source, 1.0, 0.0
            ).astype(BF)

    def project_plane():
        loads[n_first].wait()
        own_drop().wait()
        all_dropped().wait_recv()
        x[:, plane_cols] = contract(pre[:, :slots], drops[...], 1, 0).astype(BF)

        @pl.loop(0, 2 * ff // tile)
        def _(n):
            proj[:, span(n, tile)] += contract(
                x[:, plane_cols], w[plane_cols, span(n, tile)], 1, 0
            )

    gathered(0)
    spread_out(0)
    spread_out(1)
    target = (
        lax.broadcasted_iota(jnp.int32, (rows, n_tok), 0) * cols + col
    ).astype(F32)
    for c in range(cols):
        ids = metas[row * cols + c, :top]
        hit = jnp.zeros((rows, n_tok), F32)
        for k in range(top):
            hit = hit + (ids[k : k + 1, :] == target).astype(F32)
        rank = contract(hit.astype(BF), before, 1, 0)
        spot = jnp.where(hit > 0.5, rank + float(c * cap), -1.0)
        for r in range(rows):
            dm[r * block : (r + 1) * block, c * n_tok : (c + 1) * n_tok] = jnp.where(
                slot == spot[r : r + 1, :], 1.0, 0.0
            ).astype(BF)
    gathered(1)
    pack(0)
    send(0, mates)
    pass_on(2)
    gathered(2)
    pack(1)
    pass_on(1)
    pass_on(0)
    gathered(3)
    all_here(0)
    scores = contract(qrow[...], docs[...], 1, 1) / sharpness_divisor
    peak = jnp.max(scores, axis=1, keepdims=True)
    grown = jnp.exp(scores - peak)
    total = jnp.sum(grown, axis=1, keepdims=True)
    square = (n_qry, n_qry)
    diagonal = lax.broadcasted_iota(jnp.int32, square, 0) == lax.broadcasted_iota(jnp.int32, square, 1)
    wanted = jnp.sum(
        jnp.where(diagonal, pos_ref[...].astype(F32), 0.0), axis=1, keepdims=True
    )
    onehot = (
        wanted == lax.broadcasted_iota(jnp.int32, scores.shape, 1).astype(F32)
    ).astype(F32)
    dsc[span(row, n_qry), :] = ((grown / total - onehot) / sharpness_divisor).astype(BF)
    for c in range(cols):
        here = slice(c * n_tok, (c + 1) * n_tok)
        dmt[here, :] = dm[:, here].astype(F32).T.astype(BF)
    spread_out(3)
    send(1, near)
    gathered(4)
    pack(2)
    send(1, far)
    all_here(1)
    all_here(2)
    own_plane.wait()
    pack_plane()
    pass_on(3)
    sent(0)
    send(2, near)
    order_rows()

    lines = rows * cols
    each = lax.broadcasted_iota(jnp.int32, (lines, n_tok), 0)
    mine = me.astype(F32)
    chosen = jnp.zeros((lines, n_tok), F32)
    amount = jnp.zeros((lines, n_tok), F32)
    for b in range(lines):
        hit = (metas[b, :top] == mine).astype(F32)
        found = jnp.sum(hit, axis=0, keepdims=True)
        value = jnp.sum(hit * metas[b, top:], axis=0, keepdims=True)
        chosen = jnp.where(each == b, found, chosen)
        amount = jnp.where(each == b, value, amount)
    rank = contract(chosen.astype(BF), before, 1, 0)
    begin = (lax.rem(each, cols) * cap).astype(F32)
    place[...] = jnp.where(chosen > 0.5, rank + begin, -1.0)
    weight[...] = amount
    group[...] = (
        lax.broadcasted_iota(jnp.int32, (cols * n_tok, line_q), 0) // SEQ_LEN
        == lax.broadcasted_iota(jnp.int32, (cols * n_tok, line_q), 1)
    ).astype(BF)

    @pl.loop(0, rows)
    def _(r):
        for c in range(cols):
            here = pl.ds(r * cols + c, 1)
            placed[:, c * n_tok : (c + 1) * n_tok] = jnp.where(
                slot == place[here, :], weight[here, :], 0.0
            ).astype(BF)
        spread[span(r, block), :] = contract(placed[...], group[...], 1, 0).astype(BF)

    project(0)
    all_here(3)

    @pl.loop(0, width // tile)
    def _(n):
        cot[:, span(n, tile)] = (
            contract(dsc[...], docs[:, span(n, tile)], 1, 0) / SEQ_LEN
        ).astype(BF)

    loads[n_first + 1].wait()
    small = 256

    @pl.loop(0, ff // small)
    def _(n):
        cot_down[:, span(n, small)] = contract(
            cot[...], down[span(n, small), :], 1, 1
        ).astype(BF)

    sent(1)
    send(2, far)
    for s in mates:
        queries(s, row, flip(row, s, rows)).start()
    own_queries().start()
    project(1)
    project_plane()

    def returning(f, s, origin, to):
        part = pl.ds(*last[f])
        return remote(packed.at[span(to, block), part], ret.at[span(origin, block), part],
                      es.at[f], er.at[f], (to, col))

    def all_returned(f):
        part = pl.ds(*last[f])
        here = pl.ds(0, (rows - 1) * block)
        return remote(packed.at[here, part], ret.at[here, part], es.at[f], er.at[f], (row, col))

    def held(f):
        part = pl.ds(*last[f])
        return pltpu.make_async_copy(
            packed.at[span(row, block), part], ret.at[span(row, block), part],
            own_sem.at[4 + 2 * n_first + f],
        )

    def home(f, s, origin, to):
        part = pl.ds(*last[f])
        return remote(comb.at[span(to, n_tok), part], parts.at[origin, :, part],
                      fs.at[f], fr.at[f], (row, to))

    def all_home(f):
        part = pl.ds(*last[f])
        here = pl.ds(0, cols - 1)
        return remote(parts.at[here, :, part], parts.at[here, :, part], fs.at[f], fr.at[f], (row, col))

    f_end = n_first - 1
    loads[f_end].wait()
    kept(f_end).wait()
    end = pl.ds(*first[f_end])
    groups = [[0, 1], [2, 3], [4, 5], list(range(6, n_last))]

    def group_cols(g):
        return pl.ds(last[groups[g][0]][0], sum(last[f][1] for f in groups[g]))

    begin_cols = group_cols(0)
    lane = 128

    for s in [k for k in (1, 2, 3, 0) if k < chips]:
        other = flip(chip, s, chips)
        count = 2 if s else 1
        batch(f_end, count, ds.at[f_end], dr.at[f_end + s]).wait_recv()
        here = span(other, pair)

        @pl.loop(0, 2 * ff // tile)
        def _(n):
            proj[here, span(n, tile)] += contract(x[here, end], w[end, span(n, tile)], 1, 0)

        for k in range(2):
            r = 2 * other + k
            at = span(r, block)
            hgrad[...] = contract(spread[at, :], cot_down[span(r, line_q), :], 1, 0)

            @pl.loop(0, ff // lane)
            def _(n):
                left = span(n, lane)
                right = pl.ds(pl.multiple_of(ff + n * lane, lane), lane)
                gate, up = proj[at, left], proj[at, right]
                sig = jax.nn.sigmoid(gate)
                act = gate * sig
                grad = hgrad[:, left]
                hidden[at, left] = (act * up).astype(BF)
                pre[at, left] = (grad * up * (sig * (1.0 + gate * (1.0 - sig)))).astype(BF)
                pre[at, right] = (grad * act).astype(BF)

        packed[here, begin_cols] = contract(pre[here, :], w[begin_cols, :], 1, 1).astype(BF)
        for f in groups[0]:
            for k in (2 * s, 2 * s + 1):
                if k:
                    returning(f, k, row, flip(row, k, rows)).start()
                else:
                    held(f).start()

    def give_back(g):
        part = group_cols(g)
        if g == 2:
            sent(final)
            sent(final, late=True)
        if g == 3:
            all_dropped().wait_send()

        @pl.loop(0, 2)
        def _(m):
            half = span(m, slots // 2)
            packed[half, part] = contract(pre[half, :], w[part, :], 1, 1).astype(BF)

        for f in groups[g]:
            for s in mates:
                returning(f, s, row, flip(row, s, rows)).start()
            held(f).start()

    n_gate, n_down = width // small, ff // small

    def grad_tile(i):
        if i < n_gate:
            here = slice(i * small, (i + 1) * small)
            w[here, :] = contract(x[:, here], pre[...], 0, 0).astype(BF)
        else:
            here = slice((i - n_gate) * small, (i - n_gate + 1) * small)
            down[here, :] = contract(hbq[:, here], cot[...], 0, 0).astype(BF)

    def merge(f):
        held(f).wait()
        all_returned(f).wait_recv()
        part = pl.ds(*last[f])
        comb[:, part] = contract(dmt[...], ret[:, part], 1, 0).astype(BF)
        for s in range(1, cols):
            home(f, s, col, lax.rem(col + s, cols)).start()

    per_dev = n_tok // SEQ_LEN
    repeat = (
        lax.broadcasted_iota(jnp.int32, (n_tok, per_dev), 0) // SEQ_LEN
        == lax.broadcasted_iota(jnp.int32, (n_tok, per_dev), 1)
    ).astype(BF)

    def finish(f):
        part = pl.ds(*last[f])
        sums = contract(repeat, cot[span(me, per_dev), part], 1, 0)
        sums = sums + comb[span(col, n_tok), part].astype(F32)
        all_home(f).wait_recv()
        for s in range(1, cols):
            origin = lax.rem(col + s, cols)
            sums = sums + parts[origin, :, part].astype(F32)
        out_ref[:, part] = sums.astype(BF)

    def by_query():
        @pl.loop(0, rows)
        def _(r):
            hbq[span(r, line_q), :] = contract(
                spread[span(r, block), :], hidden[span(r, block), :], 0, 0
            ).astype(BF)

    def settle_sends():
        for kind in range(4):
            all_out(kind)
            passed(kind)
        for kind in range(2 + n_first):
            settle(kind)
        all_queries().wait_send()

    todo = list(range(n_gate, n_gate + n_down)) + list(range(n_gate))

    def grads(count):
        for i in todo[:count]:
            grad_tile(i)
        del todo[:count]

    give_back(1)
    merge(0)
    give_back(2)
    merge(1)
    by_query()
    finish(0)
    all_queries().wait_recv()
    own_queries().wait()
    passage_ref[...] = contract(dsc[:, span(col, n_doc)], qcols[...], 0, 0)
    settle_sends()
    grads(2)
    merge(2)
    finish(1)
    give_back(3)
    for f in range(3, n_last - 2):
        grads(2)
        merge(f)
        finish(f - 1)
    grads(len(todo))
    for f in range(n_last - 2, n_last):
        merge(f)
    for f in range(n_last - 3, n_last):
        finish(f)

    for f in range(n_last):
        all_returned(f).wait_send()
        all_home(f).wait_send()


def fused_plan(rows, cols, cap, top, plane_width, tokens, documents, questions, down):
    n_tok, width = tokens.shape
    n_doc, w_doc = documents.shape
    n_qry = questions.shape[0]
    ff = down.shape[0]
    block = cols * cap
    slots = rows * block
    line = cols * n_tok
    line_q = line // SEQ_LEN
    n_all = rows * n_qry
    return [
        ((2 * top, n_tok), F32),
        ((rows * cols, 2 * top, n_tok), F32),
        ((line, width - plane_width), BF),
        ((slots, width), BF),
        ((slots, width), BF),
        ((slots, 2 * ff), F32),
        ((slots, line), BF),
        ((line, slots), BF),
        ((rows * cols, n_tok), F32),
        ((rows * cols, n_tok), F32),
        ((block, line), BF),
        ((line, line_q), BF),
        ((cols * n_doc, width), BF),
        ((n_qry, width), BF),
        ((n_all, w_doc), BF),
        ((n_all, cols * n_doc), BF),
        ((n_all, width), BF),
        ((n_all, ff), BF),
        ((slots, line_q), BF),
        ((block, ff), F32),
        ((slots, ff), BF),
        ((slots, 2 * ff), BF),
        ((slots, width), BF),
        ((line, width), BF),
        ((cols, n_tok, width), BF),
        ((n_all, ff), BF),
        ((rows * n_tok, plane_width), BF),
        ((slots, plane_width), BF),
    ]


def plan_bytes(plan):
    return sum(math.prod(shape) * jnp.dtype(kind).itemsize for shape, kind in plan)


def fused(rows, cols, cap, plan, tokens, documents, questions, positive, ids, weights, gate_up, down):
    n_tok, width = tokens.shape
    n_doc, w_doc = documents.shape
    hidden2 = gate_up.shape[1]
    first = [width * k // 16 for k in (4, 5, 4)]
    plane_width = width - sum(first)
    last = [width // 8] * 7 + [width // 16] * 2
    dma = pltpu.SemaphoreType.DMA
    vmem = pl.BlockSpec(memory_space=pltpu.VMEM)
    hbm = pl.BlockSpec(memory_space=pl.ANY)
    n_first, n_last = len(first), len(last)
    return pl.pallas_call(
        functools.partial(fused_kernel, rows, cols, cap, first, plane_width, last),
        out_shape=(
            pltpu.VMEM((n_doc, w_doc), F32),
            pltpu.VMEM((n_tok, width), BF),
            pltpu.VMEM((width, hidden2), BF),
            pltpu.VMEM(down.shape, BF),
        ),
        in_specs=[vmem] * 6 + [hbm] * 2,
        out_specs=[vmem] * 4,
        scratch_shapes=[pltpu.VMEM(shape, kind) for shape, kind in plan]
        + [
            dma((6 + 2 * n_first + n_last,)),
            dma((n_first + 2,)),
            dma((3 + n_first, 2)),
            dma((3 + n_first, cols)),
            dma((4,)),
            dma((4, 2)),
            dma((4,)),
            dma((n_first + 1,)),
            dma((n_first + rows // 2,)),
            dma((1,)),
            dma((1,)),
            dma((1,)),
            dma((1,)),
            dma((n_last,)),
            dma((n_last,)),
            dma((n_last,)),
            dma((n_last,)),
        ],
        compiler_params=pltpu.CompilerParams(
            collective_id=2, has_side_effects=True, vmem_limit_bytes=FUSED_LIMIT
        ),
        name="fused",
    )(tokens, documents, questions, positive.reshape(1, -1), ids.T, weights.T, gate_up, down)


def settle_kernel(pieces, *refs):
    count = len(pieces)
    sources, targets, sem = refs[:count], refs[count:-1], refs[-1]
    copies = []
    for i, parts in enumerate(pieces):
        size = sources[i].shape[0] // parts
        for p in range(parts):
            at = pl.ds(p * size, size)
            copies.append(
                pltpu.make_async_copy(sources[i].at[at], targets[i].at[at], sem.at[len(copies)])
            )
    for copy in copies:
        copy.start()
    for copy in copies:
        copy.wait()


def settled(*arrays):
    sizes = [a.size * a.dtype.itemsize // (1 << 20) for a in arrays]
    pieces = [1 << max(0, n.bit_length() - 1) for n in sizes]
    vmem = pl.BlockSpec(memory_space=pltpu.VMEM)
    hbm = pl.BlockSpec(memory_space=pl.ANY)
    return pl.pallas_call(
        functools.partial(settle_kernel, pieces),
        out_shape=tuple(pltpu.HBM(a.shape, a.dtype) for a in arrays),
        in_specs=[vmem] * len(arrays),
        out_specs=[hbm] * len(arrays),
        scratch_shapes=[pltpu.SemaphoreType.DMA((sum(pieces),))],
        compiler_params=pltpu.CompilerParams(vmem_limit_bytes=1 << 20),
        name="settle",
    )(*[pltpu.with_memory_space_constraint(a, pltpu.VMEM) for a in arrays])


def shards(
    question_vectors,
    document_vectors,
    positive,
    tokens,
    expert_ids,
    route_weights,
    expert_gate_up,
    expert_down,
):
    rows = lax.axis_size("row")
    cols = lax.axis_size("col")
    row = lax.axis_index("row")
    col = lax.axis_index("col")
    devices_all = rows * cols
    me = row * cols + col
    n_tok, width = tokens.shape
    top = expert_ids.shape[1]
    experts_all = devices_all * expert_gate_up.shape[0]
    cap = max(2, (n_tok * top * 9 + 8 * experts_all - 1) // (8 * experts_all))
    block = cols * cap
    hidden_width = expert_down.shape[1]
    gate_up = expert_gate_up[0]
    down = expert_down[0]

    plan = fused_plan(rows, cols, cap, top, width * 3 // 16, tokens, document_vectors, question_vectors, down)
    if rows == 8 and plan_bytes(plan) < FUSED_LIMIT - 4_000_000:
        passage_grad, token_grad, gate_up_grad, down_grad = fused(
            rows, cols, cap, plan, tokens, document_vectors, question_vectors, positive,
            expert_ids, route_weights, gate_up, down,
        )
        passage_grad, token_grad, gate_up_grad, down_grad = settled(
            passage_grad, token_grad, gate_up_grad, down_grad
        )
        return (passage_grad, token_grad, gate_up_grad[None], down_grad[None])

    n_qry = positive.shape[0]
    pos_rows = -(-n_qry // (8 * LANES)) * 8
    pos = jnp.pad(positive, (0, pos_rows * LANES - n_qry)).astype(F32).reshape(pos_rows, LANES)
    meta = jnp.concatenate([expert_ids.T.astype(F32), route_weights.T, pos], axis=0)
    slot_inputs, docs, qrys, metas, projected, dm = dispatch(
        rows, cols, cap, top, tokens, document_vectors, question_vectors, meta, gate_up
    )

    ids = metas[:, :top].astype(jnp.int32)
    weights = metas[:, top : 2 * top]
    positive_all = metas.reshape(rows, cols, -1, LANES)[:, 0, 2 * top :].reshape(rows, -1)
    positive_all = positive_all[:, :n_qry].reshape(-1).astype(jnp.int32)

    scores = contract(qrys, docs, 1, 1) / sharpness_divisor
    peak = jnp.max(scores, axis=1, keepdims=True)
    grown = jnp.exp(scores - peak)
    total = jnp.sum(grown, axis=1, keepdims=True)
    onehot = (
        positive_all[:, None] == jnp.arange(docs.shape[0], dtype=jnp.int32)[None, :]
    ).astype(F32)
    dscore = ((grown / total - onehot) / sharpness_divisor).astype(BF)
    cot = (contract(dscore, docs, 1, 0) / SEQ_LEN).astype(BF)
    n_doc, w_doc = document_vectors.shape
    passage_grad = contract(
        lax.dynamic_slice_in_dim(dscore, col * n_doc, n_doc, 1),
        lax.dynamic_slice_in_dim(qrys, row * w_doc, w_doc, 1),
        0, 0,
    )

    mine = ids == me
    chosen = jnp.any(mine, axis=1)
    weight = jnp.sum(jnp.where(mine, weights, 0.0), axis=1)
    earlier = (
        lax.broadcasted_iota(jnp.int32, (n_tok, n_tok), 0)
        < lax.broadcasted_iota(jnp.int32, (n_tok, n_tok), 1)
    ).astype(BF)
    rank = contract(chosen.astype(BF), earlier, 1, 0).astype(jnp.int32)
    first = jnp.tile(jnp.arange(cols, dtype=jnp.int32) * cap, rows)[:, None]
    place = jnp.where(chosen, first + rank, -1).reshape(rows, 1, cols * n_tok)
    line_weight = weight.reshape(rows, 1, cols * n_tok)
    placed = jnp.where(
        place == jnp.arange(block, dtype=jnp.int32)[None, :, None], line_weight, 0.0
    ).astype(BF)
    line_q = cols * n_tok // SEQ_LEN
    grouped = (
        lax.broadcasted_iota(jnp.int32, (cols * n_tok, line_q), 0) // SEQ_LEN
        == lax.broadcasted_iota(jnp.int32, (cols * n_tok, line_q), 1)
    ).astype(BF)
    spread = contract(placed.reshape(-1, cols * n_tok), grouped, 1, 0).astype(BF)
    spread = spread.reshape(rows, block, line_q)

    gate_part = projected[:, :hidden_width]
    up_part = projected[:, hidden_width:]
    sigmoid_gate = jax.nn.sigmoid(gate_part)
    activated = gate_part * sigmoid_gate
    hidden = (activated * up_part).astype(BF)
    cot_down = contract(cot, down, 1, 1).astype(BF).reshape(rows, line_q, hidden_width)
    hidden_grad = lax.dot_general(
        spread, cot_down, (((2,), (1,)), ((0,), (0,))), preferred_element_type=F32
    ).reshape(-1, hidden_width)
    slope = sigmoid_gate * (1.0 + gate_part * (1.0 - sigmoid_gate))
    pre_grad = jnp.concatenate(
        [hidden_grad * up_part * slope, hidden_grad * activated], axis=1
    ).astype(BF)

    per_dev = n_tok // SEQ_LEN
    cot_own = lax.dynamic_slice_in_dim(cot, me * per_dev, per_dev, 0)
    cot_tok = jnp.repeat(cot_own, SEQ_LEN, axis=0)
    token_grad, gate_up_grad = combine(
        rows, cols, pre_grad, dm.T, cot_tok, gate_up, slot_inputs
    )

    hidden_by_query = lax.dot_general(
        spread, hidden.reshape(rows, block, hidden_width), (((1,), (1,)), ((0,), (0,))),
        preferred_element_type=F32,
    ).astype(BF).reshape(-1, hidden_width)
    down_grad = contract(hidden_by_query, cot, 0, 0).astype(BF)
    return (passage_grad, token_grad, gate_up_grad[None], down_grad[None])


def solution(mesh):
    in_specs = (
        P("row", "col"),
        P("col", "row"),
        P("row"),
        P(("row", "col"), None),
        P(("row", "col"), None),
        P(("row", "col"), None),
        P(("row", "col"), None, None),
        P(("row", "col"), None, None),
    )
    out_specs = (
        P("col", "row"),
        P(("row", "col"), None),
        P(("row", "col"), None, None),
        P(("row", "col"), None, None),
    )
    return jax.shard_map(shards, mesh=mesh, in_specs=in_specs, out_specs=out_specs, check_vma=False)
```

```python
import functools
import math

import jax
import jax.numpy as jnp
from jax import lax
from jax.experimental import pallas as pl
from jax.experimental.pallas import tpu as pltpu
from jax.sharding import PartitionSpec as P

SEQ_LEN = 8
LANES = 128
CHUNKS = 4
VMEM_LIMIT = 67_000_000
FUSED_LIMIT = 56_600_000

sharpness_divisor = 0.02

BF = jnp.bfloat16
F32 = jnp.float32
MESH = pl.DeviceIdType.MESH


def contract(a, b, da, db):
    return lax.dot_general(a, b, (((da,), (db,)), ((), ())), preferred_element_type=F32)


def span(index, size):
    return pl.ds(pl.multiple_of(index * size, size), size)


def remote(src, dst, send_sem, recv_sem, to):
    return pltpu.make_async_remote_copy(
        src_ref=src, dst_ref=dst, send_sem=send_sem, recv_sem=recv_sem,
        device_id=to, device_id_type=MESH,
    )


def greet_signal(rows, cols):
    row, col = lax.axis_index("row"), lax.axis_index("col")
    barrier = pltpu.get_barrier_semaphore()
    for s in range(1, rows):
        pl.semaphore_signal(
            barrier, inc=1, device_id=(lax.rem(row + s, rows), col), device_id_type=MESH
        )
    for s in range(1, cols):
        pl.semaphore_signal(
            barrier, inc=1, device_id=(row, lax.rem(col + s, cols)), device_id_type=MESH
        )


def greet_wait(rows, cols):
    pl.semaphore_wait(pltpu.get_barrier_semaphore(), rows + cols - 2)


def greet(rows, cols):
    greet_signal(rows, cols)
    greet_wait(rows, cols)


def dispatch_kernel(
    rows, cols, cap, top,
    tok_ref, doc_ref, qry_ref, meta_ref, wgu_ref,
    x_ref, docs_ref, qrys_ref, metas_ref, proj_ref, dm_ref,
    tokc, packed, w, own_sem, w_sem, zs, zr, gs, gr, rs, ds, dr,
):
    row, col = lax.axis_index("row"), lax.axis_index("col")
    n_tok, width = tok_ref.shape
    n_doc, w_doc = doc_ref.shape
    n_qry, w_qry = qry_ref.shape
    step = width // CHUNKS
    block = cols * cap
    chips = rows // 2
    core = lax.rem(row, 2)
    chip = lax.div(row, 2)
    sibling = row + 1 - 2 * core

    def doc_strip(r):
        return docs_ref.at[:, span(r, w_doc)]

    def qry_strip(r):
        return qrys_ref.at[span(r, n_qry), :]

    def meta_strip(r):
        return metas_ref.at[pl.ds(r * cols, cols)]

    strips = (meta_strip, doc_strip, qry_strip)

    def line_piece(kind, c):
        if kind == 0:
            return meta_ref, metas_ref.at[row * cols + c]
        if kind == 1:
            return doc_ref, docs_ref.at[span(c, n_doc), span(row, w_doc)]
        if kind == 2:
            return qry_ref, qrys_ref.at[span(row, n_qry), span(c, w_qry)]
        f = kind - 3
        part = pl.ds(f * step, step)
        return tok_ref.at[:, part], tokc.at[span(c, n_tok), part]

    def along_line(kind, s, origin, to):
        src, dst = line_piece(kind, origin)
        return remote(src, dst, zs.at[kind, s], zr.at[kind, origin], (row, to))

    own = []
    for kind in range(3 + CHUNKS):
        src, dst = line_piece(kind, col)
        own.append(pltpu.make_async_copy(src, dst, own_sem.at[kind]))
    loads = [
        pltpu.make_async_copy(wgu_ref.at[span(f, step)], w.at[span(f, step)], w_sem.at[f])
        for f in range(CHUNKS)
    ]
    for copy in own:
        copy.start()
    for copy in loads:
        copy.start()
    greet(rows, cols)
    for kind in range(3 + CHUNKS):
        for s in range(1, cols):
            along_line(kind, s, col, lax.rem(col + s, cols)).start()

    def line_arrived(kind):
        own[kind].wait()
        for s in range(1, cols):
            origin = lax.rem(col + s, cols)
            along_line(kind, s, origin, origin).wait_recv()

    def peer(s):
        return 2 * lax.rem(chip + s, chips) + core

    def direct(kind, s, origin, to):
        return remote(strips[kind](origin), strips[kind](origin), gs.at[kind, s],
                      gr.at[kind, origin], (to, col))

    def relay(kind, s, origin):
        return remote(strips[kind](origin), strips[kind](origin), rs.at[kind, s],
                      gr.at[kind, origin], (sibling, col))

    for kind in range(3):
        line_arrived(kind)
        for s in range(1, chips):
            direct(kind, s, row, peer(s)).start()
        direct(kind, 0, row, sibling).start()

    target = (
        lax.broadcasted_iota(jnp.int32, (rows, n_tok), 0) * cols + col
    ).astype(F32)
    before = (
        lax.broadcasted_iota(jnp.int32, (n_tok, n_tok), 0)
        < lax.broadcasted_iota(jnp.int32, (n_tok, n_tok), 1)
    ).astype(BF)
    slot = lax.broadcasted_iota(jnp.int32, (block, n_tok), 0).astype(F32)
    for c in range(cols):
        ids = metas_ref[row * cols + c]
        hit = jnp.zeros((rows, n_tok), F32)
        for k in range(top):
            hit = hit + (ids[k : k + 1, :] == target).astype(F32)
        rank = contract(hit.astype(BF), before, 1, 0)
        place = jnp.where(hit > 0.5, rank + float(c * cap), -1.0)
        for r in range(rows):
            dm_ref[r * block : (r + 1) * block, c * n_tok : (c + 1) * n_tok] = jnp.where(
                slot == place[r : r + 1, :], 1.0, 0.0
            ).astype(BF)

    def outgoing(f, s, origin, to):
        part = pl.ds(f * step, step)
        return remote(packed.at[span(to, block), part], x_ref.at[span(origin, block), part],
                      ds.at[f, s], dr.at[f, origin], (to, col))

    def kept(f):
        part = pl.ds(f * step, step)
        return pltpu.make_async_copy(
            packed.at[span(row, block), part], x_ref.at[span(row, block), part],
            own_sem.at[3 + CHUNKS + f],
        )

    pair = 2 * block
    for f in range(CHUNKS):
        line_arrived(3 + f)
        part = slice(f * step, (f + 1) * step)

        @pl.loop(0, rows // 2)
        def _(m):
            packed[span(m, pair), part] = contract(
                dm_ref[span(m, pair), :], tokc[:, part], 1, 0
            ).astype(BF)

        for s in range(1, rows):
            outgoing(f, s, row, lax.rem(row + s, rows)).start()
        kept(f).start()

    for kind in range(3):
        for s in range(1, chips):
            origin = peer(s)
            direct(kind, s, origin, origin).wait_recv()
            relay(kind, s, origin).start()

    hidden2 = proj_ref.shape[1]
    tile = 512
    for f in range(CHUNKS):
        loads[f].wait()
        kept(f).wait()
        for s in range(1, rows):
            origin = lax.rem(row + s, rows)
            outgoing(f, s, origin, origin).wait_recv()
        part = slice(f * step, (f + 1) * step)

        @pl.loop(0, hidden2 // tile)
        def _(n):
            term = contract(x_ref[:, part], w[part, span(n, tile)], 1, 0)
            if f == 0:
                proj_ref[:, span(n, tile)] = term
            else:
                proj_ref[:, span(n, tile)] += term

    for kind in range(3):
        direct(kind, 0, sibling, sibling).wait_recv()
        for s in range(1, chips):
            origin = 2 * lax.rem(chip + s, chips) + 1 - core
            relay(kind, s, origin).wait_recv()
    for kind in range(3):
        for s in range(1, chips):
            direct(kind, s, row, peer(s)).wait_send()
            relay(kind, s, peer(s)).wait_send()
        direct(kind, 0, row, sibling).wait_send()
    for kind in range(3 + CHUNKS):
        for s in range(1, cols):
            along_line(kind, s, col, lax.rem(col + s, cols)).wait_send()
    for f in range(CHUNKS):
        for s in range(1, rows):
            outgoing(f, s, row, lax.rem(row + s, rows)).wait_send()


def dispatch(rows, cols, cap, top, tokens, documents, questions, meta, gate_up):
    n_tok, width = tokens.shape
    n_doc, w_doc = documents.shape
    n_qry, w_qry = questions.shape
    slots = rows * cols * cap
    hidden2 = gate_up.shape[1]
    dma = pltpu.SemaphoreType.DMA
    vmem = pl.BlockSpec(memory_space=pltpu.VMEM)
    hbm = pl.BlockSpec(memory_space=pl.ANY)
    return pl.pallas_call(
        functools.partial(dispatch_kernel, rows, cols, cap, top),
        out_shape=(
            jax.ShapeDtypeStruct((slots, width), BF),
            jax.ShapeDtypeStruct((cols * n_doc, rows * w_doc), BF),
            jax.ShapeDtypeStruct((rows * n_qry, cols * w_qry), BF),
            jax.ShapeDtypeStruct((rows * cols,) + meta.shape, F32),
            jax.ShapeDtypeStruct((slots, hidden2), F32),
            jax.ShapeDtypeStruct((slots, cols * n_tok), BF),
        ),
        in_specs=[vmem] * 4 + [hbm],
        out_specs=[vmem, hbm, hbm, vmem, vmem, vmem],
        scratch_shapes=[
            pltpu.VMEM((cols * n_tok, width), BF),
            pltpu.VMEM((slots, width), BF),
            pltpu.VMEM((width, hidden2), BF),
            dma((3 + 2 * CHUNKS,)),
            dma((CHUNKS,)),
            dma((3 + CHUNKS, cols)),
            dma((3 + CHUNKS, cols)),
            dma((3, rows)),
            dma((3, rows)),
            dma((3, rows)),
            dma((CHUNKS, rows)),
            dma((CHUNKS, rows)),
        ],
        compiler_params=pltpu.CompilerParams(
            collective_id=0, has_side_effects=True, vmem_limit_bytes=VMEM_LIMIT
        ),
        name="dispatch",
    )(tokens, documents, questions, meta, gate_up)


def combine_kernel(
    rows, cols,
    pre_ref, dmt_ref, cot_ref, wgu_ref, xin_ref,
    tok_ref, gug_ref,
    w, x, back, ret, comb, parts, stage,
    load_sem, own_sem, es, er, fs, fr, out_sem,
):
    row, col = lax.axis_index("row"), lax.axis_index("col")
    slots = pre_ref.shape[0]
    block = slots // rows
    width = wgu_ref.shape[0]
    n_tok = cot_ref.shape[0]
    step = width // CHUNKS

    loads = [
        pltpu.make_async_copy(wgu_ref.at[span(f, step)], w.at[span(f, step)], load_sem.at[f])
        for f in range(CHUNKS)
    ]
    loads.append(pltpu.make_async_copy(xin_ref, x, load_sem.at[CHUNKS]))
    for copy in loads:
        copy.start()
    greet(rows, cols)

    def returning(f, s, origin, to):
        part = pl.ds(f * step, step)
        return remote(back.at[span(to, block), part], ret.at[span(origin, block), part],
                      es.at[f, s], er.at[f, origin], (to, col))

    def kept(f):
        part = pl.ds(f * step, step)
        return pltpu.make_async_copy(
            back.at[span(row, block), part], ret.at[span(row, block), part], own_sem.at[f]
        )

    def home(f, s, origin, to):
        part = pl.ds(f * step, step)
        return remote(comb.at[span(to, n_tok), part], parts.at[origin, :, part],
                      fs.at[f, s], fr.at[f, origin], (row, to))

    tile = 256
    for f in range(CHUNKS):
        loads[f].wait()

        @pl.loop(0, step // tile)
        def _(n):
            back[:, pl.ds(pl.multiple_of(f * step + n * tile, tile), tile)] = contract(
                pre_ref[...], w[pl.ds(pl.multiple_of(f * step + n * tile, tile), tile), :], 1, 1
            ).astype(BF)

        for s in range(1, rows):
            returning(f, s, row, lax.rem(row + s, rows)).start()
        kept(f).start()
    loads[CHUNKS].wait()

    def grad_tile(i):
        here = slice(i * step, (i + 1) * step)
        stage[i % 2] = contract(x[:, here], pre_ref[...], 0, 0).astype(BF)

    def grad_out(i):
        return pltpu.make_async_copy(
            stage.at[i % 2], gug_ref.at[pl.ds(i * step, step)], out_sem.at[i % 2]
        )

    def merge(f):
        kept(f).wait()
        for s in range(1, rows):
            origin = lax.rem(row + s, rows)
            returning(f, s, origin, origin).wait_recv()
        part = slice(f * step, (f + 1) * step)
        comb[:, part] = contract(dmt_ref[...], ret[:, part], 1, 0).astype(BF)
        for s in range(1, cols):
            home(f, s, col, lax.rem(col + s, cols)).start()

    def finish(f):
        part = slice(f * step, (f + 1) * step)
        total = cot_ref[:, part].astype(F32) + comb[span(col, n_tok), part].astype(F32)
        for s in range(1, cols):
            origin = lax.rem(col + s, cols)
            home(f, s, origin, origin).wait_recv()
            total = total + parts[origin, :, part].astype(F32)
        tok_ref[:, part] = total.astype(BF)

    for i in range(CHUNKS):
        if i >= 2:
            grad_out(i - 2).wait()
        grad_tile(i)
        grad_out(i).start()
        merge(i)
        if i >= 1:
            finish(i - 1)
    finish(CHUNKS - 1)
    for i in range(CHUNKS - 2, CHUNKS):
        grad_out(i).wait()
    for f in range(CHUNKS):
        for s in range(1, rows):
            returning(f, s, row, lax.rem(row + s, rows)).wait_send()
        for s in range(1, cols):
            home(f, s, col, lax.rem(col + s, cols)).wait_send()


def combine(rows, cols, pre_grad, dispatch_t, cot_tok, gate_up, slot_inputs):
    slots, hidden2 = pre_grad.shape
    n_tok, width = cot_tok.shape
    step = width // CHUNKS
    dma = pltpu.SemaphoreType.DMA
    vmem = pl.BlockSpec(memory_space=pltpu.VMEM)
    hbm = pl.BlockSpec(memory_space=pl.ANY)
    return pl.pallas_call(
        functools.partial(combine_kernel, rows, cols),
        out_shape=(
            jax.ShapeDtypeStruct((n_tok, width), BF),
            jax.ShapeDtypeStruct((width, hidden2), BF),
        ),
        in_specs=[vmem, vmem, vmem, hbm, hbm],
        out_specs=[vmem, hbm],
        scratch_shapes=[
            pltpu.VMEM((width, hidden2), BF),
            pltpu.VMEM((slots, width), BF),
            pltpu.VMEM((slots, width), BF),
            pltpu.VMEM((slots, width), BF),
            pltpu.VMEM((cols * n_tok, width), BF),
            pltpu.VMEM((cols, n_tok, width), BF),
            pltpu.VMEM((2, step, hidden2), BF),
            dma((CHUNKS + 1,)),
            dma((CHUNKS,)),
            dma((CHUNKS, rows)),
            dma((CHUNKS, rows)),
            dma((CHUNKS, cols)),
            dma((CHUNKS, cols)),
            dma((2,)),
        ],
        compiler_params=pltpu.CompilerParams(
            collective_id=1, has_side_effects=True, vmem_limit_bytes=VMEM_LIMIT
        ),
        name="combine",
    )(pre_grad, dispatch_t, cot_tok, gate_up, slot_inputs)


def fused_kernel(
    rows, cols, cap, first_widths, plane_width, last_widths,
    tok_ref, doc_ref, qry_ref, pos_in, ids_in, rw_in, wgu_ref, down_ref,
    passage_ref, out_ref, w, down,
    meta, metas, tokc, packed, x, proj, dm, dmt, place, weight, placed, group,
    docs, qrow, qcols, dsc, cot, cot_down, spread, hgrad, hidden, pre, ret, comb, parts,
    hbq, plane, drops, pos_ref, ids_ref, rw_ref,
    own_sem, load_sem, zs, zr, gs, gr, rs, ds, dr, qs, qr, ps, pr, es, er, fs, fr,
):
    row, col = lax.axis_index("row"), lax.axis_index("col")
    me = row * cols + col
    n_tok, width = tok_ref.shape
    n_doc, w_doc = doc_ref.shape
    n_qry, w_qry = qry_ref.shape
    top = ids_ref.shape[0]
    ff = down.shape[0]
    slots = x.shape[0]
    block = slots // rows
    pair = 2 * block
    chips = rows // 2
    core = lax.rem(row, 2)
    chip = lax.div(row, 2)
    sibling = row + 1 - 2 * core

    def flip(index, k, count):
        total, bit = 0, 1
        while bit < count:
            digit = lax.rem(lax.div(index, bit), 2)
            total = total + bit * (1 - digit if k & bit else digit)
            bit *= 2
        return total

    mates = list(range(2, rows)) + [1]
    line_q = cols * n_tok // SEQ_LEN

    def cuts(widths):
        edges, at = [], 0
        for size in widths:
            edges.append((at, size))
            at += size
        return edges

    first, last = cuts(first_widths), cuts(last_widths)
    n_first, n_last = len(first), len(last)

    def line_piece(kind, c):
        if kind == 0:
            return doc_ref, docs.at[span(c, n_doc), span(row, w_doc)]
        if kind == 1:
            return meta, metas.at[row * cols + c]
        if kind == 2:
            return qry_ref, qrow.at[:, span(c, w_qry)]
        at, size = first[kind - 3]
        return tok_ref.at[:, pl.ds(at, size)], tokc.at[span(c, n_tok), pl.ds(at, size)]

    ways = ((0, 1), (1, -1))

    def can_send(way):
        return col < cols - 1 if way == 0 else col > 0

    def hop(kind, step, way, block, to):
        src, dst = line_piece(kind, block)
        return remote(src if step == 0 else dst, dst, zs.at[kind, way],
                      zr.at[kind, block], (row, to))

    def advance(kinds, step):
        for kind in kinds:
            for way, d in ways:
                origin = col - d * step
                came = origin >= 0 if way == 0 else origin < cols
                if step:
                    @pl.when(came)
                    def _():
                        hop(kind, step, way, origin, col).wait_recv()

                    @pl.when(jnp.logical_and(came, can_send(way)))
                    def _():
                        hop(kind, step - 1, way, col, col + d).wait_send()

                @pl.when(jnp.logical_and(came, can_send(way)))
                def _():
                    hop(kind, step, way, origin, col + d).start()

    def settle(kind):
        for way, d in ways:
            @pl.when(can_send(way))
            def _():
                hop(kind, 0, way, col, col + d).wait_send()

    def own(kind):
        src, dst = line_piece(kind, col)
        return pltpu.make_async_copy(src, dst, own_sem.at[kind])

    plane_cut = (sum(first_widths), plane_width)
    plane_cols = pl.ds(*plane_cut)
    loads = [
        pltpu.make_async_copy(wgu_ref.at[pl.ds(at, size)], w.at[pl.ds(at, size)], load_sem.at[f])
        for f, (at, size) in enumerate(first + [plane_cut])
    ]
    loads.append(pltpu.make_async_copy(down_ref, down, load_sem.at[n_first + 1]))

    greet_signal(rows, cols)
    fetches = [
        pltpu.make_async_copy(src, dst, load_sem.at[n_first + 2 + n])
        for n, (src, dst) in enumerate(((ids_in, ids_ref), (rw_in, rw_ref), (pos_in, pos_ref)))
    ]
    for copy in fetches:
        copy.start()
    for copy in fetches:
        copy.wait()
    meta[...] = jnp.concatenate([ids_ref[...].astype(F32), rw_ref[...]], axis=0).astype(BF)
    for kind in range(3 + n_first):
        own(kind).start()
    greet_wait(rows, cols)
    queue = [(0, 1), (3,), (4,), (2,)] + [(kind,) for kind in range(5, 3 + n_first)]
    advance(queue[0], 0)
    advance(queue[1], 0)

    def gathered(i):
        for step in range(1, cols):
            advance(queue[i], step)
        for kind in queue[i]:
            own(kind).wait()
        if i + 2 < len(queue):
            advance(queue[i + 2], 0)

    def strip(kind, r):
        if kind == 0:
            return docs.at[:, span(r, w_doc)]
        if kind == 1:
            return metas.at[pl.ds(r * cols, cols)]
        if kind == 2:
            return plane.at[span(r, n_tok), :]
        return dsc.at[span(r, n_qry), :]

    def peer(s):
        return 2 * flip(chip, s, chips) + core

    def direct(kind, s, origin, to):
        src = tok_ref.at[:, plane_cols] if kind == 2 else strip(kind, origin)
        return remote(src, strip(kind, origin), gs.at[kind], gr.at[kind, 0 if s else 1], (to, col))

    def relay(kind, origin):
        return remote(strip(kind, origin), strip(kind, origin), rs.at[kind], gr.at[kind, 1],
                      (sibling, col))

    def several(kind, count, send_sem, recv_sem):
        if kind == 0:
            part = docs.at[:, pl.ds(0, count * w_doc)]
        elif kind == 1:
            part = metas.at[pl.ds(0, count * cols)]
        elif kind == 2:
            part = plane.at[pl.ds(0, count * n_tok), :]
        else:
            part = dsc.at[pl.ds(0, count * n_qry), :]
        return remote(part, part, send_sem, recv_sem, (sibling, col))

    def spread_out(kind):
        for s in range(1, chips):
            direct(kind, s, row, peer(s)).start()
        direct(kind, 0, row, sibling).start()

    def pass_on(kind):
        several(kind, chips - 1, rs.at[kind], gr.at[kind, 0]).wait_recv()
        for s in range(1, chips):
            relay(kind, peer(s)).start()

    def all_here(kind):
        several(kind, chips, rs.at[kind], gr.at[kind, 1]).wait_recv()

    def all_out(kind):
        several(kind, chips, gs.at[kind], gr.at[kind, 0]).wait_send()

    def passed(kind):
        several(kind, chips - 1, rs.at[kind], gr.at[kind, 1]).wait_send()

    own_plane = pltpu.make_async_copy(
        tok_ref.at[:, plane_cols], strip(2, row), own_sem.at[4 + 2 * n_first + n_last]
    )
    spread_out(2)
    own_plane.start()
    for copy in loads:
        copy.start()

    before = (
        lax.broadcasted_iota(jnp.int32, (n_tok, n_tok), 0)
        < lax.broadcasted_iota(jnp.int32, (n_tok, n_tok), 1)
    ).astype(BF)
    slot = lax.broadcasted_iota(jnp.int32, (block, n_tok), 0).astype(F32)

    near = tuple(k for k in mates if k < 6)
    far = tuple(k for k in mates if k >= 6)
    final = n_first - 1

    def outgoing(f, k, origin, to):
        part = pl.ds(*first[f])
        late = f == final
        return remote(
            packed.at[span(to, block), part], x.at[span(origin, block), part],
            ds.at[f + 1 if late and k in far else f], dr.at[f + k // 2 if late else f], (to, col),
        )

    def batch(f, count, send_sem, recv_sem):
        part = pl.ds(*first[f])
        here = pl.ds(0, count * block)
        return remote(packed.at[here, part], x.at[here, part], send_sem, recv_sem, (row, col))

    def sent(f, late=False):
        if f < final:
            batch(f, rows - 1, ds.at[f], dr.at[f]).wait_send()
        elif late:
            batch(f, len(far), ds.at[f + 1], dr.at[f]).wait_send()
        else:
            batch(f, len(near), ds.at[f], dr.at[f]).wait_send()

    def kept(f):
        part = pl.ds(*first[f])
        return pltpu.make_async_copy(
            packed.at[span(row, block), part], x.at[span(row, block), part],
            own_sem.at[3 + n_first + f],
        )

    def send(f, offsets):
        for s in offsets:
            outgoing(f, s, row, flip(row, s, rows)).start()

    def pack(f):
        part = pl.ds(*first[f])

        @pl.loop(0, chips)
        def _(m):
            packed[span(m, pair), part] = contract(
                dm[span(m, pair), :], tokc[:, part], 1, 0
            ).astype(BF)

        kept(f).start()

    tile = 512

    def project(f):
        loads[f].wait()
        kept(f).wait()
        batch(f, rows - 1, ds.at[f], dr.at[f]).wait_recv()
        part = pl.ds(*first[f])

        @pl.loop(0, 2 * ff // tile)
        def _(n):
            term = contract(x[:, part], w[part, span(n, tile)], 1, 0)
            if f == 0:
                proj[:, span(n, tile)] = term
            else:
                proj[:, span(n, tile)] += term

    def query_piece(origin, to):
        return qrow.at[:, span(to, w_doc)], qcols.at[span(origin, n_qry), :]

    def queries(s, origin, to):
        src, dst = query_piece(origin, to)
        return remote(src, dst, qs.at[0], qr.at[0], (to, col))

    def all_queries():
        part = qcols.at[pl.ds(0, (rows - 1) * n_qry), :]
        return remote(part, part, qs.at[0], qr.at[0], (sibling, col))

    def own_queries():
        src, dst = query_piece(row, row)
        return pltpu.make_async_copy(src, dst, own_sem.at[3 + 2 * n_first])

    share = rows * cap

    def dropped(s, origin, to):
        return remote(packed.at[span(to, share), plane_cols], drops.at[span(origin, share), :],
                      ps.at[0], pr.at[0], (row, to))

    def all_dropped():
        part = drops.at[pl.ds(0, (cols - 1) * share), :]
        return remote(part, part, ps.at[0], pr.at[0], (row, col))

    def own_drop():
        return pltpu.make_async_copy(
            packed.at[span(col, share), plane_cols], drops.at[span(col, share), :],
            own_sem.at[5 + 2 * n_first + n_last],
        )

    def pack_plane():
        wanted_by = (
            lax.broadcasted_iota(jnp.int32, (cols, n_tok), 0) + row * cols
        ).astype(F32)
        spots = lax.broadcasted_iota(jnp.int32, (share, n_tok), 0).astype(F32)
        for r in range(rows):
            ids = metas[r * cols + col].astype(F32)
            hit = jnp.zeros((cols, n_tok), F32)
            for k in range(top):
                hit = hit + (ids[k : k + 1, :] == wanted_by).astype(F32)
            rank = contract(hit.astype(BF), before, 1, 0)
            spot = jnp.where(hit > 0.5, rank + float(r * cap), -1.0)
            for c in range(cols):
                pre[c * share : (c + 1) * share, r * n_tok : (r + 1) * n_tok] = jnp.where(
                    spots == spot[c : c + 1, :], 1.0, 0.0
                ).astype(BF)

        @pl.loop(0, cols)
        def _(c):
            packed[span(c, share), plane_cols] = contract(
                pre[span(c, share), : rows * n_tok], plane[...], 1, 0
            ).astype(BF)

        for s in range(1, cols):
            dropped(s, col, lax.rem(col + s, cols)).start()
        own_drop().start()

    def order_rows():
        at = lax.broadcasted_iota(jnp.int32, (slots, LANES), 0).astype(F32)
        lane_at = lax.broadcasted_iota(jnp.int32, (slots, LANES), 1).astype(F32)
        line_of = jnp.floor((at + 0.5) * (1.0 / block))
        rest = at - line_of * block
        plane_of = jnp.floor((rest + 0.5) * (1.0 / cap))
        source = plane_of * share + line_of * cap + (rest - plane_of * cap)
        for n in range(slots // LANES):
            pre[:, n * LANES : (n + 1) * LANES] = jnp.where(
                lane_at + float(n * LANES) == source, 1.0, 0.0
            ).astype(BF)

    def project_plane():
        loads[n_first].wait()
        own_drop().wait()
        all_dropped().wait_recv()
        x[:, plane_cols] = contract(pre[:, :slots], drops[...], 1, 0).astype(BF)

        @pl.loop(0, 2 * ff // tile)
        def _(n):
            proj[:, span(n, tile)] += contract(
                x[:, plane_cols], w[plane_cols, span(n, tile)], 1, 0
            )

    gathered(0)
    spread_out(0)
    spread_out(1)
    target = (
        lax.broadcasted_iota(jnp.int32, (rows, n_tok), 0) * cols + col
    ).astype(F32)
    for c in range(cols):
        ids = metas[row * cols + c].astype(F32)
        hit = jnp.zeros((rows, n_tok), F32)
        for k in range(top):
            hit = hit + (ids[k : k + 1, :] == target).astype(F32)
        rank = contract(hit.astype(BF), before, 1, 0)
        spot = jnp.where(hit > 0.5, rank + float(c * cap), -1.0)
        for r in range(rows):
            dm[r * block : (r + 1) * block, c * n_tok : (c + 1) * n_tok] = jnp.where(
                slot == spot[r : r + 1, :], 1.0, 0.0
            ).astype(BF)
    gathered(1)
    pack(0)
    send(0, mates)
    pass_on(2)
    gathered(2)
    pack(1)
    pass_on(1)
    pass_on(0)
    gathered(3)
    all_here(0)
    scores = contract(qrow[...], docs[...], 1, 1) / sharpness_divisor
    peak = jnp.max(scores, axis=1, keepdims=True)
    grown = jnp.exp(scores - peak)
    total = jnp.sum(grown, axis=1, keepdims=True)
    square = (n_qry, n_qry)
    diagonal = lax.broadcasted_iota(jnp.int32, square, 0) == lax.broadcasted_iota(jnp.int32, square, 1)
    wanted = jnp.sum(
        jnp.where(diagonal, pos_ref[...].astype(F32), 0.0), axis=1, keepdims=True
    )
    onehot = (
        wanted == lax.broadcasted_iota(jnp.int32, scores.shape, 1).astype(F32)
    ).astype(F32)
    dsc[span(row, n_qry), :] = ((grown / total - onehot) / sharpness_divisor).astype(BF)
    for c in range(cols):
        here = slice(c * n_tok, (c + 1) * n_tok)
        dmt[here, :] = dm[:, here].astype(F32).T.astype(BF)
    spread_out(3)
    send(1, near)
    send(1, far)
    gathered(4)
    pack(2)
    all_here(1)
    all_here(2)
    own_plane.wait()
    pack_plane()
    pass_on(3)
    sent(0)
    send(2, near)
    order_rows()

    lines = rows * cols
    each = lax.broadcasted_iota(jnp.int32, (lines, n_tok), 0)
    mine = me.astype(F32)
    chosen = jnp.zeros((lines, n_tok), F32)
    amount = jnp.zeros((lines, n_tok), F32)
    for b in range(lines):
        entry = metas[b].astype(F32)
        hit = (entry[:top] == mine).astype(F32)
        found = jnp.sum(hit, axis=0, keepdims=True)
        value = jnp.sum(hit * entry[top:], axis=0, keepdims=True)
        chosen = jnp.where(each == b, found, chosen)
        amount = jnp.where(each == b, value, amount)
    rank = contract(chosen.astype(BF), before, 1, 0)
    begin = (lax.rem(each, cols) * cap).astype(F32)
    place[...] = jnp.where(chosen > 0.5, rank + begin, -1.0)
    weight[...] = amount
    group[...] = (
        lax.broadcasted_iota(jnp.int32, (cols * n_tok, line_q), 0) // SEQ_LEN
        == lax.broadcasted_iota(jnp.int32, (cols * n_tok, line_q), 1)
    ).astype(BF)

    @pl.loop(0, rows)
    def _(r):
        for c in range(cols):
            here = pl.ds(r * cols + c, 1)
            placed[:, c * n_tok : (c + 1) * n_tok] = jnp.where(
                slot == place[here, :], weight[here, :], 0.0
            ).astype(BF)
        spread[span(r, block), :] = contract(placed[...], group[...], 1, 0).astype(BF)

    project(0)
    all_here(3)

    @pl.loop(0, width // tile)
    def _(n):
        cot[:, span(n, tile)] = (
            contract(dsc[...], docs[:, span(n, tile)], 1, 0) / SEQ_LEN
        ).astype(BF)

    loads[n_first + 1].wait()
    small = 256

    @pl.loop(0, ff // small)
    def _(n):
        cot_down[:, span(n, small)] = contract(
            cot[...], down[span(n, small), :], 1, 1
        ).astype(BF)

    sent(1)
    send(2, far)
    for s in mates:
        queries(s, row, flip(row, s, rows)).start()
    own_queries().start()
    project(1)
    project_plane()

    def returning(f, s, origin, to):
        part = pl.ds(*last[f])
        return remote(packed.at[span(to, block), part], ret.at[span(origin, block), part],
                      es.at[f], er.at[f], (to, col))

    def all_returned(f):
        part = pl.ds(*last[f])
        here = pl.ds(0, (rows - 1) * block)
        return remote(packed.at[here, part], ret.at[here, part], es.at[f], er.at[f], (row, col))

    def held(f):
        part = pl.ds(*last[f])
        return pltpu.make_async_copy(
            packed.at[span(row, block), part], ret.at[span(row, block), part],
            own_sem.at[4 + 2 * n_first + f],
        )

    def home(f, s, origin, to):
        part = pl.ds(*last[f])
        return remote(comb.at[span(to, n_tok), part], parts.at[origin, :, part],
                      fs.at[f], fr.at[f], (row, to))

    def all_home(f):
        part = pl.ds(*last[f])
        here = pl.ds(0, cols - 1)
        return remote(parts.at[here, :, part], parts.at[here, :, part], fs.at[f], fr.at[f], (row, col))

    f_end = n_first - 1
    loads[f_end].wait()
    kept(f_end).wait()
    end = pl.ds(*first[f_end])
    groups = [[0, 1], [2, 3], [4, 5], list(range(6, n_last))]

    def group_cols(g):
        return pl.ds(last[groups[g][0]][0], sum(last[f][1] for f in groups[g]))

    begin_cols = group_cols(0)
    lane = 128

    for s in [k for k in (1, 2, 3, 0) if k < chips]:
        other = flip(chip, s, chips)
        count = 2 if s else 1
        batch(f_end, count, ds.at[f_end], dr.at[f_end + s]).wait_recv()
        here = span(other, pair)

        @pl.loop(0, 2 * ff // tile)
        def _(n):
            proj[here, span(n, tile)] += contract(x[here, end], w[end, span(n, tile)], 1, 0)

        for k in range(2):
            r = 2 * other + k
            at = span(r, block)
            hgrad[...] = contract(spread[at, :], cot_down[span(r, line_q), :], 1, 0)

            @pl.loop(0, ff // lane)
            def _(n):
                left = span(n, lane)
                right = pl.ds(pl.multiple_of(ff + n * lane, lane), lane)
                gate, up = proj[at, left], proj[at, right]
                sig = jax.nn.sigmoid(gate)
                act = gate * sig
                grad = hgrad[:, left]
                hidden[at, left] = (act * up).astype(BF)
                pre[at, left] = (grad * up * (sig * (1.0 + gate * (1.0 - sig)))).astype(BF)
                pre[at, right] = (grad * act).astype(BF)

        packed[here, begin_cols] = contract(pre[here, :], w[begin_cols, :], 1, 1).astype(BF)
        for f in groups[0]:
            for k in (2 * s, 2 * s + 1):
                if k:
                    returning(f, k, row, flip(row, k, rows)).start()
                else:
                    held(f).start()

    def give_back(g):
        part = group_cols(g)
        if g == 2:
            sent(final)
            sent(final, late=True)
        if g == 3:
            all_dropped().wait_send()

        @pl.loop(0, 2)
        def _(m):
            half = span(m, slots // 2)
            packed[half, part] = contract(pre[half, :], w[part, :], 1, 1).astype(BF)

        for f in groups[g]:
            for s in mates:
                returning(f, s, row, flip(row, s, rows)).start()
            held(f).start()

    n_gate, n_down = width // small, ff // small

    def grad_tile(i):
        if i < n_gate:
            here = slice(i * small, (i + 1) * small)
            w[here, :] = contract(x[:, here], pre[...], 0, 0).astype(BF)
        else:
            here = slice((i - n_gate) * small, (i - n_gate + 1) * small)
            down[here, :] = contract(hbq[:, here], cot[...], 0, 0).astype(BF)

    def merge(f):
        held(f).wait()
        all_returned(f).wait_recv()
        part = pl.ds(*last[f])
        comb[:, part] = contract(dmt[...], ret[:, part], 1, 0).astype(BF)
        for s in range(1, cols):
            home(f, s, col, lax.rem(col + s, cols)).start()

    per_dev = n_tok // SEQ_LEN
    repeat = (
        lax.broadcasted_iota(jnp.int32, (n_tok, per_dev), 0) // SEQ_LEN
        == lax.broadcasted_iota(jnp.int32, (n_tok, per_dev), 1)
    ).astype(BF)

    def finish(f):
        part = pl.ds(*last[f])
        sums = contract(repeat, cot[span(me, per_dev), part], 1, 0)
        sums = sums + comb[span(col, n_tok), part].astype(F32)
        all_home(f).wait_recv()
        for s in range(1, cols):
            origin = lax.rem(col + s, cols)
            sums = sums + parts[origin, :, part].astype(F32)
        out_ref[:, part] = sums.astype(BF)

    def by_query():
        @pl.loop(0, rows)
        def _(r):
            hbq[span(r, line_q), :] = contract(
                spread[span(r, block), :], hidden[span(r, block), :], 0, 0
            ).astype(BF)

    def settle_sends():
        for kind in range(4):
            all_out(kind)
            passed(kind)
        for kind in range(3 + n_first):
            settle(kind)
        all_queries().wait_send()

    todo = list(range(n_gate, n_gate + n_down)) + list(range(n_gate))

    def grads(count):
        for i in todo[:count]:
            grad_tile(i)
        del todo[:count]

    merge(0)
    give_back(1)
    merge(1)
    give_back(2)
    by_query()
    all_queries().wait_recv()
    own_queries().wait()
    passage_ref[...] = contract(dsc[:, span(col, n_doc)], qcols[...], 0, 0)
    settle_sends()
    grads(2)
    merge(2)
    finish(0)
    give_back(3)
    for f in range(3, n_last - 2):
        grads(2)
        merge(f)
        finish(f - 2)
    grads(len(todo))
    for f in range(n_last - 2, n_last):
        merge(f)
    for f in range(n_last - 4, n_last):
        finish(f)

    for f in range(n_last):
        all_returned(f).wait_send()
        all_home(f).wait_send()


def fused_plan(rows, cols, cap, top, plane_width, tokens, documents, questions, down):
    n_tok, width = tokens.shape
    n_doc, w_doc = documents.shape
    n_qry = questions.shape[0]
    ff = down.shape[0]
    block = cols * cap
    slots = rows * block
    line = cols * n_tok
    line_q = line // SEQ_LEN
    n_all = rows * n_qry
    return [
        ((2 * top, n_tok), BF),
        ((rows * cols, 2 * top, n_tok), BF),
        ((line, width - plane_width), BF),
        ((slots, width), BF),
        ((slots, width), BF),
        ((slots, 2 * ff), F32),
        ((slots, line), BF),
        ((line, slots), BF),
        ((rows * cols, n_tok), F32),
        ((rows * cols, n_tok), F32),
        ((block, line), BF),
        ((line, line_q), BF),
        ((cols * n_doc, width), BF),
        ((n_qry, width), BF),
        ((n_all, w_doc), BF),
        ((n_all, cols * n_doc), BF),
        ((n_all, width), BF),
        ((n_all, ff), BF),
        ((slots, line_q), BF),
        ((block, ff), F32),
        ((slots, ff), BF),
        ((slots, 2 * ff), BF),
        ((slots, width), BF),
        ((line, width), BF),
        ((cols, n_tok, width), BF),
        ((n_all, ff), BF),
        ((rows * n_tok, plane_width), BF),
        ((slots, plane_width), BF),
        ((1, n_qry), jnp.int32),
        ((top, n_tok), jnp.int32),
        ((top, n_tok), F32),
    ]


def plan_bytes(plan):
    return sum(math.prod(shape) * jnp.dtype(kind).itemsize for shape, kind in plan)


def fused(rows, cols, cap, plan, tokens, documents, questions, positive, ids, weights, gate_up, down):
    n_tok, width = tokens.shape
    n_doc, w_doc = documents.shape
    hidden2 = gate_up.shape[1]
    first = [width * k // 16 for k in (4, 4, 4)]
    plane_width = width - sum(first)
    last = [width // 8] * 7 + [width // 16] * 2
    dma = pltpu.SemaphoreType.DMA
    vmem = pl.BlockSpec(memory_space=pltpu.VMEM)
    hbm = pl.BlockSpec(memory_space=pl.ANY)
    n_first, n_last = len(first), len(last)
    return pl.pallas_call(
        functools.partial(fused_kernel, rows, cols, cap, first, plane_width, last),
        out_shape=(
            pltpu.VMEM((n_doc, w_doc), F32),
            pltpu.VMEM((n_tok, width), BF),
            pltpu.VMEM((width, hidden2), BF),
            pltpu.VMEM(down.shape, BF),
        ),
        in_specs=[hbm] * 8,
        out_specs=[vmem] * 4,
        scratch_shapes=[pltpu.VMEM(shape, kind) for shape, kind in plan]
        + [
            dma((6 + 2 * n_first + n_last,)),
            dma((n_first + 5,)),
            dma((3 + n_first, 2)),
            dma((3 + n_first, cols)),
            dma((4,)),
            dma((4, 2)),
            dma((4,)),
            dma((n_first + 1,)),
            dma((n_first + rows // 2,)),
            dma((1,)),
            dma((1,)),
            dma((1,)),
            dma((1,)),
            dma((n_last,)),
            dma((n_last,)),
            dma((n_last,)),
            dma((n_last,)),
        ],
        compiler_params=pltpu.CompilerParams(
            collective_id=2, has_side_effects=True, vmem_limit_bytes=FUSED_LIMIT
        ),
        name="fused",
    )(tokens, documents, questions, positive.reshape(1, -1), ids.T, weights.T, gate_up, down)


def settle_kernel(pieces, *refs):
    count = len(pieces)
    sources, targets, sem = refs[:count], refs[count:-1], refs[-1]
    copies = []
    for i, parts in enumerate(pieces):
        size = sources[i].shape[0] // parts
        for p in range(parts):
            at = pl.ds(p * size, size)
            copies.append(
                pltpu.make_async_copy(sources[i].at[at], targets[i].at[at], sem.at[len(copies)])
            )
    for copy in copies:
        copy.start()
    for copy in copies:
        copy.wait()


def settled(*arrays):
    sizes = [a.size * a.dtype.itemsize // (1 << 18) for a in arrays]
    pieces = [1 << max(0, n.bit_length() - 1) for n in sizes]
    vmem = pl.BlockSpec(memory_space=pltpu.VMEM)
    hbm = pl.BlockSpec(memory_space=pl.ANY)
    return pl.pallas_call(
        functools.partial(settle_kernel, pieces),
        out_shape=tuple(pltpu.HBM(a.shape, a.dtype) for a in arrays),
        in_specs=[vmem] * len(arrays),
        out_specs=[hbm] * len(arrays),
        scratch_shapes=[pltpu.SemaphoreType.DMA((sum(pieces),))],
        compiler_params=pltpu.CompilerParams(vmem_limit_bytes=1 << 20),
        name="settle",
    )(*[pltpu.with_memory_space_constraint(a, pltpu.VMEM) for a in arrays])


def shards(
    question_vectors,
    document_vectors,
    positive,
    tokens,
    expert_ids,
    route_weights,
    expert_gate_up,
    expert_down,
):
    rows = lax.axis_size("row")
    cols = lax.axis_size("col")
    row = lax.axis_index("row")
    col = lax.axis_index("col")
    devices_all = rows * cols
    me = row * cols + col
    n_tok, width = tokens.shape
    top = expert_ids.shape[1]
    experts_all = devices_all * expert_gate_up.shape[0]
    cap = max(2, (n_tok * top * 9 + 8 * experts_all - 1) // (8 * experts_all))
    block = cols * cap
    hidden_width = expert_down.shape[1]
    gate_up = expert_gate_up[0]
    down = expert_down[0]

    plan = fused_plan(rows, cols, cap, top, width * 4 // 16, tokens, document_vectors, question_vectors, down)
    if rows == 8 and experts_all <= 256 and plan_bytes(plan) < FUSED_LIMIT - 4_000_000:
        passage_grad, token_grad, gate_up_grad, down_grad = fused(
            rows, cols, cap, plan, tokens, document_vectors, question_vectors, positive,
            expert_ids, route_weights, gate_up, down,
        )
        passage_grad, token_grad, gate_up_grad, down_grad = settled(
            passage_grad, token_grad, gate_up_grad, down_grad
        )
        return (passage_grad, token_grad, gate_up_grad[None], down_grad[None])

    n_qry = positive.shape[0]
    pos_rows = -(-n_qry // (8 * LANES)) * 8
    pos = jnp.pad(positive, (0, pos_rows * LANES - n_qry)).astype(F32).reshape(pos_rows, LANES)
    meta = jnp.concatenate([expert_ids.T.astype(F32), route_weights.T, pos], axis=0)
    slot_inputs, docs, qrys, metas, projected, dm = dispatch(
        rows, cols, cap, top, tokens, document_vectors, question_vectors, meta, gate_up
    )

    ids = metas[:, :top].astype(jnp.int32)
    weights = metas[:, top : 2 * top]
    positive_all = metas.reshape(rows, cols, -1, LANES)[:, 0, 2 * top :].reshape(rows, -1)
    positive_all = positive_all[:, :n_qry].reshape(-1).astype(jnp.int32)

    scores = contract(qrys, docs, 1, 1) / sharpness_divisor
    peak = jnp.max(scores, axis=1, keepdims=True)
    grown = jnp.exp(scores - peak)
    total = jnp.sum(grown, axis=1, keepdims=True)
    onehot = (
        positive_all[:, None] == jnp.arange(docs.shape[0], dtype=jnp.int32)[None, :]
    ).astype(F32)
    dscore = ((grown / total - onehot) / sharpness_divisor).astype(BF)
    cot = (contract(dscore, docs, 1, 0) / SEQ_LEN).astype(BF)
    n_doc, w_doc = document_vectors.shape
    passage_grad = contract(
        lax.dynamic_slice_in_dim(dscore, col * n_doc, n_doc, 1),
        lax.dynamic_slice_in_dim(qrys, row * w_doc, w_doc, 1),
        0, 0,
    )

    mine = ids == me
    chosen = jnp.any(mine, axis=1)
    weight = jnp.sum(jnp.where(mine, weights, 0.0), axis=1)
    earlier = (
        lax.broadcasted_iota(jnp.int32, (n_tok, n_tok), 0)
        < lax.broadcasted_iota(jnp.int32, (n_tok, n_tok), 1)
    ).astype(BF)
    rank = contract(chosen.astype(BF), earlier, 1, 0).astype(jnp.int32)
    first = jnp.tile(jnp.arange(cols, dtype=jnp.int32) * cap, rows)[:, None]
    place = jnp.where(chosen, first + rank, -1).reshape(rows, 1, cols * n_tok)
    line_weight = weight.reshape(rows, 1, cols * n_tok)
    placed = jnp.where(
        place == jnp.arange(block, dtype=jnp.int32)[None, :, None], line_weight, 0.0
    ).astype(BF)
    line_q = cols * n_tok // SEQ_LEN
    grouped = (
        lax.broadcasted_iota(jnp.int32, (cols * n_tok, line_q), 0) // SEQ_LEN
        == lax.broadcasted_iota(jnp.int32, (cols * n_tok, line_q), 1)
    ).astype(BF)
    spread = contract(placed.reshape(-1, cols * n_tok), grouped, 1, 0).astype(BF)
    spread = spread.reshape(rows, block, line_q)

    gate_part = projected[:, :hidden_width]
    up_part = projected[:, hidden_width:]
    sigmoid_gate = jax.nn.sigmoid(gate_part)
    activated = gate_part * sigmoid_gate
    hidden = (activated * up_part).astype(BF)
    cot_down = contract(cot, down, 1, 1).astype(BF).reshape(rows, line_q, hidden_width)
    hidden_grad = lax.dot_general(
        spread, cot_down, (((2,), (1,)), ((0,), (0,))), preferred_element_type=F32
    ).reshape(-1, hidden_width)
    slope = sigmoid_gate * (1.0 + gate_part * (1.0 - sigmoid_gate))
    pre_grad = jnp.concatenate(
        [hidden_grad * up_part * slope, hidden_grad * activated], axis=1
    ).astype(BF)

    per_dev = n_tok // SEQ_LEN
    cot_own = lax.dynamic_slice_in_dim(cot, me * per_dev, per_dev, 0)
    cot_tok = jnp.repeat(cot_own, SEQ_LEN, axis=0)
    token_grad, gate_up_grad = combine(
        rows, cols, pre_grad, dm.T, cot_tok, gate_up, slot_inputs
    )

    hidden_by_query = lax.dot_general(
        spread, hidden.reshape(rows, block, hidden_width), (((1,), (1,)), ((0,), (0,))),
        preferred_element_type=F32,
    ).astype(BF).reshape(-1, hidden_width)
    down_grad = contract(hidden_by_query, cot, 0, 0).astype(BF)
    return (passage_grad, token_grad, gate_up_grad[None], down_grad[None])


def solution(mesh):
    in_specs = (
        P("row", "col"),
        P("col", "row"),
        P("row"),
        P(("row", "col"), None),
        P(("row", "col"), None),
        P(("row", "col"), None),
        P(("row", "col"), None, None),
        P(("row", "col"), None, None),
    )
    out_specs = (
        P("col", "row"),
        P(("row", "col"), None),
        P(("row", "col"), None, None),
        P(("row", "col"), None, None),
    )
    return jax.shard_map(shards, mesh=mesh, in_specs=in_specs, out_specs=out_specs, check_vma=False)
```
